32 devices in a mesh: dp: 8 (over z, x), fsdp: 4 (over y, core).
Axes of the slice: x: 2, y: 2, z: 4, core: 2. Of those that a mesh axis runs over, the one named last changes fastest.
Arguments:
- patches: bfloat16 [25344, 768], P(('dp', 'fsdp')), may hold values from -6 to 6
- send_counts: int32 [32, 8], P(('dp', 'fsdp')), may hold values from 50 to 99, as said below
- dec_segment: int32 [64, 529], P(('dp', 'fsdp')), may hold values from 0 to 4, as said below
- source_index: int32 [64, 529], P(('dp', 'fsdp')), may hold values from -1 to 791, as said below
- cotangent: float32 [64, 529, 512], P(('dp', 'fsdp')), may hold values from -6 to 6
- enc_norms: float32 [4, 768], P('fsdp', 'dp'), may hold values from -0.9 to 1.6, as said below
- enc_qkv: float32 [768, 2304], P('fsdp', 'dp'), may hold values from -0.21875 to 0.21875
- enc_out: float32 [768, 768], P('fsdp', 'dp'), may hold values from -0.4375 to 0.4375
- enc_up: float32 [768, 3072], P('fsdp', 'dp'), may hold values from -0.21875 to 0.21875
- enc_down: float32 [3072, 768], P('fsdp', 'dp'), may hold values from -0.109375 to 0.109375
- dec_norms: float32 [8, 512], P('fsdp', 'dp'), may hold values from -1.7 to 1.7, as said below
- dec_embed: float32 [768, 512], P('fsdp', 'dp'), may hold values from -0.21875 to 0.21875
- dec_qkv: float32 [512, 1536], P('fsdp', 'dp'), may hold values from -0.25 to 0.25
- dec_out: float32 [512, 512], P('fsdp', 'dp'), may hold values from -0.5 to 0.5
- dec_up: float32 [512, 2048], P('fsdp', 'dp'), may hold values from -0.25 to 0.25
- dec_down: float32 [2048, 512], P('fsdp', 'dp'), may hold values from -0.125 to 0.125
Outputs:
- decoded: float32 [64, 529, 512], P(('dp', 'fsdp'))
- patch_grad: float32 [25344, 768], P(('dp', 'fsdp'))
- grad_enc_norms: float32 [4, 768], P('fsdp', 'dp')
- grad_enc_qkv: float32 [768, 2304], P('fsdp', 'dp')
- grad_enc_out: float32 [768, 768], P('fsdp', 'dp')
- grad_enc_up: float32 [768, 3072], P('fsdp', 'dp')
- grad_enc_down: float32 [3072, 768], P('fsdp', 'dp')
- grad_dec_norms: float32 [8, 512], P('fsdp', 'dp')
- grad_dec_embed: float32 [768, 512], P('fsdp', 'dp')
- grad_dec_qkv: float32 [512, 1536], P('fsdp', 'dp')
- grad_dec_out: float32 [512, 512], P('fsdp', 'dp')
- grad_dec_up: float32 [512, 2048], P('fsdp', 'dp')
- grad_dec_down: float32 [2048, 512], P('fsdp', 'dp')
The draws below stay inside these ranges and needn't reach their ends.
Inputs may be any that keep to these rules, and one draw needn't show every extreme that they name: `send_counts`: entry d of device (e, f) is the number of visible patches of the one document that its slot d sends to device (d, f); they fill the slot's last rows; every entry belongs to one whole document. `dec_segment`: A strip holds 4 documents numbered in order, each whole within the strip, of 66 to 132 patches; the number 4 marks the strip's trailing padding, present in every strip. `source_index`: A visible patch names row c of the buffer that its device receives: c // 99 is the sending device along dp, c % 99 the row in that device's slot. A document of n patches has one masked span of n // 4 patches; its visible patches keep their order and come from one sender; each device receives exactly one document from every device of its dp group. Masked and padding patches have -1. `enc_norms`: even rows are gains, odd rows shifts. `dec_norms`: rows 0, 2, 4 are gains, rows 1, 3, 5, 7 shifts, row 6 the mask token.
All inputs are finite; a program needn't handle non-finite values.
Results may differ from the reference program's by a relative error of at most 0.02.
Values may be sent and summed in bfloat16 or wider, within the bound.
A program may use at most 448 MiB of HBM per device.

```python
import jax
import jax.numpy as jnp
from jax import lax

D_E = 768
HEADS_E = 12
FF_E = 3072
D_D = 512
HEADS_D = 16
FF_D = 2048
L = 529
STRIPS = 2
CAP = 99
ENC_DEV = 792
N_DP = 8
N_FSDP = 4
DEVICES = 32


def doc_layout(key):
    peer_count = N_DP
    group_count = N_FSDP
    doc_count = N_DP // STRIPS
    doc_most = L * STRIPS // N_DP
    doc_least = doc_most // 2
    slot_rows = doc_most - doc_most // 4
    device_count = peer_count * group_count
    subkeys = jax.random.split(jax.random.fold_in(key, 7), 5)
    doc_shape = (device_count, STRIPS, doc_count)
    lengths = jax.random.randint(subkeys[0], doc_shape, doc_least, doc_most + 1)
    longest = jax.random.randint(subkeys[1], (device_count, STRIPS, 1), 0, doc_count)
    shortest = (longest + 1 + jax.random.randint(subkeys[2], (device_count, STRIPS, 1), 0, doc_count - 1)) % doc_count
    doc_slot = lax.broadcasted_iota(jnp.int32, doc_shape, 2)
    lengths = jnp.where(doc_slot == longest, doc_most, jnp.where(doc_slot == shortest, doc_least, lengths))
    doc_ends = jnp.cumsum(lengths, axis=-1)
    doc_starts = doc_ends - lengths
    hidden_len = lengths // 4
    span_start = jax.random.randint(subkeys[3], doc_shape, 0, lengths - hidden_len + 1)
    drawn_len = lengths - hidden_len
    position = lax.broadcasted_iota(jnp.int32, (device_count, STRIPS, L), 2)
    segment = jnp.sum((position[..., None] >= doc_ends[:, :, None, :]).astype(jnp.int32), axis=-1)
    in_doc = segment < doc_count
    doc_index = jnp.minimum(segment, doc_count - 1)

    def per_doc(table):
        return jnp.take_along_axis(table, doc_index, axis=2)
    local_pos = position - per_doc(doc_starts)
    span_lo = per_doc(span_start)
    span_len = per_doc(hidden_len)
    masked = (local_pos >= span_lo) & (local_pos < span_lo + span_len)
    visible = in_doc & jnp.logical_not(masked)
    ordinal = local_pos - jnp.where(local_pos >= span_lo + span_len, span_len, 0)
    device_id = lax.broadcasted_iota(jnp.int32, doc_shape, 0)
    dp_index = device_id // group_count
    fsdp_index = device_id % group_count
    orders = jax.vmap(lambda subkey: jax.random.permutation(subkey, peer_count))(jax.random.split(subkeys[4], device_count))
    doc_number = lax.broadcasted_iota(jnp.int32, doc_shape, 1) * doc_count + doc_slot
    offset = jnp.take_along_axis(orders, doc_number.reshape(device_count, -1), axis=1).reshape(doc_shape)
    receiver = (dp_index + offset) % peer_count
    row_in_slot = slot_rows - per_doc(drawn_len) + ordinal
    sources = jnp.where(visible, per_doc(receiver) * slot_rows + row_in_slot, -1)
    target_device = receiver * group_count + fsdp_index
    counts = jnp.zeros((device_count, peer_count), jnp.int32).at[target_device.reshape(-1), dp_index.reshape(-1)].set(drawn_len.reshape(-1))
    return (counts, segment.reshape(device_count * STRIPS, L), sources.reshape(device_count * STRIPS, L))


def draw_send_counts(key, part):
    return doc_layout(key)[0]


def draw_dec_segment(key, part):
    return doc_layout(key)[1]


def draw_source_index(key, part):
    return doc_layout(key)[2]


def norm_table(key, row_count, width):
    first, second, third = jax.random.split(jax.random.fold_in(key, 11), 3)
    table_shape = (row_count, width)
    gain_part = jax.random.uniform(first, table_shape, jnp.float32, 0.6, 1.4)
    shift_part = jax.random.uniform(second, table_shape, jnp.float32, -0.5, 0.5)
    token_part = jax.random.uniform(third, table_shape, jnp.float32, -1.7, 1.7)
    row_id = lax.broadcasted_iota(jnp.int32, table_shape, 0)
    table = jnp.where(row_id % 2 == 0, gain_part, shift_part)
    return jnp.where(row_id == 6, token_part, table)


def draw_enc_norms(key, part):
    return norm_table(key, 4, D_E)


def draw_dec_norms(key, part):
    return norm_table(key, 8, D_D)


def spiked(values, key, source, target, shards_of, factor):
    owner, partner = [(jnp.arange(values.shape[dim]) // (values.shape[dim] // shards_of)).reshape([-1 if axis == dim else 1 for axis in range(values.ndim)]) for dim in (source, target)]
    chosen = jax.random.permutation(key, shards_of)[partner]
    strong = (owner == chosen) | (owner == (partner + shards_of // 2) % shards_of)
    return jnp.where(strong, factor * values, values)


def levels(rng, extent, cuts, smallest, top_value):
    def one(dim, blocks):
        heights = jax.random.uniform(jax.random.fold_in(jax.random.fold_in(rng, 6), dim), (blocks,), jnp.float32, smallest / len(cuts), top_value / len(cuts))
        return jnp.repeat(jnp.exp(heights), extent[dim] // blocks).reshape((-1,) + (1,) * (len(extent) - dim - 1))

    level = one(*cuts[0])
    for cut in cuts[1:]:
        level = level * one(*cut)
    return level


def normal_values(rng, extent, scale, limit, cuts=(), kind=jnp.bfloat16):
    entries = jax.random.normal(rng, extent, jnp.float32) * scale
    if len(cuts) > 0:
        entries = levels(rng, extent, cuts, -0.22, 0.18) * entries
    return jnp.clip(entries, min=-limit, max=limit).astype(kind)


def heavy_noise(key, dims, scale, bound, cuts, heavy, held_as=jnp.bfloat16):
    entries = scale * jax.random.normal(key, dims, jnp.float32)
    if cuts:
        entries = entries * levels(key, dims, cuts, -0.22, 0.18)
    return jnp.clip(spiked(entries, jax.random.fold_in(key, 3), *heavy), -bound, bound).astype(held_as)


def setup_inputs(seed: int = 0) -> dict:
    seeds = jax.random.split(jax.random.key(seed), 17)
    return {
        "patches": normal_values(seeds[0], (DEVICES * ENC_DEV, D_E), 1.0, 6.0, ((0, 32),)),
        "send_counts": draw_send_counts(jax.random.fold_in(seeds[16], 71), 0),
        "dec_segment": draw_dec_segment(jax.random.fold_in(seeds[16], 71), 0),
        "source_index": draw_source_index(jax.random.fold_in(seeds[16], 71), 0),
        "cotangent": heavy_noise(seeds[4], (DEVICES * STRIPS, L, D_D), 1.0, 6.0, ((0, 32),), (0, 2, 32, 2.75), jnp.float32),
        "enc_norms": draw_enc_norms(jax.random.fold_in(seeds[16], 71), 0),
        "enc_qkv": normal_values(seeds[6], (D_E, 3 * D_E), D_E ** -0.5, 0.21875, ((0, 4), (1, 8)), jnp.float32),
        "enc_out": normal_values(seeds[7], (D_E, D_E), (D_E // 4) ** -0.5, 0.4375, ((0, 4), (1, 8)), jnp.float32),
        "enc_up": normal_values(seeds[8], (D_E, FF_E), D_E ** -0.5, 0.21875, ((0, 4), (1, 8)), jnp.float32),
        "enc_down": normal_values(seeds[9], (FF_E, D_E), FF_E ** -0.5, 0.109375, ((0, 4), (1, 8)), jnp.float32),
        "dec_norms": draw_dec_norms(jax.random.fold_in(seeds[16], 71), 0),
        "dec_embed": normal_values(seeds[11], (D_E, D_D), D_E ** -0.5, 0.21875, ((0, 4), (1, 8)), jnp.float32),
        "dec_qkv": normal_values(seeds[12], (D_D, 3 * D_D), D_D ** -0.5, 0.25, ((0, 4), (1, 8)), jnp.float32),
        "dec_out": normal_values(seeds[13], (D_D, D_D), (D_D // 4) ** -0.5, 0.5, ((0, 4), (1, 8)), jnp.float32),
        "dec_up": normal_values(seeds[14], (D_D, FF_D), D_D ** -0.5, 0.25, ((0, 4), (1, 8)), jnp.float32),
        "dec_down": normal_values(seeds[15], (FF_D, D_D), FF_D ** -0.5, 0.125, ((0, 4), (1, 8)), jnp.float32),
    }


EPSILON = 1e-06
NEGATIVE = -1000000000.0
BEST = lax.Precision.HIGHEST

@jax.custom_vjp
def low(v):
    return lax.optimization_barrier(v.astype(jnp.bfloat16)).astype(jnp.float32)

@jax.custom_vjp
def low_back(v):
    return v

def low_keep(v):
    return (low(v), None)

def low_pass(kept, grad):
    return (grad,)

def back_keep(v):
    return (v, None)

def back_low(kept, grad):
    return (low(grad),)
low.defvjp(low_keep, low_pass)
low_back.defvjp(back_keep, back_low)

def layer_norm(values, scale_gain, norm_shift):
    row_mean = lax.optimization_barrier(jnp.mean(values, axis=-1, keepdims=True))
    centred = values - row_mean
    spread = lax.optimization_barrier(jnp.mean(centred * centred, axis=-1, keepdims=True))
    return centred * lax.rsqrt(spread + EPSILON) * scale_gain + norm_shift

def attend(joined_qkv, allowed, head_count):
    groups, row_count, triple = joined_qkv.shape
    width = triple // 3
    head_size = width // head_count
    pieces = joined_qkv.reshape(groups, row_count, 3, head_count, head_size)
    scores = jnp.einsum('grhd,gshd->ghrs', pieces[:, :, 0], pieces[:, :, 1], precision=BEST) * head_size ** (-0.5)
    scores = low_back(scores)
    probability = jax.nn.softmax(jnp.where(allowed[:, None], scores, NEGATIVE), axis=-1)
    mixture = jnp.einsum('ghrs,gshd->grhd', low(probability), pieces[:, :, 2], precision=BEST)
    return mixture.reshape(groups, row_count, width)

def block(inputs, params, allowed, head_count):
    norm_rows, w_qkv, w_out, w_up, w_down = params
    h_one = low(layer_norm(inputs, norm_rows[0], norm_rows[1]))
    joined_qkv = low_back(low(jnp.einsum('grw,wc->grc', h_one, w_qkv, precision=BEST)))
    mixture = low_back(low(attend(joined_qkv, allowed, head_count)))
    x_one = inputs + low_back(jnp.einsum('grw,wc->grc', mixture, w_out, precision=BEST))
    h_two = low(layer_norm(x_one, norm_rows[2], norm_rows[3]))
    up_proj = low_back(jnp.einsum('grw,wc->grc', h_two, w_up, precision=BEST))
    activated = low(jax.nn.gelu(up_proj, approximate=False))
    return x_one + low_back(jnp.einsum('grf,fw->grw', activated, w_down, precision=BEST))

def reference(patches, send_counts, dec_segment, source_index, cotangent, enc_norms, enc_qkv, enc_out, enc_up, enc_down, dec_norms, dec_embed, dec_qkv, dec_out, dec_up, dec_down):
    device_count = N_DP * N_FSDP
    slot_rows = CAP
    slot_index = jnp.arange(slot_rows, dtype=jnp.int32)
    live_slot = slot_index[None, None, :] >= (slot_rows - send_counts)[:, :, None]
    enc_allowed = jnp.broadcast_to(live_slot[:, :, None, :], (device_count, N_DP, slot_rows, slot_rows))
    segments = dec_segment.reshape(device_count, STRIPS, L)
    sources = source_index.reshape(device_count, STRIPS, L)
    device_ids = jnp.arange(device_count, dtype=jnp.int32)[:, None, None]
    dp_index = device_ids // N_FSDP
    fsdp_index = device_ids % N_FSDP
    sender = sources // slot_rows
    within = sources % slot_rows
    visible = sources >= 0
    global_row = (sender * N_FSDP + fsdp_index) * ENC_DEV + dp_index * slot_rows + within
    global_row = jnp.where(visible, global_row, 0).astype(jnp.int32)
    masters = (enc_norms, enc_qkv, enc_out, enc_up, enc_down, dec_norms, dec_embed, dec_qkv, dec_out, dec_up, dec_down)

    def forward(patch_values, master_values):
        params = tuple((low(master) for master in master_values))
        enc_params = params[:5]
        dec_gains = params[5]
        enc_rows = patch_values.reshape(device_count, N_DP, slot_rows, D_E)

        def enc_step(operands):
            return block(operands[0], enc_params, operands[1], HEADS_E)
        enc_result = lax.map(jax.checkpoint(enc_step), (enc_rows, enc_allowed))
        enc_send = low(low_back(enc_result)).reshape(device_count * ENC_DEV, D_E)
        embedded = low_back(low(jnp.dot(enc_send, params[6], precision=BEST) + dec_gains[7]))
        dec_start = jnp.where(visible[..., None], embedded[global_row], dec_gains[6])
        dec_params = (dec_gains, params[7], params[8], params[9], params[10])

        def dec_step(operands):
            allowed = operands[1][:, :, None] == operands[1][:, None, :]
            finished = block(operands[0], dec_params, allowed, HEADS_D)
            return layer_norm(finished, dec_gains[4], dec_gains[5])
        return lax.map(jax.checkpoint(dec_step), (dec_start, segments))
    decoded, pullback = jax.vjp(forward, patches.astype(jnp.float32), masters)
    d_patch, d_masters = pullback(cotangent.astype(jnp.float32).reshape(decoded.shape))
    return (decoded.reshape(cotangent.shape), d_patch, d_masters[0], d_masters[1], d_masters[2], d_masters[3], d_masters[4], d_masters[5], d_masters[6], d_masters[7], d_masters[8], d_masters[9], d_masters[10])
```

```python
import dataclasses
import functools

import jax
import jax.numpy as jnp
from jax import lax
from jax.experimental import pallas as pl
from jax.experimental.pallas import tpu as pltpu
from jax.sharding import PartitionSpec as P

HEADS_E = 12
HEADS_D = 16


EPSILON = 1e-06
NEGATIVE = -1000000000.0
MESH = pl.DeviceIdType.MESH
BF16 = jnp.bfloat16
F32 = jnp.float32


@dataclasses.dataclass(frozen=True)
class Entry:
    rows: int
    width: int
    by_core: bool

    @property
    def q(self):
        return self.width // 2 if self.by_core else self.width // 4

    @property
    def part(self):
        return self.rows // 2 if self.by_core else self.rows

    @property
    def whole(self):
        if self.by_core:
            return (4, 2, 2, self.part, self.width)
        return (4, 2, self.part, self.width)

    @property
    def cut(self):
        return -(-self.part // 32) * 16


def entry_of(rows, width):
    return Entry(rows, width, (width // 4) % 128 != 0)


def region(e, ref, zs, xs, rows, y, c):
    if e.by_core:
        return ref.at[zs, xs, c, rows, pl.ds(pl.multiple_of(y * e.q, 128), e.q)]
    return ref.at[zs, xs, rows, pl.ds(pl.multiple_of((2 * y + c) * e.q, 128), e.q)]


def region_pair(e, ref, zs, xs, rows, c):
    if e.by_core:
        return [ref.at[zs, xs, c, rows, :]]
    return [region(e, ref, zs, xs, rows, y, c) for y in range(2)]


def place():
    d, s = lax.axis_index("dp"), lax.axis_index("fsdp")
    return d // 2, lax.rem(d, 2), s // 2, lax.rem(s, 2)


def at(z, x, y, c):
    return (z * 2 + x, y * 2 + c)


def greet(z, x, y, c):
    barrier = pltpu.get_barrier_semaphore()
    peers = [at(lax.rem(z + k, 4), x, y, c) for k in (1, 2, 3)]
    peers += [at(z, 1 - x, y, c), at(z, x, 1 - y, c), at(z, x, y, 1 - c)]
    for peer in peers:
        pl.semaphore_signal(barrier, inc=1, device_id=peer, device_id_type=MESH)
    pl.semaphore_wait(barrier, len(peers))


def send(src, dst, sems, i, k, peer):
    return pltpu.make_async_remote_copy(
        src_ref=src,
        dst_ref=dst,
        send_sem=sems[0].at[i, k],
        recv_sem=sems[1].at[i, k],
        device_id=peer,
        device_id_type=MESH,
    )


ALL = slice(None)


def gather_stages(e, i, piece, out, sems, local_sem):
    z, x, y, c = place()
    top, bottom = slice(0, e.cut), slice(e.cut, e.part)

    def first():
        here = region(e, out, z, x, ALL, y, c)
        return [
            send(piece, here, sems, i, k - 1, at(lax.rem(z + k, 4), x, y, c)) for k in (1, 2, 3)
        ]

    def local():
        return pltpu.make_async_copy(piece, region(e, out, z, x, ALL, y, c), local_sem.at[i])

    def second():
        a = region(e, out, ALL, x, top, y, c)
        b = region(e, out, ALL, x, bottom, y, c)
        return [
            send(a, a, sems, i, 3, at(z, 1 - x, y, c)),
            send(b, b, sems, i, 4, at(z, x, 1 - y, c)),
        ]

    def third():
        a = region(e, out, ALL, ALL, top, y, c)
        found = [send(a, a, sems, i, 5, at(z, x, 1 - y, c))]
        for k, b in enumerate(region_pair(e, out, ALL, x, bottom, c)):
            found.append(send(b, b, sems, i, 6 + k, at(z, 1 - x, y, c)))
        return found

    def fourth():
        return [
            send(b, b, sems, i, 8 + k, at(z, x, y, 1 - c))
            for k, b in enumerate(region_pair(e, out, ALL, ALL, ALL, c))
        ]

    return local, [first, second, third, fourth]


def gather_kernel(entries, *refs):
    n = len(entries)
    pieces, outs = refs[:n], refs[n : 2 * n]
    send_sem, recv_sem, local_sem = refs[2 * n :]
    sems = (send_sem, recv_sem)
    z, x, y, c = place()
    plans = [
        gather_stages(e, i, pieces[i], outs[i], sems, local_sem) for i, e in enumerate(entries)
    ]
    locals_ = [plan[0]() for plan in plans]
    for copy in locals_:
        copy.start()
    greet(z, x, y, c)
    moving = {}
    for t in range(n + 4):
        for stage in (3, 2, 1, 0):
            i = t - stage
            if not 0 <= i < n:
                continue
            if stage > 0:
                for copy in moving[i, stage - 1]:
                    copy.wait_recv()
                if stage == 1:
                    locals_[i].wait()
            moving[i, stage] = plans[i][1][stage]()
            for copy in moving[i, stage]:
                copy.start()
    for i in range(n):
        for copy in moving[i, 3]:
            copy.wait_recv()
        for stage in range(4):
            for copy in moving[i, stage]:
                copy.wait_send()


def gather_all(entries, pieces):
    any_space = pl.BlockSpec(memory_space=pl.ANY)
    n = len(entries)
    return pl.pallas_call(
        functools.partial(gather_kernel, entries),
        out_shape=[jax.ShapeDtypeStruct(e.whole, BF16) for e in entries],
        in_specs=[any_space] * n,
        out_specs=[any_space] * n,
        scratch_shapes=[
            pltpu.SemaphoreType.DMA((n, 10)),
            pltpu.SemaphoreType.DMA((n, 10)),
            pltpu.SemaphoreType.DMA((n,)),
        ],
        compiler_params=pltpu.CompilerParams(
            collective_id=0, has_side_effects=True, vmem_limit_bytes=16 << 20
        ),
        name="gather_weights",
    )(*pieces)


def add_into(dst, src, count):
    def step(i, carry):
        dst[i] = (dst[i].astype(F32) + src[i].astype(F32)).astype(BF16)
        return carry

    lax.fori_loop(0, count, step, 0)


def reduce_stages(e, i, grad, out, buf, sems, local_sem):
    z, x, y, c = place()
    acc, r4, r3a, r3b, r2a, r2b, r1 = buf
    q, cut, part = e.q, e.cut, e.part
    top, bottom = slice(0, cut), slice(cut, part)

    def lanes(y):
        return pl.ds(pl.multiple_of(y * q, 128), q)

    def pair(ref):
        return [ref] if e.by_core else [ref.at[:, :, :, pl.ds(k * q, q)] for k in range(2)]

    def local():
        mine = zip(region_pair(e, grad, ALL, ALL, ALL, c), pair(acc))
        return [
            pltpu.make_async_copy(src, dst, local_sem.at[i, k]) for k, (src, dst) in enumerate(mine)
        ]

    def first():
        theirs = zip(region_pair(e, grad, ALL, ALL, ALL, 1 - c), pair(r4))
        return [
            send(src, dst, sems, i, k, at(z, x, y, 1 - c)) for k, (src, dst) in enumerate(theirs)
        ]

    def add_first():
        def step(k, carry):
            a, b = k // 2, lax.rem(k, 2)
            acc[a, b] = (acc[a, b].astype(F32) + r4[a, b].astype(F32)).astype(BF16)
            return carry

        lax.fori_loop(0, 8, step, 0)

    def second():
        return [
            send(acc.at[:, :, top, lanes(1 - y)], r3a, sems, i, 2, at(z, x, 1 - y, c)),
            send(acc.at[:, 1 - x, bottom, :], r3b, sems, i, 3, at(z, 1 - x, y, c)),
        ]

    def add_second():
        def step(k, carry):
            for b in range(2):
                acc[k, b, top, lanes(y)] = (
                    acc[k, b, top, lanes(y)].astype(F32) + r3a[k, b].astype(F32)
                ).astype(BF16)
            acc[k, x, bottom, :] = (
                acc[k, x, bottom, :].astype(F32) + r3b[k].astype(F32)
            ).astype(BF16)
            return carry

        lax.fori_loop(0, 4, step, 0)

    def third():
        return [
            send(acc.at[:, 1 - x, top, lanes(y)], r2a, sems, i, 4, at(z, 1 - x, y, c)),
            send(acc.at[:, x, bottom, lanes(1 - y)], r2b, sems, i, 5, at(z, x, 1 - y, c)),
        ]

    def add_third():
        def step(k, carry):
            acc[k, x, top, lanes(y)] = (
                acc[k, x, top, lanes(y)].astype(F32) + r2a[k].astype(F32)
            ).astype(BF16)
            acc[k, x, bottom, lanes(y)] = (
                acc[k, x, bottom, lanes(y)].astype(F32) + r2b[k].astype(F32)
            ).astype(BF16)
            return carry

        lax.fori_loop(0, 4, step, 0)

    def fourth():
        found = []
        for k in (1, 2, 3):
            there = lax.rem(z + k, 4)
            found.append(
                send(acc.at[there, x, :, lanes(y)], r1.at[k - 1], sems, i, 5 + k, at(there, x, y, c))
            )
        return found

    def add_fourth():
        total = acc[z, x, :, lanes(y)].astype(F32)
        for k in range(3):
            total = total + r1[k].astype(F32)
        out[...] = total

    return local, [(first, add_first), (second, add_second), (third, add_third), (fourth, add_fourth)]


def reduce_buffers(e):
    return [
        (4, 2, e.part, 2 * e.q),
        (4, 2, e.part, 2 * e.q),
        (4, 2, e.cut, e.q),
        (4, e.part - e.cut, 2 * e.q),
        (4, e.cut, e.q),
        (4, e.part - e.cut, e.q),
        (3, e.part, e.q),
    ]


def reduce_kernel(entries, *refs):
    n = len(entries)
    grads, outs = refs[:n], refs[n : 2 * n]
    bufs = [refs[2 * n + 7 * i : 2 * n + 7 * i + 7] for i in range(n)]
    send_sem, recv_sem, local_sem = refs[9 * n :]
    sems = (send_sem, recv_sem)
    z, x, y, c = place()
    plans = [
        reduce_stages(e, i, grads[i], outs[i], bufs[i], sems, local_sem)
        for i, e in enumerate(entries)
    ]
    locals_ = [plan[0]() for plan in plans]
    for copies in locals_:
        for copy in copies:
            copy.start()
    greet(z, x, y, c)
    moving = {}
    for t in range(n + 4):
        for stage in (4, 3, 2, 1, 0):
            i = t - stage
            if not 0 <= i < n:
                continue
            if stage > 0:
                for copy in moving[i, stage - 1]:
                    copy.wait_recv()
                if stage == 1:
                    for copy in locals_[i]:
                        copy.wait()
                plans[i][1][stage - 1][1]()
            if stage < 4:
                moving[i, stage] = plans[i][1][stage][0]()
                for copy in moving[i, stage]:
                    copy.start()
    for i in range(n):
        for stage in range(4):
            for copy in moving[i, stage]:
                copy.wait_send()


def reduce_all(entries, grads):
    any_space = pl.BlockSpec(memory_space=pl.ANY)
    n = len(entries)
    scratch = [pltpu.VMEM(shape, BF16) for e in entries for shape in reduce_buffers(e)]
    return pl.pallas_call(
        functools.partial(reduce_kernel, entries),
        out_shape=[jax.ShapeDtypeStruct((e.part, e.q), F32) for e in entries],
        in_specs=[any_space] * n,
        out_specs=[pl.BlockSpec(memory_space=pltpu.VMEM)] * n,
        scratch_shapes=scratch
        + [
            pltpu.SemaphoreType.DMA((n, 9)),
            pltpu.SemaphoreType.DMA((n, 9)),
            pltpu.SemaphoreType.DMA((n, 2)),
        ],
        compiler_params=pltpu.CompilerParams(
            collective_id=1, has_side_effects=True, vmem_limit_bytes=56 << 20
        ),
        name="reduce_gradients",
    )(*grads)


CORE_SWAP = [(0, 1), (1, 0), (2, 3), (3, 2)]
NORM_ROWS = 32


def halves_to_pieces(blocks):
    c = lax.rem(lax.axis_index("fsdp"), 2)
    both = jnp.concatenate([b.reshape(2, b.shape[0] // 2, b.shape[1]) for b in blocks], axis=1)
    mine = lax.dynamic_index_in_dim(both, c, 0, keepdims=False)
    other = lax.dynamic_index_in_dim(both, 1 - c, 0, keepdims=False)
    came = lax.ppermute(other, "fsdp", CORE_SWAP)
    left, right = jnp.where(c == 0, mine, came), jnp.where(c == 0, came, mine)
    return jnp.concatenate([left, right], axis=1)


def pieces_to_halves(pieces):
    c = lax.rem(lax.axis_index("fsdp"), 2)
    whole = jnp.concatenate(pieces, axis=0)
    q = whole.shape[1] // 2
    left, right = whole[:, :q], whole[:, q:]
    mine, other = jnp.where(c == 0, left, right), jnp.where(c == 0, right, left)
    came = lax.ppermute(other, "fsdp", CORE_SWAP)
    first, second = jnp.where(c == 0, mine, came), jnp.where(c == 0, came, mine)
    sizes = [p.shape[0] for p in pieces]
    ends = [sum(sizes[:k]) for k in range(1, len(sizes))]
    return [
        jnp.concatenate([a, b], axis=0)
        for a, b in zip(jnp.split(first, ends, axis=0), jnp.split(second, ends, axis=0))
    ]


def gather_masters(staged, enc_norms, dec_norms, weights):
    blocks = [w.astype(BF16).T for w in weights]
    if not staged:
        whole = []
        for b in blocks:
            tall = lax.all_gather(b, "dp", axis=0, tiled=True)
            whole.append(lax.all_gather(tall, "fsdp", axis=1, tiled=True))
        norms = []
        for rows in (enc_norms, dec_norms):
            wide = lax.all_gather(rows.astype(BF16), "dp", axis=1, tiled=True)
            norms.append(lax.all_gather(wide, "fsdp", axis=0, tiled=True))
        return norms[0], norms[1], whole
    entries = [entry_of(b.shape[0], 4 * b.shape[1]) for b in blocks]
    pieces = list(blocks)
    cores = [k for k, e in enumerate(entries) if e.by_core]
    joined = halves_to_pieces([blocks[k] for k in cores])
    start = 0
    for k in cores:
        pieces[k] = lax.slice_in_dim(joined, start, start + entries[k].part, axis=0)
        start += entries[k].part
    small = jnp.zeros((NORM_ROWS, 128), BF16)
    small = small.at[: enc_norms.shape[0], : enc_norms.shape[1]].set(enc_norms.astype(BF16))
    half = NORM_ROWS // 2
    small = small.at[half : half + dec_norms.shape[0], : dec_norms.shape[1]].set(
        dec_norms.astype(BF16)
    )
    entries = [entry_of(NORM_ROWS, 512)] + entries
    whole = gather_all(entries, [small] + pieces)
    tiles = whole[0].reshape(8, NORM_ROWS, 4, 128)
    norms = []
    for start, rows in ((0, enc_norms), (half, dec_norms)):
        n, width = rows.shape
        part = tiles[:, start : start + n, :, :width]
        norms.append(part.transpose(2, 1, 0, 3).reshape(4 * n, 8 * width))
    return norms[0], norms[1], [w.reshape(-1, e.width) for w, e in zip(whole[1:], entries[1:])]


def reduce_masters(staged, g_enc_norms, g_dec_norms, grads):
    if not staged:
        def owner(value, rows, lanes):
            part = lax.psum_scatter(value.astype(BF16), "fsdp", scatter_dimension=lanes, tiled=True)
            return sum_at_owner(part, "dp", rows)

        return (
            owner(g_enc_norms, 1, 0),
            owner(g_dec_norms, 1, 0),
            [owner(g, 0, 1).T for g in grads],
        )
    entries = [entry_of(g.shape[0] // 8, g.shape[1]) for g in grads]
    values = [g.astype(BF16).reshape(e.whole) for g, e in zip(grads, entries)]
    half = NORM_ROWS // 2
    tiles = jnp.zeros((8, NORM_ROWS, 4, 128), BF16)
    for start, rows in ((0, g_enc_norms), (half, g_dec_norms)):
        n, width = rows.shape[0] // 4, rows.shape[1] // 8
        part = rows.astype(BF16).reshape(4, n, 8, width).transpose(2, 1, 0, 3)
        tiles = tiles.at[:, start : start + n, :, :width].set(part)
    small = entry_of(NORM_ROWS, 512)
    sums = reduce_all([small] + entries, [tiles.reshape(small.whole)] + values)
    blocks = list(sums[1:])
    cores = [k for k, e in enumerate(entries) if e.by_core]
    for k, b in zip(cores, pieces_to_halves([blocks[k] for k in cores])):
        blocks[k] = b
    n_enc, w_enc = g_enc_norms.shape[0] // 4, g_enc_norms.shape[1] // 8
    n_dec, w_dec = g_dec_norms.shape[0] // 4, g_dec_norms.shape[1] // 8
    return (
        sums[0][:n_enc, :w_enc],
        sums[0][half : half + n_dec, :w_dec],
        [b.T for b in blocks],
    )


def in_blocks(value, dim, length):
    dims = value.shape
    pieces = value.reshape(*dims[:dim], length, dims[dim] // length, *dims[dim + 1 :])
    return jnp.moveaxis(pieces, dim, 0)


def sum_at_owner(value, axis, dim):
    length = lax.axis_size(axis)
    pieces = lax.all_to_all(in_blocks(value, dim, length), axis, 0, 0, tiled=True)
    return jnp.sum(pieces.astype(jnp.float32), axis=0)


def layer_norm(values, scale_gain, norm_shift):
    row_mean = jnp.mean(values, axis=-1, keepdims=True)
    centred = values - row_mean
    spread = jnp.mean(centred * centred, axis=-1, keepdims=True)
    return centred * lax.rsqrt(spread + EPSILON) * scale_gain + norm_shift


def gelu_exact(values):
    return jax.nn.gelu(values, approximate=False)


def project(left_side, right_side):
    return jnp.einsum("grw,cw->grc", left_side, right_side, preferred_element_type=jnp.float32)


def project_back(gradient, right_side):
    return jnp.einsum("grc,cw->grw", gradient, right_side, preferred_element_type=jnp.float32)


def outer_sum(left_side, gradient):
    return jnp.einsum("grc,grw->cw", gradient, left_side, preferred_element_type=jnp.float32)


def split_heads(joined_qkv, head_count):
    groups, row_count, triple = joined_qkv.shape
    head_size = triple // 3 // head_count
    pieces = joined_qkv.reshape(groups, row_count, 3, head_count, head_size)
    return (pieces[:, :, 0], pieces[:, :, 1], pieces[:, :, 2], head_size)


def scores_of(queries, key_part, allowed, head_size):
    raw_scores = jnp.einsum(
        "grhd,gshd->ghrs", queries, key_part, preferred_element_type=jnp.float32
    ) * head_size ** (-0.5)
    return jnp.where(allowed[:, None], raw_scores, NEGATIVE)


def attend(joined_qkv, allowed, head_count):
    queries, key_part, values, head_size = split_heads(joined_qkv, head_count)
    scores = scores_of(queries, key_part, allowed, head_size)
    row_max = jnp.max(scores, axis=-1, keepdims=True)
    weights = jnp.exp(scores - row_max)
    row_total = jnp.sum(weights, axis=-1, keepdims=True)
    probability = weights / row_total
    log_total = row_max + jnp.log(row_total)
    mixture = jnp.einsum(
        "ghrs,gshd->grhd",
        probability.astype(jnp.bfloat16),
        values,
        preferred_element_type=jnp.float32,
    )
    return (mixture.reshape(joined_qkv.shape[0], joined_qkv.shape[1], -1), log_total)


def attend_back(joined_qkv, allowed, head_count, log_total, d_mixed):
    queries, key_part, values, head_size = split_heads(joined_qkv, head_count)
    scores = scores_of(queries, key_part, allowed, head_size)
    probability = jnp.exp(scores - log_total)
    groups, row_count = (d_mixed.shape[0], d_mixed.shape[1])
    d_heads = d_mixed.reshape(groups, row_count, head_count, head_size)
    d_probs = jnp.einsum("grhd,gshd->ghrs", d_heads, values, preferred_element_type=jnp.float32)
    d_value = jnp.einsum(
        "ghrs,grhd->gshd",
        probability.astype(jnp.bfloat16),
        d_heads,
        preferred_element_type=jnp.float32,
    )
    centre = jnp.sum(d_probs * probability, axis=-1, keepdims=True)
    d_scores = (probability * (d_probs - centre)).astype(jnp.bfloat16)
    score_scale = head_size ** (-0.5)
    d_query = (
        jnp.einsum("ghrs,gshd->grhd", d_scores, key_part, preferred_element_type=jnp.float32)
        * score_scale
    )
    d_key = (
        jnp.einsum("ghrs,grhd->gshd", d_scores, queries, preferred_element_type=jnp.float32)
        * score_scale
    )
    stacked = jnp.stack([d_query, d_key, d_value], axis=2)
    return stacked.reshape(groups, row_count, -1).astype(jnp.bfloat16)


def block_forward(inputs, params, allowed, head_count):
    norm_rows, w_qkv, w_out, w_up, w_down = params
    gain_rows = norm_rows.astype(jnp.float32)
    h_one = layer_norm(inputs, gain_rows[0], gain_rows[1]).astype(jnp.bfloat16)
    joined_qkv = project(h_one, w_qkv).astype(jnp.bfloat16)
    mixture, log_total = attend(joined_qkv, allowed, head_count)
    mixture = mixture.astype(jnp.bfloat16)
    x_one = inputs + project(mixture, w_out)
    h_two = layer_norm(x_one, gain_rows[2], gain_rows[3]).astype(jnp.bfloat16)
    up_proj = project(h_two, w_up)
    activated = gelu_exact(up_proj).astype(jnp.bfloat16)
    x_two = x_one + project(activated, w_down)
    return (x_two, (joined_qkv, log_total, mixture, x_one, up_proj))


def block_backward(inputs, params, allowed, head_count, stored, d_two):
    norm_rows, w_qkv, w_out, w_up, w_down = params
    gain_rows = norm_rows.astype(jnp.float32)
    joined_qkv, log_total, mixture, x_one, up_proj = stored
    d_branch = d_two.astype(jnp.bfloat16)
    activated, gelu_pull = jax.vjp(gelu_exact, up_proj)
    g_down = outer_sum(activated.astype(jnp.bfloat16), d_branch)
    d_up = gelu_pull(project_back(d_branch, w_down))[0].astype(jnp.bfloat16)
    h_two, norm_two_pull = jax.vjp(layer_norm, x_one, gain_rows[2], gain_rows[3])
    g_up = outer_sum(h_two.astype(jnp.bfloat16), d_up)
    d_x_two_norm, d_gain_two, d_shift_two = norm_two_pull(project_back(d_up, w_up))
    d_one = d_two + d_x_two_norm
    d_attn = d_one.astype(jnp.bfloat16)
    g_out = outer_sum(mixture, d_attn)
    d_mixed = project_back(d_attn, w_out).astype(jnp.bfloat16)
    d_qkv = attend_back(joined_qkv, allowed, head_count, log_total, d_mixed)
    h_one, norm_one_pull = jax.vjp(layer_norm, inputs, gain_rows[0], gain_rows[1])
    g_qkv = outer_sum(h_one.astype(jnp.bfloat16), d_qkv)
    d_x_one_norm, d_gain_one, d_shift_one = norm_one_pull(project_back(d_qkv, w_qkv))
    g_norms = jnp.stack([d_gain_one, d_shift_one, d_gain_two, d_shift_two])
    return (d_one + d_x_one_norm, (g_norms, g_qkv, g_out, g_up, g_down))


def per_device(
    staged,
    patches,
    send_counts,
    dec_segment,
    source_index,
    cotangent,
    enc_norms,
    enc_qkv,
    enc_out,
    enc_up,
    enc_down,
    dec_norms,
    dec_embed,
    dec_qkv,
    dec_out,
    dec_up,
    dec_down,
):
    peer_count = lax.axis_size("dp")
    width_enc = patches.shape[1]
    slot_rows = patches.shape[0] // peer_count
    masters = (enc_qkv, enc_out, enc_up, enc_down, dec_embed, dec_qkv, dec_out, dec_up, dec_down)
    norms_e, norms_d, whole = gather_masters(staged, enc_norms, dec_norms, masters)
    enc_rows = patches.astype(jnp.float32).reshape(peer_count, slot_rows, width_enc)
    live_counts = send_counts.reshape(peer_count)
    live_rows = (
        jnp.arange(slot_rows, dtype=jnp.int32)[None, :] >= (slot_rows - live_counts)[:, None]
    )
    enc_allowed = jnp.broadcast_to(live_rows[:, None, :], (peer_count, slot_rows, slot_rows))
    enc_params = (norms_e, *whole[:4])
    enc_result, enc_stored = block_forward(enc_rows, enc_params, enc_allowed, HEADS_E)
    enc_send = enc_result.astype(jnp.bfloat16)
    dec_gains = norms_d.astype(jnp.float32)
    w_embed = whole[4]
    embedded = (project(enc_send, w_embed) + dec_gains[7]).astype(jnp.bfloat16)
    arrived = lax.all_to_all(embedded, "dp", split_axis=0, concat_axis=0, tiled=True)
    slot_count = peer_count * slot_rows
    slot_table = arrived.reshape(slot_count, -1)
    visible = source_index >= 0
    picked = jnp.take(slot_table, jnp.where(visible, source_index, 0), axis=0)
    dec_start = jnp.where(visible[..., None], picked.astype(jnp.float32), dec_gains[6])
    dec_allowed = dec_segment[:, :, None] == dec_segment[:, None, :]
    dec_params = (norms_d, *whole[5:])
    dec_two, dec_stored = block_forward(dec_start, dec_params, dec_allowed, HEADS_D)
    decoded, final_pull = jax.vjp(layer_norm, dec_two, dec_gains[4], dec_gains[5])
    d_final, d_gain_final, d_shift_final = final_pull(cotangent)
    d_start, dec_grads = block_backward(
        dec_start, dec_params, dec_allowed, HEADS_D, dec_stored, d_final
    )
    d_token = jnp.sum(jnp.where(visible[..., None], 0.0, d_start), axis=(0, 1))
    d_picked = jnp.where(visible[..., None], d_start, 0.0).astype(jnp.bfloat16)
    d_table = jnp.zeros((slot_count, d_start.shape[-1]), jnp.bfloat16)
    d_table = d_table.at[jnp.where(visible, source_index, slot_count)].set(d_picked, mode="drop")
    d_table = d_table.reshape(peer_count, slot_rows, -1)
    returned = lax.all_to_all(d_table, "dp", split_axis=0, concat_axis=0, tiled=True)
    g_embed = outer_sum(enc_send, returned)
    d_bias = jnp.sum(returned.astype(jnp.float32), axis=(0, 1))
    d_enc = project_back(returned, w_embed).astype(jnp.bfloat16)
    d_patches, enc_grads = block_backward(
        enc_rows, enc_params, enc_allowed, HEADS_E, enc_stored, d_enc.astype(jnp.float32)
    )
    g_dec_norms = jnp.concatenate(
        [dec_grads[0], jnp.stack([d_gain_final, d_shift_final, d_token, d_bias])], axis=0
    )
    s_enc_norms, s_dec_norms, sums = reduce_masters(
        staged, enc_grads[0], g_dec_norms, [*enc_grads[1:], g_embed, *dec_grads[1:]]
    )
    return (
        decoded,
        d_patches.reshape(-1, width_enc),
        s_enc_norms,
        *sums[:4],
        s_dec_norms,
        *sums[4:],
    )


def solution(mesh):
    placed = (
        P(("dp", "fsdp"), None),
        P(("dp", "fsdp"), None),
        P(("dp", "fsdp"), None),
        P(("dp", "fsdp"), None),
        P(("dp", "fsdp"), None, None),
        P("fsdp", "dp"),
        P("fsdp", "dp"),
        P("fsdp", "dp"),
        P("fsdp", "dp"),
        P("fsdp", "dp"),
        P("fsdp", "dp"),
        P("fsdp", "dp"),
        P("fsdp", "dp"),
        P("fsdp", "dp"),
        P("fsdp", "dp"),
        P("fsdp", "dp"),
    )
    staged = (mesh.shape["dp"], mesh.shape["fsdp"]) == (8, 4)
    return jax.shard_map(
        functools.partial(per_device, staged),
        mesh=mesh,
        in_specs=placed,
        out_specs=(
            P(("dp", "fsdp"), None, None),
            P(("dp", "fsdp"), None),
            P("fsdp", "dp"),
            P("fsdp", "dp"),
            P("fsdp", "dp"),
            P("fsdp", "dp"),
            P("fsdp", "dp"),
            P("fsdp", "dp"),
            P("fsdp", "dp"),
            P("fsdp", "dp"),
            P("fsdp", "dp"),
            P("fsdp", "dp"),
            P("fsdp", "dp"),
        ),
        check_vma=False,
    )
```

```python
import dataclasses
import functools

import jax
import jax.numpy as jnp
from jax import lax
from jax.experimental import pallas as pl
from jax.experimental.pallas import tpu as pltpu
from jax.sharding import PartitionSpec as P

HEADS_E = 12
HEADS_D = 16


EPSILON = 1e-06
NEGATIVE = -1000000000.0
LANES = 128
MESH = pl.DeviceIdType.MESH
BF16 = jnp.bfloat16
F32 = jnp.float32


def in_blocks(value, dim, length):
    dims = value.shape
    pieces = value.reshape(*dims[:dim], length, dims[dim] // length, *dims[dim + 1 :])
    return jnp.moveaxis(pieces, dim, 0)


def sum_at_owner(value, axis, dim):
    length = lax.axis_size(axis)
    pieces = lax.all_to_all(in_blocks(value, dim, length), axis, 0, 0, tiled=True)
    return jnp.sum(pieces.astype(jnp.float32), axis=0)


@dataclasses.dataclass(frozen=True)
class Entry:
    rows: int
    width: int
    by_core: bool

    @property
    def q(self):
        return self.width // 2 if self.by_core else self.width // 4

    @property
    def part(self):
        return self.rows // 2 if self.by_core else self.rows

    @property
    def whole(self):
        if self.by_core:
            return (4, 2, 2, self.part, self.width)
        return (4, 2, self.part, self.width)

    @property
    def cut(self):
        return -(-self.part // 32) * 16


def entry_of(rows, width):
    return Entry(rows, width, (width // 4) % 128 != 0)


def region(e, ref, zs, xs, rows, y, c):
    if e.by_core:
        return ref.at[zs, xs, c, rows, pl.ds(pl.multiple_of(y * e.q, 128), e.q)]
    return ref.at[zs, xs, rows, pl.ds(pl.multiple_of((2 * y + c) * e.q, 128), e.q)]


def region_pair(e, ref, zs, xs, rows, c):
    if e.by_core:
        return [ref.at[zs, xs, c, rows, :]]
    return [region(e, ref, zs, xs, rows, y, c) for y in range(2)]


def place():
    d, s = lax.axis_index("dp"), lax.axis_index("fsdp")
    return d // 2, lax.rem(d, 2), s // 2, lax.rem(s, 2)


def at(z, x, y, c):
    return (z * 2 + x, y * 2 + c)


def greet(z, x, y, c):
    barrier = pltpu.get_barrier_semaphore()
    peers = [at(lax.rem(z + k, 4), x, y, c) for k in (1, 2, 3)]
    peers += [at(z, 1 - x, y, c), at(z, x, 1 - y, c), at(z, x, y, 1 - c)]
    for peer in peers:
        pl.semaphore_signal(barrier, inc=1, device_id=peer, device_id_type=MESH)
    pl.semaphore_wait(barrier, len(peers))


def send(src, dst, sems, i, k, peer):
    return pltpu.make_async_remote_copy(
        src_ref=src,
        dst_ref=dst,
        send_sem=sems[0].at[i, k],
        recv_sem=sems[1].at[i, k],
        device_id=peer,
        device_id_type=MESH,
    )


ALL = slice(None)


def gather_stages(e, i, piece, out, sems, local_sem):
    z, x, y, c = place()
    top, bottom = slice(0, e.cut), slice(e.cut, e.part)

    def first():
        here = region(e, out, z, x, ALL, y, c)
        return [
            send(piece, here, sems, i, k - 1, at(lax.rem(z + k, 4), x, y, c)) for k in (1, 2, 3)
        ]

    def local():
        return pltpu.make_async_copy(piece, region(e, out, z, x, ALL, y, c), local_sem.at[i])

    def second():
        a = region(e, out, ALL, x, top, y, c)
        b = region(e, out, ALL, x, bottom, y, c)
        return [
            send(a, a, sems, i, 3, at(z, 1 - x, y, c)),
            send(b, b, sems, i, 4, at(z, x, 1 - y, c)),
        ]

    def third():
        a = region(e, out, ALL, ALL, top, y, c)
        found = [send(a, a, sems, i, 5, at(z, x, 1 - y, c))]
        for k, b in enumerate(region_pair(e, out, ALL, x, bottom, c)):
            found.append(send(b, b, sems, i, 6 + k, at(z, 1 - x, y, c)))
        return found

    def fourth():
        return [
            send(b, b, sems, i, 8 + k, at(z, x, y, 1 - c))
            for k, b in enumerate(region_pair(e, out, ALL, ALL, ALL, c))
        ]

    return local, [first, second, third, fourth]


def gather_kernel(entries, *refs):
    n = len(entries)
    pieces, outs = refs[:n], refs[n : 2 * n]
    send_sem, recv_sem, local_sem = refs[2 * n :]
    sems = (send_sem, recv_sem)
    z, x, y, c = place()
    plans = [
        gather_stages(e, i, pieces[i], outs[i], sems, local_sem) for i, e in enumerate(entries)
    ]
    locals_ = [plan[0]() for plan in plans]
    for copy in locals_:
        copy.start()
    greet(z, x, y, c)
    moving = {}
    for t in range(n + 4):
        for stage in (3, 2, 1, 0):
            i = t - stage
            if not 0 <= i < n:
                continue
            if stage > 0:
                for copy in moving[i, stage - 1]:
                    copy.wait_recv()
                if stage == 1:
                    locals_[i].wait()
            moving[i, stage] = plans[i][1][stage]()
            for copy in moving[i, stage]:
                copy.start()
    for i in range(n):
        for copy in moving[i, 3]:
            copy.wait_recv()
        for stage in range(4):
            for copy in moving[i, stage]:
                copy.wait_send()


def gather_all(entries, pieces):
    any_space = pl.BlockSpec(memory_space=pl.ANY)
    n = len(entries)
    return pl.pallas_call(
        functools.partial(gather_kernel, entries),
        out_shape=[jax.ShapeDtypeStruct(e.whole, BF16) for e in entries],
        in_specs=[any_space] * n,
        out_specs=[any_space] * n,
        scratch_shapes=[
            pltpu.SemaphoreType.DMA((n, 10)),
            pltpu.SemaphoreType.DMA((n, 10)),
            pltpu.SemaphoreType.DMA((n,)),
        ],
        compiler_params=pltpu.CompilerParams(
            collective_id=0, has_side_effects=True, vmem_limit_bytes=16 << 20
        ),
        name="gather_weights",
    )(*pieces)


def add_into(dst, src, count):
    def step(i, carry):
        dst[i] = (dst[i].astype(F32) + src[i].astype(F32)).astype(BF16)
        return carry

    lax.fori_loop(0, count, step, 0)


def reduce_stages(e, i, grad, out, buf, sems, local_sem):
    z, x, y, c = place()
    acc, r4, r3a, r3b, r2a, r2b, r1 = buf
    q, cut, part = e.q, e.cut, e.part
    top, bottom = slice(0, cut), slice(cut, part)

    def lanes(y):
        return pl.ds(pl.multiple_of(y * q, 128), q)

    def pair(ref):
        return [ref] if e.by_core else [ref.at[:, :, :, pl.ds(k * q, q)] for k in range(2)]

    def local():
        mine = zip(region_pair(e, grad, ALL, ALL, ALL, c), pair(acc))
        return [
            pltpu.make_async_copy(src, dst, local_sem.at[i, k]) for k, (src, dst) in enumerate(mine)
        ]

    def first():
        theirs = zip(region_pair(e, grad, ALL, ALL, ALL, 1 - c), pair(r4))
        return [
            send(src, dst, sems, i, k, at(z, x, y, 1 - c)) for k, (src, dst) in enumerate(theirs)
        ]

    def add_first():
        def step(k, carry):
            a, b = k // 2, lax.rem(k, 2)
            acc[a, b] = (acc[a, b].astype(F32) + r4[a, b].astype(F32)).astype(BF16)
            return carry

        lax.fori_loop(0, 8, step, 0)

    def second():
        return [
            send(acc.at[:, :, top, lanes(1 - y)], r3a, sems, i, 2, at(z, x, 1 - y, c)),
            send(acc.at[:, 1 - x, bottom, :], r3b, sems, i, 3, at(z, 1 - x, y, c)),
        ]

    def add_second():
        def step(k, carry):
            for b in range(2):
                acc[k, b, top, lanes(y)] = (
                    acc[k, b, top, lanes(y)].astype(F32) + r3a[k, b].astype(F32)
                ).astype(BF16)
            acc[k, x, bottom, :] = (
                acc[k, x, bottom, :].astype(F32) + r3b[k].astype(F32)
            ).astype(BF16)
            return carry

        lax.fori_loop(0, 4, step, 0)

    def third():
        return [
            send(acc.at[:, 1 - x, top, lanes(y)], r2a, sems, i, 4, at(z, 1 - x, y, c)),
            send(acc.at[:, x, bottom, lanes(1 - y)], r2b, sems, i, 5, at(z, x, 1 - y, c)),
        ]

    def add_third():
        def step(k, carry):
            acc[k, x, top, lanes(y)] = (
                acc[k, x, top, lanes(y)].astype(F32) + r2a[k].astype(F32)
            ).astype(BF16)
            acc[k, x, bottom, lanes(y)] = (
                acc[k, x, bottom, lanes(y)].astype(F32) + r2b[k].astype(F32)
            ).astype(BF16)
            return carry

        lax.fori_loop(0, 4, step, 0)

    def fourth():
        found = []
        for k in (1, 2, 3):
            there = lax.rem(z + k, 4)
            found.append(
                send(acc.at[there, x, :, lanes(y)], r1.at[k - 1], sems, i, 5 + k, at(there, x, y, c))
            )
        return found

    def add_fourth():
        total = acc[z, x, :, lanes(y)].astype(F32)
        for k in range(3):
            total = total + r1[k].astype(F32)
        out[...] = total

    return local, [(first, add_first), (second, add_second), (third, add_third), (fourth, add_fourth)]


def reduce_buffers(e):
    return [
        (4, 2, e.part, 2 * e.q),
        (4, 2, e.part, 2 * e.q),
        (4, 2, e.cut, e.q),
        (4, e.part - e.cut, 2 * e.q),
        (4, e.cut, e.q),
        (4, e.part - e.cut, e.q),
        (3, e.part, e.q),
    ]


def reduce_kernel(entries, *refs):
    n = len(entries)
    grads, outs = refs[:n], refs[n : 2 * n]
    bufs = [refs[2 * n + 7 * i : 2 * n + 7 * i + 7] for i in range(n)]
    send_sem, recv_sem, local_sem = refs[9 * n :]
    sems = (send_sem, recv_sem)
    z, x, y, c = place()
    plans = [
        reduce_stages(e, i, grads[i], outs[i], bufs[i], sems, local_sem)
        for i, e in enumerate(entries)
    ]
    locals_ = [plan[0]() for plan in plans]
    for copies in locals_:
        for copy in copies:
            copy.start()
    greet(z, x, y, c)
    moving = {}
    for t in range(n + 4):
        for stage in (4, 3, 2, 1, 0):
            i = t - stage
            if not 0 <= i < n:
                continue
            if stage > 0:
                for copy in moving[i, stage - 1]:
                    copy.wait_recv()
                if stage == 1:
                    for copy in locals_[i]:
                        copy.wait()
                plans[i][1][stage - 1][1]()
            if stage < 4:
                moving[i, stage] = plans[i][1][stage][0]()
                for copy in moving[i, stage]:
                    copy.start()
    for i in range(n):
        for stage in range(4):
            for copy in moving[i, stage]:
                copy.wait_send()


def reduce_all(entries, grads):
    any_space = pl.BlockSpec(memory_space=pl.ANY)
    n = len(entries)
    scratch = [pltpu.VMEM(shape, BF16) for e in entries for shape in reduce_buffers(e)]
    return pl.pallas_call(
        functools.partial(reduce_kernel, entries),
        out_shape=[jax.ShapeDtypeStruct((e.part, e.q), F32) for e in entries],
        in_specs=[any_space] * n,
        out_specs=[pl.BlockSpec(memory_space=pltpu.VMEM)] * n,
        scratch_shapes=scratch
        + [
            pltpu.SemaphoreType.DMA((n, 9)),
            pltpu.SemaphoreType.DMA((n, 9)),
            pltpu.SemaphoreType.DMA((n, 2)),
        ],
        compiler_params=pltpu.CompilerParams(
            collective_id=1, has_side_effects=True, vmem_limit_bytes=56 << 20
        ),
        name="reduce_gradients",
    )(*grads)


CORE_SWAP = [(0, 1), (1, 0), (2, 3), (3, 2)]
NORM_ROWS = 32


def halves_to_pieces(blocks):
    c = lax.rem(lax.axis_index("fsdp"), 2)
    both = jnp.concatenate([b.reshape(2, b.shape[0] // 2, b.shape[1]) for b in blocks], axis=1)
    mine = lax.dynamic_index_in_dim(both, c, 0, keepdims=False)
    other = lax.dynamic_index_in_dim(both, 1 - c, 0, keepdims=False)
    came = lax.ppermute(other, "fsdp", CORE_SWAP)
    left, right = jnp.where(c == 0, mine, came), jnp.where(c == 0, came, mine)
    return jnp.concatenate([left, right], axis=1)


def pieces_to_halves(pieces):
    c = lax.rem(lax.axis_index("fsdp"), 2)
    whole = jnp.concatenate(pieces, axis=0)
    q = whole.shape[1] // 2
    left, right = whole[:, :q], whole[:, q:]
    mine, other = jnp.where(c == 0, left, right), jnp.where(c == 0, right, left)
    came = lax.ppermute(other, "fsdp", CORE_SWAP)
    first, second = jnp.where(c == 0, mine, came), jnp.where(c == 0, came, mine)
    sizes = [p.shape[0] for p in pieces]
    ends = [sum(sizes[:k]) for k in range(1, len(sizes))]
    return [
        jnp.concatenate([a, b], axis=0)
        for a, b in zip(jnp.split(first, ends, axis=0), jnp.split(second, ends, axis=0))
    ]


def gather_masters(staged, enc_norms, dec_norms, weights):
    blocks = [w.astype(BF16).T for w in weights]
    if not staged:
        whole = []
        for b in blocks:
            tall = lax.all_gather(b, "dp", axis=0, tiled=True)
            whole.append(lax.all_gather(tall, "fsdp", axis=1, tiled=True))
        norms = []
        for rows in (enc_norms, dec_norms):
            wide = lax.all_gather(rows.astype(BF16), "dp", axis=1, tiled=True)
            norms.append(lax.all_gather(wide, "fsdp", axis=0, tiled=True))
        return norms[0], norms[1], whole
    entries = [entry_of(b.shape[0], 4 * b.shape[1]) for b in blocks]
    pieces = list(blocks)
    cores = [k for k, e in enumerate(entries) if e.by_core]
    joined = halves_to_pieces([blocks[k] for k in cores])
    start = 0
    for k in cores:
        pieces[k] = lax.slice_in_dim(joined, start, start + entries[k].part, axis=0)
        start += entries[k].part
    small = jnp.zeros((NORM_ROWS, 128), BF16)
    small = small.at[: enc_norms.shape[0], : enc_norms.shape[1]].set(enc_norms.astype(BF16))
    half = NORM_ROWS // 2
    small = small.at[half : half + dec_norms.shape[0], : dec_norms.shape[1]].set(
        dec_norms.astype(BF16)
    )
    entries = [entry_of(NORM_ROWS, 512)] + entries
    whole = gather_all(entries, [small] + pieces)
    tiles = whole[0].reshape(8, NORM_ROWS, 4, 128)
    norms = []
    for start, rows in ((0, enc_norms), (half, dec_norms)):
        n, width = rows.shape
        part = tiles[:, start : start + n, :, :width]
        norms.append(part.transpose(2, 1, 0, 3).reshape(4 * n, 8 * width))
    return norms[0], norms[1], [w.reshape(-1, e.width) for w, e in zip(whole[1:], entries[1:])]


def reduce_masters(staged, g_enc_norms, g_dec_norms, grads):
    if not staged:
        def owner(value, rows, lanes):
            part = lax.psum_scatter(value.astype(BF16), "fsdp", scatter_dimension=lanes, tiled=True)
            return sum_at_owner(part, "dp", rows)

        return (
            owner(g_enc_norms, 1, 0),
            owner(g_dec_norms, 1, 0),
            [owner(g, 0, 1).T for g in grads],
        )
    entries = [entry_of(g.shape[0] // 8, g.shape[1]) for g in grads]
    values = [g.astype(BF16).reshape(e.whole) for g, e in zip(grads, entries)]
    half = NORM_ROWS // 2
    tiles = jnp.zeros((8, NORM_ROWS, 4, 128), BF16)
    for start, rows in ((0, g_enc_norms), (half, g_dec_norms)):
        n, width = rows.shape[0] // 4, rows.shape[1] // 8
        part = rows.astype(BF16).reshape(4, n, 8, width).transpose(2, 1, 0, 3)
        tiles = tiles.at[:, start : start + n, :, :width].set(part)
    small = entry_of(NORM_ROWS, 512)
    sums = reduce_all([small] + entries, [tiles.reshape(small.whole)] + values)
    blocks = list(sums[1:])
    cores = [k for k, e in enumerate(entries) if e.by_core]
    for k, b in zip(cores, pieces_to_halves([blocks[k] for k in cores])):
        blocks[k] = b
    n_enc, w_enc = g_enc_norms.shape[0] // 4, g_enc_norms.shape[1] // 8
    n_dec, w_dec = g_dec_norms.shape[0] // 4, g_dec_norms.shape[1] // 8
    return (
        sums[0][:n_enc, :w_enc],
        sums[0][half : half + n_dec, :w_dec],
        [b.T for b in blocks],
    )


def nn(a, b):
    return lax.dot_general(a, b, (((1,), (0,)), ((), ())), preferred_element_type=F32)


def nt(a, b):
    return lax.dot_general(a, b, (((1,), (1,)), ((), ())), preferred_element_type=F32)


def tn(a, b):
    return lax.dot_general(a, b, (((0,), (0,)), ((), ())), preferred_element_type=F32)


def unit(values):
    centred = values - jnp.mean(values, axis=-1, keepdims=True)
    scale = lax.rsqrt(jnp.mean(centred * centred, axis=-1, keepdims=True) + EPSILON)
    return centred * scale, scale


def unit_back(d_hat, hat, scale):
    along = jnp.mean(d_hat * hat, axis=-1, keepdims=True)
    return scale * (d_hat - jnp.mean(d_hat, axis=-1, keepdims=True) - hat * along)


def column_sum(values):
    return jnp.sum(values, axis=0, keepdims=True)


def gelu_pair(u):
    phi = 0.5 + 0.5 * lax.erf(u * 0.7071067811865476)
    return u * phi, phi + u * (0.3989422804014327 * jnp.exp(-0.5 * u * u))


def head_lanes(shape, head_size, h):
    return lax.broadcasted_iota(jnp.int32, shape, 1) // head_size == h


def pick(values, head_size, h):
    return jnp.where(head_lanes(values.shape, head_size, h), values, jnp.zeros_like(values))


def attend_tile(q, k, v, bias, head_size):
    v_t = v.astype(F32).T.astype(BF16)
    mixed, totals = [], []
    for h in range(LANES // head_size):
        scores = nt(pick(k, head_size, h), q) * head_size**-0.5 + bias
        top = jnp.max(scores, axis=0, keepdims=True)
        weight = jnp.exp(scores - top)
        total = jnp.sum(weight, axis=0, keepdims=True)
        part = nn(v_t[h * head_size : (h + 1) * head_size], weight.astype(BF16))
        mixed.append(part * (1.0 / total))
        totals.append(top + jnp.log(total))
    return jnp.concatenate(mixed, axis=0).T, totals


def attend_tile_back(q, k, v, d_mixed, bias, totals, head_size):
    k_t = k.astype(F32).T.astype(BF16)
    d_q, d_k, d_v = [], 0.0, 0.0
    for h in range(LANES // head_size):
        scores = nt(pick(k, head_size, h), q) * head_size**-0.5 + bias
        prob = jnp.exp(scores - totals[h])
        d_prob = nt(pick(v, head_size, h), d_mixed)
        centre = jnp.sum(d_prob * prob, axis=0, keepdims=True)
        d_score = (prob * (d_prob - centre)).astype(BF16)
        d_v = d_v + nn(prob.astype(BF16), pick(d_mixed, head_size, h))
        d_k = d_k + nn(d_score, pick(q, head_size, h))
        d_q.append(nn(k_t[h * head_size : (h + 1) * head_size], d_score))
    d_q = jnp.concatenate(d_q, axis=0).T
    return d_q * head_size**-0.5, d_k * head_size**-0.5, d_v


def lane_tile(t):
    return pl.ds(pl.multiple_of(t * LANES, LANES), LANES)


def rows_of(i, n):
    return pl.ds(pl.multiple_of(i * n, 16), n)


def mask_bias(own, keys):
    return jnp.where(keys == own, 0.0, NEGATIVE).astype(F32)


def outer_loop(count, body):
    def step(i, carry):
        body(i)
        return carry

    lax.fori_loop(0, count, step, 0)


def weight_sum(dst, left, right, stage, sem):
    _, tile, width = stage.shape
    count = left.shape[1] // tile

    def off(t):
        slot = lax.rem(t, 2)
        rows = pl.ds(pl.multiple_of(t * tile, LANES), tile)
        return pltpu.make_async_copy(stage.at[slot], dst.at[rows, :], sem.at[slot])

    def one(t):
        @pl.when(t >= 2)
        def _():
            off(t - 2).wait()

        cols = pl.ds(pl.multiple_of(t * tile, LANES), tile)
        stage[lax.rem(t, 2)] = tn(left[:, cols], right[...]).astype(BF16)
        off(t).start()

    outer_loop(count, one)
    for t in range(max(0, count - 2), count):
        off(t).wait()


def decoder_kernel(
    head_size,
    chunk,
    table,
    index_col,
    index_row,
    seg_col,
    seg_row,
    cot,
    norms,
    w_qkv,
    w_out,
    w_up,
    w_down,
    decoded,
    d_table,
    g_norms,
    g_qkv,
    g_out,
    g_up,
    g_down,
    x,
    h_one,
    qkv,
    mixed,
    totals,
    h_two,
    act,
    slope,
    d_up,
    e_two,
    e_one,
    bias,
    stage,
    stage_wide,
    sem,
):
    groups, n, width = cot.shape
    real = decoded.shape[1]
    rows = groups * n
    per_group = n // chunk
    tiles = width // LANES
    per_tile = LANES // head_size
    gain = [norms[k : k + 1, :].astype(F32) for k in range(8)]
    g_norms[...] = jnp.zeros_like(g_norms)
    d_x = cot

    def start(i):
        r = rows_of(i, chunk)
        slots = lax.broadcasted_iota(jnp.int32, (chunk, table.shape[0]), 1)
        named = index_col[r, :]
        chosen = jnp.where(slots == named, 1.0, 0.0).astype(BF16)
        picked = nn(chosen, table[...])
        begin = jnp.where(named >= 0, picked, gain[6])
        x[r, :] = begin
        hat, _ = unit(begin)
        h = (hat * gain[0] + gain[1]).astype(BF16)
        h_one[r, :] = h
        qkv[r, :] = nt(h, w_qkv[...]).astype(BF16)

    outer_loop(rows // chunk, start)

    def attend(g):
        bias[...] = mask_bias(seg_row[g], seg_col[rows_of(g, n), :])
        r = rows_of(g, n)

        def one(t):
            q, k, v = [qkv[r, lane_tile(t + j * tiles)] for j in range(3)]
            out, logs = attend_tile(q, k, v, bias[...], head_size)
            mixed[r, lane_tile(t)] = out.astype(BF16)
            for h in range(per_tile):
                totals[g * tiles + t, h : h + 1, :] = logs[h]

        outer_loop(tiles, one)

    outer_loop(groups, attend)

    def middle(i):
        g, j = i // per_group, lax.rem(i, per_group)
        r = rows_of(i, chunk)
        one = x[r, :] + nt(mixed[r, :], w_out[...])
        hat_two, scale_two = unit(one)
        h = (hat_two * gain[2] + gain[3]).astype(BF16)
        h_two[r, :] = h
        step = 512
        for t in range(w_up.shape[0] // step):
            u = nt(h, w_up[t * step : (t + 1) * step, :])
            a, s = gelu_pair(u)
            act[r, t * step : (t + 1) * step] = a.astype(BF16)
            slope[:, t * step : (t + 1) * step] = s.astype(BF16)
        two = one + nt(act[r, :], w_down[...])
        hat, scale = unit(two)
        result = hat * gain[4] + gain[5]
        for b in range(groups):
            for c in range(per_group):
                lo = c * chunk
                hi = min(lo + chunk, real)

                @pl.when(i == b * per_group + c)
                def _(b=b, lo=lo, hi=hi):
                    decoded[b, lo:hi, :] = result[: hi - lo]

        cr = rows_of(j, chunk)
        d = cot[g, cr, :]
        g_norms[4:5, :] += column_sum(d * hat)
        g_norms[5:6, :] += column_sum(d)
        d_two = unit_back(d * gain[4], hat, scale)
        e = d_two.astype(BF16)
        e_two[r, :] = e
        for t in range(w_up.shape[0] // step):
            cols = slice(t * step, (t + 1) * step)
            d_act = nn(e, w_down[:, cols])
            d_up[r, cols] = (d_act * slope[:, cols].astype(F32)).astype(BF16)
        d_h = nn(d_up[r, :], w_up[...])
        g_norms[2:3, :] += column_sum(d_h * hat_two)
        g_norms[3:4, :] += column_sum(d_h)
        d_one = d_two + unit_back(d_h * gain[2], hat_two, scale_two)
        d_x[g, cr, :] = d_one
        e_one[r, :] = d_one.astype(BF16)

    outer_loop(rows // chunk, middle)

    weight_sum(g_down, e_two, act, stage_wide, sem)
    weight_sum(g_up, d_up, h_two, stage, sem)
    weight_sum(g_out, e_one, mixed, stage, sem)

    def mix_back(i):
        r = rows_of(i, chunk)
        mixed[r, :] = nn(e_one[r, :], w_out[...]).astype(BF16)

    outer_loop(rows // chunk, mix_back)
    d_qkv = act

    def attend_back(g):
        bias[...] = mask_bias(seg_row[g], seg_col[rows_of(g, n), :])
        r = rows_of(g, n)

        def one(t):
            q, k, v = [qkv[r, lane_tile(t + j * tiles)] for j in range(3)]
            logs = [totals[g * tiles + t, h : h + 1, :] for h in range(per_tile)]
            found = attend_tile_back(q, k, v, mixed[r, lane_tile(t)], bias[...], logs, head_size)
            for j in range(3):
                d_qkv[r, lane_tile(t + j * tiles)] = found[j].astype(BF16)

        outer_loop(tiles, one)

    outer_loop(groups, attend_back)

    weight_sum(g_qkv, d_qkv.at[:, : 3 * width], h_one, stage, sem)

    def finish(i):
        g, j = i // per_group, lax.rem(i, per_group)
        r, cr = rows_of(i, chunk), rows_of(j, chunk)
        d_h = nn(d_qkv[r, : 3 * width], w_qkv[...])
        hat, scale = unit(x[r, :])
        g_norms[0:1, :] += column_sum(d_h * hat)
        g_norms[1:2, :] += column_sum(d_h)
        d_start = d_x[g, cr, :] + unit_back(d_h * gain[0], hat, scale)
        seen = index_col[r, :] >= 0
        g_norms[6:7, :] += column_sum(jnp.where(seen, 0.0, d_start))
        e_two[r, :] = jnp.where(seen, d_start, 0.0).astype(BF16)

    outer_loop(rows // chunk, finish)

    def back(s):
        sr = rows_of(s, 128)
        slots = lax.broadcasted_iota(jnp.int32, (128, rows), 0) + s * 128
        chosen = jnp.where(slots == index_row[...], 1.0, 0.0).astype(BF16)
        d_table[sr, :] = nn(chosen, e_two[...]).astype(BF16)

    outer_loop(table.shape[0] // 128, back)


def decoder(table, index, segment, cotangent, norms, weights, heads):
    groups, real, width = cotangent.shape
    n = -(-real // 32) * 32
    chunk = n // 2
    rows = groups * n
    head_size = width // heads
    pad = n - real
    index = jnp.pad(index, ((0, 0), (0, pad)), constant_values=-1).reshape(rows)
    segment = jnp.pad(segment, ((0, 0), (0, pad)), constant_values=-1)
    cot = jnp.pad(cotangent, ((0, 0), (0, pad), (0, 0)))
    tiles = width // LANES
    ff = weights[2].shape[0]
    vm = pl.BlockSpec(memory_space=pltpu.VMEM)
    return pl.pallas_call(
        functools.partial(decoder_kernel, head_size, chunk),
        out_shape=[
            jax.ShapeDtypeStruct(cotangent.shape, F32),
            jax.ShapeDtypeStruct(table.shape, BF16),
            jax.ShapeDtypeStruct((8, width), F32),
        ]
        + [jax.ShapeDtypeStruct(w.shape, BF16) for w in weights],
        in_specs=[vm] * 11,
        out_specs=[vm] * 3 + [pl.BlockSpec(memory_space=pl.ANY)] * 4,
        scratch_shapes=[
            pltpu.VMEM((rows, width), F32),
            pltpu.VMEM((rows, width), BF16),
            pltpu.VMEM((rows, 3 * width), BF16),
            pltpu.VMEM((rows, width), BF16),
            pltpu.VMEM((groups * tiles, LANES // head_size, n), F32),
            pltpu.VMEM((rows, width), BF16),
            pltpu.VMEM((rows, ff), BF16),
            pltpu.VMEM((chunk, ff), BF16),
            pltpu.VMEM((rows, ff), BF16),
            pltpu.VMEM((rows, width), BF16),
            pltpu.VMEM((rows, width), BF16),
            pltpu.VMEM((n, n), F32),
            pltpu.VMEM((2, 256, width), BF16),
            pltpu.VMEM((2, LANES, ff), BF16),
            pltpu.SemaphoreType.DMA((2,)),
        ],
        compiler_params=pltpu.CompilerParams(vmem_limit_bytes=60 << 20),
        name="decoder",
    )(
        table,
        index[:, None],
        index[None, :],
        segment.reshape(rows, 1),
        segment[:, None, :],
        cot,
        norms,
        *weights,
    )


def encoder_kernel(
    head_size,
    groups,
    chunk,
    patches,
    key_col,
    own_row,
    norms,
    shift,
    w_qkv,
    w_out,
    w_up,
    w_down,
    w_embed,
    embedded,
    qkv,
    totals,
    mixed,
    x_one,
    act,
    slope,
    sent,
):
    rows, width = patches.shape
    n = rows // groups
    tiles = width // LANES
    per_tile = LANES // head_size
    gain = [norms[k : k + 1, :].astype(F32) for k in range(4)]
    add = shift[7:8, :].astype(F32)

    def start(i):
        r = rows_of(i, chunk)
        hat, _ = unit(patches[r, :].astype(F32))
        qkv[r, :] = nt((hat * gain[0] + gain[1]).astype(BF16), w_qkv[...]).astype(BF16)

    outer_loop(rows // chunk, start)

    def attend(g):
        r = rows_of(g, n)
        bias = mask_bias(own_row[g], key_col[r, :])
        for t in range(tiles):
            q, k, v = [qkv[r, (t + j * tiles) * LANES : (t + j * tiles + 1) * LANES] for j in range(3)]
            out, logs = attend_tile(q, k, v, bias, head_size)
            mixed[r, t * LANES : (t + 1) * LANES] = out.astype(BF16)
            for h in range(per_tile):
                totals[g, t * per_tile + h : t * per_tile + h + 1, :] = logs[h]

    outer_loop(groups, attend)

    def middle(i):
        r = rows_of(i, chunk)
        one = patches[r, :].astype(F32) + nt(mixed[r, :], w_out[...])
        x_one[r, :] = one
        hat, _ = unit(one)
        h = (hat * gain[2] + gain[3]).astype(BF16)
        step = 512
        for t in range(w_up.shape[0] // step):
            u = nt(h, w_up[t * step : (t + 1) * step, :])
            a, s = gelu_pair(u)
            act[r, t * step : (t + 1) * step] = a.astype(BF16)
            slope[r, t * step : (t + 1) * step] = s.astype(BF16)
        two = (one + nt(act[r, :], w_down[...])).astype(BF16)
        sent[r, :] = two
        embedded[r, :] = (nt(two, w_embed[...]) + add).astype(BF16)

    outer_loop(rows // chunk, middle)


def encoder_back_kernel(
    head_size,
    groups,
    chunk,
    patches,
    key_col,
    own_row,
    norms,
    w_qkv,
    w_out,
    w_up,
    w_down,
    w_embed,
    d_table,
    qkv,
    totals,
    mixed,
    x_one,
    act,
    slope,
    sent,
    d_patches,
    g_norms,
    g_shift,
    g_qkv,
    g_out,
    g_up,
    g_down,
    g_embed,
    e_two,
    e_one,
    stage,
    stage_wide,
    sem,
):
    rows, width = patches.shape
    n = rows // groups
    tiles = width // LANES
    per_tile = LANES // head_size
    gain = [norms[k : k + 1, :].astype(F32) for k in range(4)]
    g_norms[...] = jnp.zeros_like(g_norms)
    g_shift[...] = jnp.zeros_like(g_shift)
    step = 512
    weight_sum(g_embed, d_table, sent, stage, sem)
    h_two = sent

    def middle(i):
        r = rows_of(i, chunk)
        d_emb = d_table[r, :]
        g_shift[0:1, :] += column_sum(d_emb.astype(F32))
        e = nn(d_emb, w_embed[...]).astype(BF16)
        e_two[r, :] = e
        for t in range(w_up.shape[0] // step):
            cols = slice(t * step, (t + 1) * step)
            d_act = nn(e, w_down[:, cols])
            slope[r, cols] = (d_act * slope[r, cols].astype(F32)).astype(BF16)
        d_h = nn(slope[r, :], w_up[...])
        hat, scale = unit(x_one[r, :])
        h_two[r, :] = (hat * gain[2] + gain[3]).astype(BF16)
        g_norms[2:3, :] += column_sum(d_h * hat)
        g_norms[3:4, :] += column_sum(d_h)
        d_one = e.astype(F32) + unit_back(d_h * gain[2], hat, scale)
        d_patches[r, :] = d_one
        e_one[r, :] = d_one.astype(BF16)

    outer_loop(rows // chunk, middle)
    weight_sum(g_down, e_two, act, stage_wide, sem)
    weight_sum(g_up, slope, h_two, stage, sem)
    weight_sum(g_out, e_one, mixed, stage, sem)

    def mix_back(i):
        r = rows_of(i, chunk)
        mixed[r, :] = nn(e_one[r, :], w_out[...]).astype(BF16)

    outer_loop(rows // chunk, mix_back)

    def attend_back(g):
        r = rows_of(g, n)
        bias = mask_bias(own_row[g], key_col[r, :])
        for t in range(tiles):
            cols = [slice((t + j * tiles) * LANES, (t + j * tiles + 1) * LANES) for j in range(3)]
            q, k, v = [qkv[r, col] for col in cols]
            logs = [totals[g, t * per_tile + h : t * per_tile + h + 1, :] for h in range(per_tile)]
            found = attend_tile_back(q, k, v, mixed[r, cols[0]], bias, logs, head_size)
            for j in range(3):
                act[r, cols[j]] = found[j].astype(BF16)

    outer_loop(groups, attend_back)
    h_one = h_two

    def finish(i):
        r = rows_of(i, chunk)
        d_h = nn(act[r, : 3 * width], w_qkv[...])
        hat, scale = unit(patches[r, :].astype(F32))
        h_one[r, :] = (hat * gain[0] + gain[1]).astype(BF16)
        g_norms[0:1, :] += column_sum(d_h * hat)
        g_norms[1:2, :] += column_sum(d_h)
        d_patches[r, :] += unit_back(d_h * gain[0], hat, scale)

    outer_loop(rows // chunk, finish)
    weight_sum(g_qkv, act.at[:, : 3 * width], h_one, stage, sem)


def slot_plan(peers, slot_rows):
    padded = -(-slot_rows // 16) * 16
    joined = max(1, 128 // padded)
    return padded, joined


def encoder(patches, counts, norms, shift, weights, embed, heads):
    peers = counts.shape[0]
    width = patches.shape[1]
    slot_rows = patches.shape[0] // peers
    padded, joined = slot_plan(peers, slot_rows)
    rows, groups = peers * padded, peers // joined
    n = rows // groups
    head_size = width // heads
    x = jnp.pad(patches.reshape(peers, slot_rows, width), ((0, 0), (0, padded - slot_rows), (0, 0)))
    x = x.reshape(rows, width)
    row = jnp.arange(padded, dtype=jnp.int32)[None, :]
    slot = jnp.arange(peers, dtype=jnp.int32)[:, None]
    live = (row >= slot_rows - counts[:, None]) & (row < slot_rows)
    keys = jnp.where(live, slot, -1).reshape(rows, 1)
    own = jnp.broadcast_to(slot, (peers, padded)).reshape(groups, 1, n)
    ff = weights[2].shape[0]
    vm = pl.BlockSpec(memory_space=pltpu.VMEM)
    shapes = [
        ((rows, weights[0].shape[0]), BF16),
        ((groups, -(-heads // 8) * 8, n), F32),
        ((rows, width), BF16),
        ((rows, width), F32),
        ((rows, ff), BF16),
        ((rows, ff), BF16),
        ((rows, width), BF16),
    ]
    shapes = [jax.ShapeDtypeStruct(s, t) for s, t in shapes]
    embedded, *stored = pl.pallas_call(
        functools.partial(encoder_kernel, head_size, groups, 2 * n),
        out_shape=[jax.ShapeDtypeStruct((rows, embed.shape[0]), BF16)] + shapes,
        in_specs=[vm] * 10,
        out_specs=[vm] * 8,
        compiler_params=pltpu.CompilerParams(vmem_limit_bytes=60 << 20),
        name="encoder",
    )(x, keys, own, norms, shift, *weights, embed)
    return embedded, (x, keys, own), stored


def encoder_back(rows_in, norms, weights, embed, d_table, stored, heads):
    x, keys, own = rows_in
    rows, width = x.shape
    groups, _, n = own.shape
    head_size = width // heads
    vm = pl.BlockSpec(memory_space=pltpu.VMEM)
    return pl.pallas_call(
        functools.partial(encoder_back_kernel, head_size, groups, 2 * n),
        out_shape=[
            jax.ShapeDtypeStruct((rows, width), F32),
            jax.ShapeDtypeStruct((8, width), F32),
            jax.ShapeDtypeStruct((8, embed.shape[0]), F32),
        ]
        + [jax.ShapeDtypeStruct(w.shape, BF16) for w in weights]
        + [jax.ShapeDtypeStruct(embed.shape, BF16)],
        in_specs=[vm] * 17,
        out_specs=[vm] * 3 + [pl.BlockSpec(memory_space=pl.ANY)] * 5,
        scratch_shapes=[pltpu.VMEM((rows, width), BF16)] * 2
        + [
            pltpu.VMEM((2, 256, width), BF16),
            pltpu.VMEM((2, LANES, weights[2].shape[0]), BF16),
            pltpu.SemaphoreType.DMA((2,)),
        ],
        compiler_params=pltpu.CompilerParams(vmem_limit_bytes=62 << 20),
        name="encoder_back",
    )(x, keys, own, norms, *weights, embed, d_table, *stored)


def per_device(
    staged,
    patches,
    send_counts,
    dec_segment,
    source_index,
    cotangent,
    enc_norms,
    enc_qkv,
    enc_out,
    enc_up,
    enc_down,
    dec_norms,
    dec_embed,
    dec_qkv,
    dec_out,
    dec_up,
    dec_down,
):
    peers = lax.axis_size("dp")
    width = patches.shape[1]
    slot_rows = patches.shape[0] // peers
    masters = (enc_qkv, enc_out, enc_up, enc_down, dec_embed, dec_qkv, dec_out, dec_up, dec_down)
    norms_e, norms_d, whole = gather_masters(staged, enc_norms, dec_norms, masters)
    enc_weights, embed, dec_weights = whole[:4], whole[4], whole[5:]
    embedded, enc_inputs, stored = encoder(
        patches, send_counts.reshape(peers), norms_e, norms_d, enc_weights, embed, HEADS_E
    )
    padded = embedded.shape[0] // peers

    def swap(table):
        slots = table.reshape(peers, padded, table.shape[1])
        return lax.all_to_all(slots, "dp", split_axis=0, concat_axis=0, tiled=True).reshape(table.shape)

    place_of = source_index // slot_rows * padded + source_index % slot_rows
    index = jnp.where(source_index >= 0, place_of, -1)
    decoded, d_table, g_dec_norms, *dec_grads = decoder(
        swap(embedded), index, dec_segment, cotangent, norms_d, dec_weights, HEADS_D
    )
    d_patches, g_enc_norms, g_shift, *enc_grads = encoder_back(
        enc_inputs, norms_e, enc_weights, embed, swap(d_table), stored, HEADS_E
    )
    g_dec_norms = jnp.concatenate([g_dec_norms[:7], g_shift[:1]], axis=0)
    s_enc_norms, s_dec_norms, sums = reduce_masters(
        staged, g_enc_norms[:4], g_dec_norms, [*enc_grads, *dec_grads]
    )
    d_patches = d_patches.reshape(peers, padded, width)[:, :slot_rows]
    return (
        decoded,
        d_patches.reshape(-1, width),
        s_enc_norms,
        *sums[:4],
        s_dec_norms,
        *sums[4:],
    )


def solution(mesh):
    placed = (
        P(("dp", "fsdp"), None),
        P(("dp", "fsdp"), None),
        P(("dp", "fsdp"), None),
        P(("dp", "fsdp"), None),
        P(("dp", "fsdp"), None, None),
        P("fsdp", "dp"),
        P("fsdp", "dp"),
        P("fsdp", "dp"),
        P("fsdp", "dp"),
        P("fsdp", "dp"),
        P("fsdp", "dp"),
        P("fsdp", "dp"),
        P("fsdp", "dp"),
        P("fsdp", "dp"),
        P("fsdp", "dp"),
        P("fsdp", "dp"),
    )
    staged = (mesh.shape["dp"], mesh.shape["fsdp"]) == (8, 4)
    return jax.shard_map(
        functools.partial(per_device, staged),
        mesh=mesh,
        in_specs=placed,
        out_specs=(
            P(("dp", "fsdp"), None, None),
            P(("dp", "fsdp"), None),
            P("fsdp", "dp"),
            P("fsdp", "dp"),
            P("fsdp", "dp"),
            P("fsdp", "dp"),
            P("fsdp", "dp"),
            P("fsdp", "dp"),
            P("fsdp", "dp"),
            P("fsdp", "dp"),
            P("fsdp", "dp"),
            P("fsdp", "dp"),
            P("fsdp", "dp"),
        ),
        check_vma=False,
    )
```

```python
import dataclasses
import functools

import jax
import jax.numpy as jnp
from jax import lax
from jax.experimental import pallas as pl
from jax.experimental.pallas import tpu as pltpu
from jax.sharding import PartitionSpec as P

HEADS_E = 12
HEADS_D = 16


EPSILON = 1e-06
NEGATIVE = -1000000000.0
LANES = 128
MESH = pl.DeviceIdType.MESH
BF16 = jnp.bfloat16
F32 = jnp.float32


def in_blocks(value, dim, length):
    dims = value.shape
    pieces = value.reshape(*dims[:dim], length, dims[dim] // length, *dims[dim + 1 :])
    return jnp.moveaxis(pieces, dim, 0)


def sum_at_owner(value, axis, dim):
    length = lax.axis_size(axis)
    pieces = lax.all_to_all(in_blocks(value, dim, length), axis, 0, 0, tiled=True)
    return jnp.sum(pieces.astype(jnp.float32), axis=0)


@dataclasses.dataclass(frozen=True)
class Entry:
    rows: int
    width: int
    by_core: bool

    @property
    def q(self):
        return self.width // 2 if self.by_core else self.width // 4

    @property
    def part(self):
        return self.rows // 2 if self.by_core else self.rows

    @property
    def whole(self):
        if self.by_core:
            return (4, 2, 2, self.part, self.width)
        return (4, 2, self.part, self.width)

    @property
    def cut(self):
        return -(-self.part // 32) * 16


def entry_of(rows, width):
    return Entry(rows, width, (width // 4) % 128 != 0)


def region(e, ref, zs, xs, rows, y, c):
    if e.by_core:
        return ref.at[zs, xs, c, rows, pl.ds(pl.multiple_of(y * e.q, 128), e.q)]
    return ref.at[zs, xs, rows, pl.ds(pl.multiple_of((2 * y + c) * e.q, 128), e.q)]


def region_pair(e, ref, zs, xs, rows, c):
    if e.by_core:
        return [ref.at[zs, xs, c, rows, :]]
    return [region(e, ref, zs, xs, rows, y, c) for y in range(2)]


def place():
    d, s = lax.axis_index("dp"), lax.axis_index("fsdp")
    return d // 2, lax.rem(d, 2), s // 2, lax.rem(s, 2)


def at(z, x, y, c):
    return (z * 2 + x, y * 2 + c)


def greet(z, x, y, c):
    barrier = pltpu.get_barrier_semaphore()
    peers = [at(lax.rem(z + k, 4), x, y, c) for k in (1, 2, 3)]
    peers += [at(z, 1 - x, y, c), at(z, x, 1 - y, c), at(z, x, y, 1 - c)]
    for peer in peers:
        pl.semaphore_signal(barrier, inc=1, device_id=peer, device_id_type=MESH)
    pl.semaphore_wait(barrier, len(peers))


def send(src, dst, sems, i, k, peer):
    return pltpu.make_async_remote_copy(
        src_ref=src,
        dst_ref=dst,
        send_sem=sems[0].at[i, k],
        recv_sem=sems[1].at[i, k],
        device_id=peer,
        device_id_type=MESH,
    )


ALL = slice(None)


def gather_stages(e, i, piece, out, sems, local_sem):
    z, x, y, c = place()
    top, bottom = slice(0, e.cut), slice(e.cut, e.part)

    def first():
        here = region(e, out, z, x, ALL, y, c)
        return [
            send(piece, here, sems, i, k - 1, at(lax.rem(z + k, 4), x, y, c)) for k in (1, 2, 3)
        ]

    def local():
        return pltpu.make_async_copy(piece, region(e, out, z, x, ALL, y, c), local_sem.at[i])

    def second():
        a = region(e, out, ALL, x, top, y, c)
        b = region(e, out, ALL, x, bottom, y, c)
        return [
            send(a, a, sems, i, 3, at(z, 1 - x, y, c)),
            send(b, b, sems, i, 4, at(z, x, 1 - y, c)),
        ]

    def third():
        a = region(e, out, ALL, ALL, top, y, c)
        found = [send(a, a, sems, i, 5, at(z, x, 1 - y, c))]
        for k, b in enumerate(region_pair(e, out, ALL, x, bottom, c)):
            found.append(send(b, b, sems, i, 6 + k, at(z, 1 - x, y, c)))
        return found

    def fourth():
        return [
            send(b, b, sems, i, 8 + k, at(z, x, y, 1 - c))
            for k, b in enumerate(region_pair(e, out, ALL, ALL, ALL, c))
        ]

    return local, [first, second, third, fourth]


def reduce_stages(e, i, grad, out, buf, sems, local_sem):
    z, x, y, c = place()
    acc, r4, r3a, r3b, r2a, r2b, r1 = buf
    q, cut, part = e.q, e.cut, e.part
    top, bottom = slice(0, cut), slice(cut, part)

    def lanes(y):
        return pl.ds(pl.multiple_of(y * q, 128), q)

    def pair(ref):
        return [ref] if e.by_core else [ref.at[:, :, :, pl.ds(k * q, q)] for k in range(2)]

    def local():
        mine = zip(region_pair(e, grad, ALL, ALL, ALL, c), pair(acc))
        return [
            pltpu.make_async_copy(src, dst, local_sem.at[i, k]) for k, (src, dst) in enumerate(mine)
        ]

    def first():
        theirs = zip(region_pair(e, grad, ALL, ALL, ALL, 1 - c), pair(r4))
        return [
            send(src, dst, sems, i, k, at(z, x, y, 1 - c)) for k, (src, dst) in enumerate(theirs)
        ]

    def add_first():
        def step(k, carry):
            a, b = k // 2, lax.rem(k, 2)
            acc[a, b] = (acc[a, b].astype(F32) + r4[a, b].astype(F32)).astype(BF16)
            return carry

        lax.fori_loop(0, 8, step, 0)

    def second():
        return [
            send(acc.at[:, :, top, lanes(1 - y)], r3a, sems, i, 2, at(z, x, 1 - y, c)),
            send(acc.at[:, 1 - x, bottom, :], r3b, sems, i, 3, at(z, 1 - x, y, c)),
        ]

    def add_second():
        def step(k, carry):
            for b in range(2):
                acc[k, b, top, lanes(y)] = (
                    acc[k, b, top, lanes(y)].astype(F32) + r3a[k, b].astype(F32)
                ).astype(BF16)
            acc[k, x, bottom, :] = (
                acc[k, x, bottom, :].astype(F32) + r3b[k].astype(F32)
            ).astype(BF16)
            return carry

        lax.fori_loop(0, 4, step, 0)

    def third():
        return [
            send(acc.at[:, 1 - x, top, lanes(y)], r2a, sems, i, 4, at(z, 1 - x, y, c)),
            send(acc.at[:, x, bottom, lanes(1 - y)], r2b, sems, i, 5, at(z, x, 1 - y, c)),
        ]

    def add_third():
        def step(k, carry):
            acc[k, x, top, lanes(y)] = (
                acc[k, x, top, lanes(y)].astype(F32) + r2a[k].astype(F32)
            ).astype(BF16)
            acc[k, x, bottom, lanes(y)] = (
                acc[k, x, bottom, lanes(y)].astype(F32) + r2b[k].astype(F32)
            ).astype(BF16)
            return carry

        lax.fori_loop(0, 4, step, 0)

    def fourth():
        found = []
        for k in (1, 2, 3):
            there = lax.rem(z + k, 4)
            found.append(
                send(acc.at[there, x, :, lanes(y)], r1.at[k - 1], sems, i, 5 + k, at(there, x, y, c))
            )
        return found

    def add_fourth():
        total = acc[z, x, :, lanes(y)].astype(F32)
        for k in range(3):
            total = total + r1[k].astype(F32)
        out[...] = total

    return local, [(first, add_first), (second, add_second), (third, add_third), (fourth, add_fourth)]


def reduce_buffers(e):
    return [
        (4, 2, e.part, 2 * e.q),
        (4, 2, e.part, 2 * e.q),
        (4, 2, e.cut, e.q),
        (4, e.part - e.cut, 2 * e.q),
        (4, e.cut, e.q),
        (4, e.part - e.cut, e.q),
        (3, e.part, e.q),
    ]


def reduce_kernel(entries, *refs):
    n = len(entries)
    grads, outs = refs[:n], refs[n : 2 * n]
    bufs = [refs[2 * n + 7 * i : 2 * n + 7 * i + 7] for i in range(n)]
    send_sem, recv_sem, local_sem = refs[9 * n :]
    sems = (send_sem, recv_sem)
    z, x, y, c = place()
    plans = [
        reduce_stages(e, i, grads[i], outs[i], bufs[i], sems, local_sem)
        for i, e in enumerate(entries)
    ]
    locals_ = [plan[0]() for plan in plans]
    for copies in locals_:
        for copy in copies:
            copy.start()
    greet(z, x, y, c)
    moving = {}
    for t in range(n + 4):
        for stage in (4, 3, 2, 1, 0):
            i = t - stage
            if not 0 <= i < n:
                continue
            if stage > 0:
                for copy in moving[i, stage - 1]:
                    copy.wait_recv()
                if stage == 1:
                    for copy in locals_[i]:
                        copy.wait()
                plans[i][1][stage - 1][1]()
            if stage < 4:
                moving[i, stage] = plans[i][1][stage][0]()
                for copy in moving[i, stage]:
                    copy.start()
    for i in range(n):
        for stage in range(4):
            for copy in moving[i, stage]:
                copy.wait_send()


def reduce_all(entries, grads):
    any_space = pl.BlockSpec(memory_space=pl.ANY)
    n = len(entries)
    scratch = [pltpu.VMEM(shape, BF16) for e in entries for shape in reduce_buffers(e)]
    return pl.pallas_call(
        functools.partial(reduce_kernel, entries),
        out_shape=[jax.ShapeDtypeStruct((e.part, e.q), F32) for e in entries],
        in_specs=[any_space] * n,
        out_specs=[pl.BlockSpec(memory_space=pltpu.VMEM)] * n,
        scratch_shapes=scratch
        + [
            pltpu.SemaphoreType.DMA((n, 9)),
            pltpu.SemaphoreType.DMA((n, 9)),
            pltpu.SemaphoreType.DMA((n, 2)),
        ],
        compiler_params=pltpu.CompilerParams(
            collective_id=1, has_side_effects=True, vmem_limit_bytes=56 << 20
        ),
        name="reduce_gradients",
    )(*grads)


CORE_SWAP = [(0, 1), (1, 0), (2, 3), (3, 2)]
NORM_ROWS = 32


def halves_to_pieces(blocks):
    c = lax.rem(lax.axis_index("fsdp"), 2)
    both = jnp.concatenate([b.reshape(2, b.shape[0] // 2, b.shape[1]) for b in blocks], axis=1)
    mine = lax.dynamic_index_in_dim(both, c, 0, keepdims=False)
    other = lax.dynamic_index_in_dim(both, 1 - c, 0, keepdims=False)
    came = lax.ppermute(other, "fsdp", CORE_SWAP)
    left, right = jnp.where(c == 0, mine, came), jnp.where(c == 0, came, mine)
    return jnp.concatenate([left, right], axis=1)


def pieces_to_halves(pieces):
    c = lax.rem(lax.axis_index("fsdp"), 2)
    whole = jnp.concatenate(pieces, axis=0)
    q = whole.shape[1] // 2
    left, right = whole[:, :q], whole[:, q:]
    mine, other = jnp.where(c == 0, left, right), jnp.where(c == 0, right, left)
    came = lax.ppermute(other, "fsdp", CORE_SWAP)
    first, second = jnp.where(c == 0, mine, came), jnp.where(c == 0, came, mine)
    sizes = [p.shape[0] for p in pieces]
    ends = [sum(sizes[:k]) for k in range(1, len(sizes))]
    return [
        jnp.concatenate([a, b], axis=0)
        for a, b in zip(jnp.split(first, ends, axis=0), jnp.split(second, ends, axis=0))
    ]


def gather_masters(enc_norms, dec_norms, weights):
    whole = []
    for w in weights:
        tall = lax.all_gather(w.astype(BF16).T, "dp", axis=0, tiled=True)
        whole.append(lax.all_gather(tall, "fsdp", axis=1, tiled=True))
    norms = []
    for rows in (enc_norms, dec_norms):
        wide = lax.all_gather(rows.astype(BF16), "dp", axis=1, tiled=True)
        norms.append(lax.all_gather(wide, "fsdp", axis=0, tiled=True))
    return norms[0], norms[1], whole


def staged_pieces(enc_norms, dec_norms, weights):
    blocks = [w.astype(BF16).T for w in weights]
    entries = [entry_of(b.shape[0], 4 * b.shape[1]) for b in blocks]
    pieces = list(blocks)
    cores = [k for k, e in enumerate(entries) if e.by_core]
    joined = halves_to_pieces([blocks[k] for k in cores])
    start = 0
    for k in cores:
        pieces[k] = lax.slice_in_dim(joined, start, start + entries[k].part, axis=0)
        start += entries[k].part
    small = jnp.zeros((NORM_ROWS, 128), BF16)
    small = small.at[: enc_norms.shape[0], : enc_norms.shape[1]].set(enc_norms.astype(BF16))
    half = NORM_ROWS // 2
    small = small.at[half : half + dec_norms.shape[0], : dec_norms.shape[1]].set(
        dec_norms.astype(BF16)
    )
    entries = [entry_of(NORM_ROWS, 512)] + entries
    return entries, [small] + pieces


def reduce_masters(staged, g_enc_norms, g_dec_norms, grads):
    if not staged:
        def owner(value, rows, lanes):
            part = lax.psum_scatter(value.astype(BF16), "fsdp", scatter_dimension=lanes, tiled=True)
            return sum_at_owner(part, "dp", rows)

        return (
            owner(g_enc_norms, 1, 0),
            owner(g_dec_norms, 1, 0),
            [owner(g, 0, 1).T for g in grads],
        )
    entries = [entry_of(g.shape[0] // 8, g.shape[1]) for g in grads]
    values = [g.astype(BF16).reshape(e.whole) for g, e in zip(grads, entries)]
    half = NORM_ROWS // 2
    tiles = jnp.zeros((8, NORM_ROWS, 4, 128), BF16)
    for start, rows in ((0, g_enc_norms), (half, g_dec_norms)):
        n, width = rows.shape[0] // 4, rows.shape[1] // 8
        part = rows.astype(BF16).reshape(4, n, 8, width).transpose(2, 1, 0, 3)
        tiles = tiles.at[:, start : start + n, :, :width].set(part)
    small = entry_of(NORM_ROWS, 512)
    sums = reduce_all([small] + entries, [tiles.reshape(small.whole)] + values)
    blocks = list(sums[1:])
    cores = [k for k, e in enumerate(entries) if e.by_core]
    for k, b in zip(cores, pieces_to_halves([blocks[k] for k in cores])):
        blocks[k] = b
    n_enc, w_enc = g_enc_norms.shape[0] // 4, g_enc_norms.shape[1] // 8
    n_dec, w_dec = g_dec_norms.shape[0] // 4, g_dec_norms.shape[1] // 8
    return (
        sums[0][:n_enc, :w_enc],
        sums[0][half : half + n_dec, :w_dec],
        [b.T for b in blocks],
    )


def nn(a, b):
    return lax.dot_general(a, b, (((1,), (0,)), ((), ())), preferred_element_type=F32)


def nt(a, b):
    return lax.dot_general(a, b, (((1,), (1,)), ((), ())), preferred_element_type=F32)


def tn(a, b):
    return lax.dot_general(a, b, (((0,), (0,)), ((), ())), preferred_element_type=F32)


def unit(values):
    centred = values - jnp.mean(values, axis=-1, keepdims=True)
    scale = lax.rsqrt(jnp.mean(centred * centred, axis=-1, keepdims=True) + EPSILON)
    return centred * scale, scale


def unit_back(d_hat, hat, scale):
    along = jnp.mean(d_hat * hat, axis=-1, keepdims=True)
    return scale * (d_hat - jnp.mean(d_hat, axis=-1, keepdims=True) - hat * along)


def column_sum(values):
    return jnp.sum(values, axis=0, keepdims=True)


def gelu_pair(u):
    phi = 0.5 + 0.5 * lax.erf(u * 0.7071067811865476)
    return u * phi, phi + u * (0.3989422804014327 * jnp.exp(-0.5 * u * u))


def head_lanes(shape, head_size, h):
    return lax.broadcasted_iota(jnp.int32, shape, 1) // head_size == h


def pick(values, head_size, h):
    return jnp.where(head_lanes(values.shape, head_size, h), values, jnp.zeros_like(values))


def attend_tile(q, k, v, bias, head_size):
    v_t = v.astype(F32).T.astype(BF16)
    mixed, totals = [], []
    for h in range(LANES // head_size):
        scores = nt(pick(k, head_size, h), q) * head_size**-0.5 + bias
        top = jnp.max(scores, axis=0, keepdims=True)
        weight = jnp.exp(scores - top)
        total = jnp.sum(weight, axis=0, keepdims=True)
        part = nn(v_t[h * head_size : (h + 1) * head_size], weight.astype(BF16))
        mixed.append(part * (1.0 / total))
        totals.append(top + jnp.log(total))
    return jnp.concatenate(mixed, axis=0).T, totals


def attend_tile_back(q, k, v, d_mixed, bias, totals, head_size):
    k_t = k.astype(F32).T.astype(BF16)
    d_q, d_k, d_v = [], 0.0, 0.0
    for h in range(LANES // head_size):
        scores = nt(pick(k, head_size, h), q) * head_size**-0.5 + bias
        prob = jnp.exp(scores - totals[h])
        d_prob = nt(pick(v, head_size, h), d_mixed)
        centre = jnp.sum(d_prob * prob, axis=0, keepdims=True)
        d_score = (prob * (d_prob - centre)).astype(BF16)
        d_v = d_v + nn(prob.astype(BF16), pick(d_mixed, head_size, h))
        d_k = d_k + nn(d_score, pick(q, head_size, h))
        d_q.append(nn(k_t[h * head_size : (h + 1) * head_size], d_score))
    d_q = jnp.concatenate(d_q, axis=0).T
    return d_q * head_size**-0.5, d_k * head_size**-0.5, d_v


def lane_tile(t):
    return pl.ds(pl.multiple_of(t * LANES, LANES), LANES)


def rows_of(i, n):
    return pl.ds(pl.multiple_of(i * n, 16), n)


def mask_bias(own, keys):
    return jnp.where(keys == own, 0.0, NEGATIVE).astype(F32)


def outer_loop(count, body):
    def step(i, carry):
        body(i)
        return carry

    lax.fori_loop(0, count, step, 0)


def weight_sum(dst, left, right, stage, sem):
    _, tile, width = stage.shape
    count = left.shape[1] // tile

    def off(t):
        slot = lax.rem(t, 2)
        rows = pl.ds(pl.multiple_of(t * tile, LANES), tile)
        return pltpu.make_async_copy(stage.at[slot], dst.at[rows, :], sem.at[slot])

    def one(t):
        @pl.when(t >= 2)
        def _():
            off(t - 2).wait()

        cols = pl.ds(pl.multiple_of(t * tile, LANES), tile)
        stage[lax.rem(t, 2)] = tn(left[:, cols], right[...]).astype(BF16)
        off(t).start()

    outer_loop(count, one)
    for t in range(max(0, count - 2), count):
        off(t).wait()


def decoder_kernel(
    head_size,
    chunk,
    table,
    index_col,
    index_row,
    seg_col,
    seg_row,
    cot,
    norms,
    w_qkv,
    w_out,
    w_up,
    w_down,
    decoded,
    d_table,
    g_norms,
    g_qkv,
    g_out,
    g_up,
    g_down,
    x,
    h_one,
    qkv,
    mixed,
    totals,
    h_two,
    act,
    slope,
    d_up,
    e_two,
    e_one,
    bias,
    stage,
    stage_wide,
    sem,
):
    groups, n, width = cot.shape
    real = decoded.shape[1]
    rows = groups * n
    per_group = n // chunk
    tiles = width // LANES
    per_tile = LANES // head_size
    gain = [norms[k : k + 1, :].astype(F32) for k in range(8)]
    g_norms[...] = jnp.zeros_like(g_norms)
    d_x = cot

    def start(i):
        r = rows_of(i, chunk)
        slots = lax.broadcasted_iota(jnp.int32, (chunk, table.shape[0]), 1)
        named = index_col[r, :]
        chosen = jnp.where(slots == named, 1.0, 0.0).astype(BF16)
        picked = nn(chosen, table[...])
        begin = jnp.where(named >= 0, picked, gain[6])
        x[r, :] = begin
        hat, _ = unit(begin)
        h = (hat * gain[0] + gain[1]).astype(BF16)
        h_one[r, :] = h
        qkv[r, :] = nt(h, w_qkv[...]).astype(BF16)

    outer_loop(rows // chunk, start)

    def attend(g):
        bias[...] = mask_bias(seg_row[g], seg_col[rows_of(g, n), :])
        r = rows_of(g, n)

        def one(t):
            q, k, v = [qkv[r, lane_tile(t + j * tiles)] for j in range(3)]
            out, logs = attend_tile(q, k, v, bias[...], head_size)
            mixed[r, lane_tile(t)] = out.astype(BF16)
            for h in range(per_tile):
                totals[g * tiles + t, h : h + 1, :] = logs[h]

        outer_loop(tiles, one)

    outer_loop(groups, attend)

    def middle(i):
        g, j = i // per_group, lax.rem(i, per_group)
        r = rows_of(i, chunk)
        one = x[r, :] + nt(mixed[r, :], w_out[...])
        hat_two, scale_two = unit(one)
        h = (hat_two * gain[2] + gain[3]).astype(BF16)
        h_two[r, :] = h
        step = 512
        for t in range(w_up.shape[0] // step):
            u = nt(h, w_up[t * step : (t + 1) * step, :])
            a, s = gelu_pair(u)
            act[r, t * step : (t + 1) * step] = a.astype(BF16)
            slope[:, t * step : (t + 1) * step] = s.astype(BF16)
        two = one + nt(act[r, :], w_down[...])
        hat, scale = unit(two)
        result = hat * gain[4] + gain[5]
        for b in range(groups):
            for c in range(per_group):
                lo = c * chunk
                hi = min(lo + chunk, real)

                @pl.when(i == b * per_group + c)
                def _(b=b, lo=lo, hi=hi):
                    decoded[b, lo:hi, :] = result[: hi - lo]

        cr = rows_of(j, chunk)
        d = cot[g, cr, :]
        g_norms[4:5, :] += column_sum(d * hat)
        g_norms[5:6, :] += column_sum(d)
        d_two = unit_back(d * gain[4], hat, scale)
        e = d_two.astype(BF16)
        e_two[r, :] = e
        for t in range(w_up.shape[0] // step):
            cols = slice(t * step, (t + 1) * step)
            d_act = nn(e, w_down[:, cols])
            d_up[r, cols] = (d_act * slope[:, cols].astype(F32)).astype(BF16)
        d_h = nn(d_up[r, :], w_up[...])
        g_norms[2:3, :] += column_sum(d_h * hat_two)
        g_norms[3:4, :] += column_sum(d_h)
        d_one = d_two + unit_back(d_h * gain[2], hat_two, scale_two)
        d_x[g, cr, :] = d_one
        e_one[r, :] = d_one.astype(BF16)

    outer_loop(rows // chunk, middle)

    weight_sum(g_down, e_two, act, stage_wide, sem)
    weight_sum(g_up, d_up, h_two, stage, sem)
    weight_sum(g_out, e_one, mixed, stage, sem)

    def mix_back(i):
        r = rows_of(i, chunk)
        mixed[r, :] = nn(e_one[r, :], w_out[...]).astype(BF16)

    outer_loop(rows // chunk, mix_back)
    d_qkv = act

    def attend_back(g):
        bias[...] = mask_bias(seg_row[g], seg_col[rows_of(g, n), :])
        r = rows_of(g, n)

        def one(t):
            q, k, v = [qkv[r, lane_tile(t + j * tiles)] for j in range(3)]
            logs = [totals[g * tiles + t, h : h + 1, :] for h in range(per_tile)]
            found = attend_tile_back(q, k, v, mixed[r, lane_tile(t)], bias[...], logs, head_size)
            for j in range(3):
                d_qkv[r, lane_tile(t + j * tiles)] = found[j].astype(BF16)

        outer_loop(tiles, one)

    outer_loop(groups, attend_back)

    weight_sum(g_qkv, d_qkv.at[:, : 3 * width], h_one, stage, sem)

    def finish(i):
        g, j = i // per_group, lax.rem(i, per_group)
        r, cr = rows_of(i, chunk), rows_of(j, chunk)
        d_h = nn(d_qkv[r, : 3 * width], w_qkv[...])
        hat, scale = unit(x[r, :])
        g_norms[0:1, :] += column_sum(d_h * hat)
        g_norms[1:2, :] += column_sum(d_h)
        d_start = d_x[g, cr, :] + unit_back(d_h * gain[0], hat, scale)
        seen = index_col[r, :] >= 0
        g_norms[6:7, :] += column_sum(jnp.where(seen, 0.0, d_start))
        e_two[r, :] = jnp.where(seen, d_start, 0.0).astype(BF16)

    outer_loop(rows // chunk, finish)

    def back(s):
        sr = rows_of(s, 128)
        slots = lax.broadcasted_iota(jnp.int32, (128, rows), 0) + s * 128
        chosen = jnp.where(slots == index_row[...], 1.0, 0.0).astype(BF16)
        d_table[sr, :] = nn(chosen, e_two[...]).astype(BF16)

    outer_loop(table.shape[0] // 128, back)


def decoder(table, index, segment, cotangent, norms, weights, heads):
    groups, real, width = cotangent.shape
    n = -(-real // 32) * 32
    chunk = n // 2
    rows = groups * n
    head_size = width // heads
    pad = n - real
    index = jnp.pad(index, ((0, 0), (0, pad)), constant_values=-1).reshape(rows)
    segment = jnp.pad(segment, ((0, 0), (0, pad)), constant_values=-1)
    cot = jnp.pad(cotangent, ((0, 0), (0, pad), (0, 0)))
    tiles = width // LANES
    ff = weights[2].shape[0]
    vm = pl.BlockSpec(memory_space=pltpu.VMEM)
    return pl.pallas_call(
        functools.partial(decoder_kernel, head_size, chunk),
        out_shape=[
            jax.ShapeDtypeStruct(cotangent.shape, F32),
            jax.ShapeDtypeStruct(table.shape, BF16),
            jax.ShapeDtypeStruct((8, width), F32),
        ]
        + [jax.ShapeDtypeStruct(w.shape, BF16) for w in weights],
        in_specs=[vm] * 11,
        out_specs=[vm] * 3 + [pl.BlockSpec(memory_space=pl.ANY)] * 4,
        scratch_shapes=[
            pltpu.VMEM((rows, width), F32),
            pltpu.VMEM((rows, width), BF16),
            pltpu.VMEM((rows, 3 * width), BF16),
            pltpu.VMEM((rows, width), BF16),
            pltpu.VMEM((groups * tiles, LANES // head_size, n), F32),
            pltpu.VMEM((rows, width), BF16),
            pltpu.VMEM((rows, ff), BF16),
            pltpu.VMEM((chunk, ff), BF16),
            pltpu.VMEM((rows, ff), BF16),
            pltpu.VMEM((rows, width), BF16),
            pltpu.VMEM((rows, width), BF16),
            pltpu.VMEM((n, n), F32),
            pltpu.VMEM((2, 256, width), BF16),
            pltpu.VMEM((2, LANES, ff), BF16),
            pltpu.SemaphoreType.DMA((2,)),
        ],
        compiler_params=pltpu.CompilerParams(vmem_limit_bytes=60 << 20),
        name="decoder",
    )(
        table,
        index[:, None],
        index[None, :],
        segment.reshape(rows, 1),
        segment[:, None, :],
        cot,
        norms,
        *weights,
    )


def encoder_kernel(
    head_size,
    groups,
    chunk,
    patches,
    key_col,
    own_row,
    norms,
    shift,
    w_qkv,
    w_out,
    w_up,
    w_down,
    w_embed,
    embedded,
    qkv,
    totals,
    mixed,
    x_one,
    act,
    slope,
    sent,
):
    rows, width = patches.shape
    n = rows // groups
    tiles = width // LANES
    per_tile = LANES // head_size
    gain = [norms[k : k + 1, :].astype(F32) for k in range(4)]
    add = shift[7:8, :].astype(F32)

    def start(i):
        r = rows_of(i, chunk)
        hat, _ = unit(patches[r, :].astype(F32))
        qkv[r, :] = nt((hat * gain[0] + gain[1]).astype(BF16), w_qkv[...]).astype(BF16)

    outer_loop(rows // chunk, start)

    def attend(g):
        r = rows_of(g, n)
        bias = mask_bias(own_row[g], key_col[r, :])
        for t in range(tiles):
            q, k, v = [qkv[r, (t + j * tiles) * LANES : (t + j * tiles + 1) * LANES] for j in range(3)]
            out, logs = attend_tile(q, k, v, bias, head_size)
            mixed[r, t * LANES : (t + 1) * LANES] = out.astype(BF16)
            for h in range(per_tile):
                totals[g, t * per_tile + h : t * per_tile + h + 1, :] = logs[h]

    outer_loop(groups, attend)

    def middle(i):
        r = rows_of(i, chunk)
        one = patches[r, :].astype(F32) + nt(mixed[r, :], w_out[...])
        x_one[r, :] = one
        hat, _ = unit(one)
        h = (hat * gain[2] + gain[3]).astype(BF16)
        step = 512
        for t in range(w_up.shape[0] // step):
            u = nt(h, w_up[t * step : (t + 1) * step, :])
            a, s = gelu_pair(u)
            act[r, t * step : (t + 1) * step] = a.astype(BF16)
            slope[r, t * step : (t + 1) * step] = s.astype(BF16)
        two = (one + nt(act[r, :], w_down[...])).astype(BF16)
        sent[r, :] = two
        embedded[r, :] = (nt(two, w_embed[...]) + add).astype(BF16)

    outer_loop(rows // chunk, middle)


def encoder_back_kernel(
    head_size,
    groups,
    chunk,
    patches,
    key_col,
    own_row,
    norms,
    w_qkv,
    w_out,
    w_up,
    w_down,
    w_embed,
    d_table,
    qkv,
    totals,
    mixed,
    x_one,
    act,
    slope,
    sent,
    d_patches,
    g_norms,
    g_shift,
    g_qkv,
    g_out,
    g_up,
    g_down,
    g_embed,
    e_two,
    e_one,
    stage,
    stage_wide,
    sem,
):
    rows, width = patches.shape
    n = rows // groups
    tiles = width // LANES
    per_tile = LANES // head_size
    gain = [norms[k : k + 1, :].astype(F32) for k in range(4)]
    g_norms[...] = jnp.zeros_like(g_norms)
    g_shift[...] = jnp.zeros_like(g_shift)
    step = 512
    weight_sum(g_embed, d_table, sent, stage, sem)
    h_two = sent

    def middle(i):
        r = rows_of(i, chunk)
        d_emb = d_table[r, :]
        g_shift[0:1, :] += column_sum(d_emb.astype(F32))
        e = nn(d_emb, w_embed[...]).astype(BF16)
        e_two[r, :] = e
        for t in range(w_up.shape[0] // step):
            cols = slice(t * step, (t + 1) * step)
            d_act = nn(e, w_down[:, cols])
            slope[r, cols] = (d_act * slope[r, cols].astype(F32)).astype(BF16)
        d_h = nn(slope[r, :], w_up[...])
        hat, scale = unit(x_one[r, :])
        h_two[r, :] = (hat * gain[2] + gain[3]).astype(BF16)
        g_norms[2:3, :] += column_sum(d_h * hat)
        g_norms[3:4, :] += column_sum(d_h)
        d_one = e.astype(F32) + unit_back(d_h * gain[2], hat, scale)
        d_patches[r, :] = d_one
        e_one[r, :] = d_one.astype(BF16)

    outer_loop(rows // chunk, middle)
    weight_sum(g_down, e_two, act, stage_wide, sem)
    weight_sum(g_up, slope, h_two, stage, sem)
    weight_sum(g_out, e_one, mixed, stage, sem)

    def mix_back(i):
        r = rows_of(i, chunk)
        mixed[r, :] = nn(e_one[r, :], w_out[...]).astype(BF16)

    outer_loop(rows // chunk, mix_back)

    def attend_back(g):
        r = rows_of(g, n)
        bias = mask_bias(own_row[g], key_col[r, :])
        for t in range(tiles):
            cols = [slice((t + j * tiles) * LANES, (t + j * tiles + 1) * LANES) for j in range(3)]
            q, k, v = [qkv[r, col] for col in cols]
            logs = [totals[g, t * per_tile + h : t * per_tile + h + 1, :] for h in range(per_tile)]
            found = attend_tile_back(q, k, v, mixed[r, cols[0]], bias, logs, head_size)
            for j in range(3):
                act[r, cols[j]] = found[j].astype(BF16)

    outer_loop(groups, attend_back)
    h_one = h_two

    def finish(i):
        r = rows_of(i, chunk)
        d_h = nn(act[r, : 3 * width], w_qkv[...])
        hat, scale = unit(patches[r, :].astype(F32))
        h_one[r, :] = (hat * gain[0] + gain[1]).astype(BF16)
        g_norms[0:1, :] += column_sum(d_h * hat)
        g_norms[1:2, :] += column_sum(d_h)
        d_patches[r, :] += unit_back(d_h * gain[0], hat, scale)

    outer_loop(rows // chunk, finish)
    weight_sum(g_qkv, act.at[:, : 3 * width], h_one, stage, sem)


def slot_plan(peers, slot_rows):
    padded = -(-slot_rows // 16) * 16
    joined = max(1, 128 // padded)
    return padded, joined


def encoder_inputs(patches, counts):
    peers = counts.shape[0]
    width = patches.shape[1]
    slot_rows = patches.shape[0] // peers
    padded, joined = slot_plan(peers, slot_rows)
    rows, groups = peers * padded, peers // joined
    n = rows // groups
    x = jnp.pad(patches.reshape(peers, slot_rows, width), ((0, 0), (0, padded - slot_rows), (0, 0)))
    x = x.reshape(rows, width)
    row = jnp.arange(padded, dtype=jnp.int32)[None, :]
    slot = jnp.arange(peers, dtype=jnp.int32)[:, None]
    live = (row >= slot_rows - counts[:, None]) & (row < slot_rows)
    keys = jnp.where(live, slot, -1).reshape(rows, 1)
    own = jnp.broadcast_to(slot, (peers, padded)).reshape(groups, 1, n)
    return x, keys, own, padded


def encoder(patches, counts, norms, shift, weights, embed, heads):
    x, keys, own, _ = encoder_inputs(patches, counts)
    rows, width = x.shape
    groups, _, n = own.shape
    head_size = width // heads
    ff = weights[2].shape[0]
    vm = pl.BlockSpec(memory_space=pltpu.VMEM)
    shapes = [
        ((rows, weights[0].shape[0]), BF16),
        ((groups, -(-heads // 8) * 8, n), F32),
        ((rows, width), BF16),
        ((rows, width), F32),
        ((rows, ff), BF16),
        ((rows, ff), BF16),
        ((rows, width), BF16),
    ]
    shapes = [jax.ShapeDtypeStruct(s, t) for s, t in shapes]
    embedded, *stored = pl.pallas_call(
        functools.partial(encoder_kernel, head_size, groups, 2 * n),
        out_shape=[jax.ShapeDtypeStruct((rows, embed.shape[0]), BF16)] + shapes,
        in_specs=[vm] * 10,
        out_specs=[vm] * 8,
        compiler_params=pltpu.CompilerParams(vmem_limit_bytes=60 << 20),
        name="encoder",
    )(x, keys, own, norms, shift, *weights, embed)
    return embedded, (x, keys, own), stored


def encoder_back(rows_in, norms, weights, embed, d_table, stored, heads):
    x, keys, own = rows_in
    rows, width = x.shape
    groups, _, n = own.shape
    head_size = width // heads
    vm = pl.BlockSpec(memory_space=pltpu.VMEM)
    return pl.pallas_call(
        functools.partial(encoder_back_kernel, head_size, groups, 2 * n),
        out_shape=[
            jax.ShapeDtypeStruct((rows, width), F32),
            jax.ShapeDtypeStruct((8, width), F32),
            jax.ShapeDtypeStruct((8, embed.shape[0]), F32),
        ]
        + [jax.ShapeDtypeStruct(w.shape, BF16) for w in weights]
        + [jax.ShapeDtypeStruct(embed.shape, BF16)],
        in_specs=[vm] * 17,
        out_specs=[vm] * 3 + [pl.BlockSpec(memory_space=pl.ANY)] * 5,
        scratch_shapes=[pltpu.VMEM((rows, width), BF16)] * 2
        + [
            pltpu.VMEM((2, 256, width), BF16),
            pltpu.VMEM((2, LANES, weights[2].shape[0]), BF16),
            pltpu.SemaphoreType.DMA((2,)),
        ],
        compiler_params=pltpu.CompilerParams(vmem_limit_bytes=62 << 20),
        name="encoder_back",
    )(x, keys, own, norms, *weights, embed, d_table, *stored)


class Ticker:
    def __init__(self, plans, locals_):
        self.plans, self.locals_, self.moving, self.t = plans, locals_, {}, 0

    def tick(self, count=1):
        for _ in range(count):
            for stage in (3, 2, 1, 0):
                i = self.t - stage
                if 0 <= i < len(self.plans):
                    self.advance(i, stage)
            self.t += 1

    def advance(self, i, stage):
        if stage > 0:
            for copy in self.moving[i, stage - 1]:
                copy.wait_recv()
            if stage == 1:
                self.locals_[i].wait()
        self.moving[i, stage] = self.plans[i][stage]()
        for copy in self.moving[i, stage]:
            copy.start()

    def arrived(self, i):
        for copy in self.moving[i, 3]:
            copy.wait_recv()

    def drain(self):
        for copies in self.moving.values():
            for copy in copies:
                copy.wait_send()


def flat(ref):
    value = ref[...]
    return value.reshape(-1, value.shape[-1])


def spread_norms(tiles, start, count, part, out):
    width = 8 * part
    lane = lax.broadcasted_iota(jnp.int32, (LANES, width), 1)
    line = lax.broadcasted_iota(jnp.int32, (LANES, width), 0)
    for f in range(4):
        total = 0.0
        for d in range(8):
            put = jnp.where((lane == line + d * part) & (line < part), 1.0, 0.0).astype(BF16)
            rows = tiles[d // 2, d % 2, start : start + 16, f * LANES : (f + 1) * LANES]
            total = total + nn(rows, put)
        out[f * count : (f + 1) * count, :] = total[:count]


def front_kernel(entries, head_size, groups, chunk, sizes, *refs):
    n_in = len(entries)
    pieces, refs = refs[:n_in], refs[n_in:]
    patches, key_col, own_row, *refs = refs
    whole, refs = refs[:n_in], refs[n_in:]
    norms_e, norms_d, table, totals, *refs = refs
    kept_out, refs = refs[:6], refs[6:]
    kept, refs = refs[:6], refs[6:]
    qkv, mixed, x_one, act, slope, sent = kept
    loaded, refs = refs[:6], refs[6:]
    tiles_v, w_qkv, w_out, w_up, w_embed, w_down = loaded
    embedded, send_sem, recv_sem, local_sem, load_sem, keep_sem, swap_send, swap_recv, swap_local = refs
    rows, width = patches.shape
    n = rows // groups
    tiles = width // LANES
    per_tile = LANES // head_size
    z, x, y, c = place()
    d = z * 2 + x

    plans, locals_ = [], []
    for i, e in enumerate(entries):
        local, stages = gather_stages(e, i, pieces[i], whole[i], (send_sem, recv_sem), local_sem)
        plans.append(stages)
        locals_.append(local())
    for copy in locals_:
        copy.start()
    barrier = pltpu.get_barrier_semaphore()
    peers = [(lax.rem(d + k, 8), y * 2 + c) for k in range(1, 8)]
    peers += [at(z, x, 1 - y, c), at(z, x, y, 1 - c)]
    for peer in peers:
        pl.semaphore_signal(barrier, inc=1, device_id=peer, device_id_type=MESH)
    pl.semaphore_wait(barrier, len(peers))
    ticker = Ticker(plans, locals_)

    def load(i):
        ticker.arrived(i)
        copy = pltpu.make_async_copy(whole[i], loaded[i], load_sem.at[i])
        copy.start()
        return copy

    keeping = []

    def keep(k):
        copy = pltpu.make_async_copy(kept[k], kept_out[k], keep_sem.at[k])
        copy.start()
        keeping.append(copy)

    def some(lo, hi, body):
        def step(i, carry):
            body(i)
            return carry

        lax.fori_loop(lo, hi, step, 0)

    ticker.tick(5)
    copies = [load(0), load(1)]
    for copy in copies:
        copy.wait()
    spread_norms(tiles_v, 0, sizes[0], sizes[1], norms_e)
    spread_norms(tiles_v, NORM_ROWS // 2, sizes[2], sizes[3], norms_d)
    gain = [norms_e[k : k + 1, :] for k in range(4)]
    add = norms_d[7:8, :]

    def start(i):
        r = rows_of(i, chunk)
        hat, _ = unit(patches[r, :].astype(F32))
        qkv[r, :] = nt((hat * gain[0] + gain[1]).astype(BF16), flat(w_qkv)).astype(BF16)

    some(0, 2, start)
    ticker.tick()
    some(2, 4, start)
    keep(0)

    def attend(g):
        r = rows_of(g, n)
        bias = mask_bias(own_row[g], key_col[r, :])
        for t in range(tiles):
            q, k, v = [qkv[r, (t + j * tiles) * LANES : (t + j * tiles + 1) * LANES] for j in range(3)]
            out, logs = attend_tile(q, k, v, bias, head_size)
            mixed[r, t * LANES : (t + 1) * LANES] = out.astype(BF16)
            for h in range(per_tile):
                totals[g, t * per_tile + h : t * per_tile + h + 1, :] = logs[h]

    some(0, groups // 2, attend)
    ticker.tick()
    some(groups // 2, groups, attend)
    keep(1)
    copies = [load(2), load(3)]
    ticker.tick()
    for copy in copies:
        copy.wait()
    step = w_up.shape[-2] * (2 if len(w_up.shape) == 5 else 1)

    def lift(i):
        r = rows_of(i, chunk)
        one = patches[r, :].astype(F32) + nt(mixed[r, :], flat(w_out))
        x_one[r, :] = one
        hat, _ = unit(one)
        h = (hat * gain[2] + gain[3]).astype(BF16)
        for t in range(8):
            u = nt(h, w_up[t // 2, t % 2].reshape(step, width))
            a, s = gelu_pair(u)
            act[r, t * step : (t + 1) * step] = a.astype(BF16)
            slope[r, t * step : (t + 1) * step] = s.astype(BF16)

    some(0, 1, lift)
    copies = [load(4)]
    some(1, 2, lift)
    ticker.tick()
    some(2, 3, lift)
    copies.append(load(5))
    some(3, 4, lift)
    for k in (2, 3, 4):
        keep(k)
    for copy in copies:
        copy.wait()
    per_chunk = chunk // embedded.shape[1]
    for i in range(4):

        def lower(i):
            r = rows_of(i, chunk)
            two = (x_one[r, :] + nt(act[r, :], flat(w_down))).astype(BF16)
            sent[r, :] = two
            out = (nt(two, flat(w_embed)) + add).astype(BF16)
            for k in range(per_chunk):
                embedded[i * per_chunk + k] = out[k * embedded.shape[1] : (k + 1) * embedded.shape[1]]

        some(i, i + 1, lower)
        for k in range(per_chunk):
            s = i * per_chunk + k

            @pl.when(s != d)
            def _(s=s):
                send_slot(embedded, table, s, d, swap_send, swap_recv, y * 2 + c).start()

            @pl.when(s == d)
            def _(s=s):
                pltpu.make_async_copy(embedded.at[s], table.at[s], swap_local.at[0]).start()

        ticker.tick()
    keep(5)
    while ticker.t < n_in + 3:
        ticker.tick()
    for i in range(6, n_in):
        ticker.arrived(i)
    finish_swap(embedded, table, d, swap_send, swap_recv, swap_local, y * 2 + c)
    ticker.drain()
    for copy in keeping:
        copy.wait()


def send_slot(src, dst, s, d, sends, recvs, f):
    return pltpu.make_async_remote_copy(
        src_ref=src.at[s],
        dst_ref=dst.at[d],
        send_sem=sends.at[s],
        recv_sem=recvs.at[d],
        device_id=(s, f),
        device_id_type=MESH,
    )


def finish_swap(src, dst, d, sends, recvs, local, f):
    for s in range(8):

        @pl.when(s != d)
        def _(s=s):
            came = pltpu.make_async_remote_copy(
                src_ref=src.at[s],
                dst_ref=dst.at[s],
                send_sem=sends.at[s],
                recv_sem=recvs.at[s],
                device_id=(s, f),
                device_id_type=MESH,
            )
            came.wait_send()
            came.wait_recv()

    pltpu.make_async_copy(src.at[d], dst.at[d], local.at[0]).wait()


def front(entries, pieces, patches, counts, sizes, heads):
    peers = 8
    width = patches.shape[1]
    x, keys, own, padded = encoder_inputs(patches, counts)
    rows = x.shape[0]
    groups, _, n = own.shape
    head_size = width // heads
    by = {k: e for k, e in enumerate(entries)}
    wide, ff = 3 * width, 8 * entries[3].rows
    embed = 8 * entries[4].rows
    kept = [
        ((rows, wide), BF16),
        ((rows, width), BF16),
        ((rows, width), F32),
        ((rows, ff), BF16),
        ((rows, ff), BF16),
        ((rows, width), BF16),
    ]
    vm, hbm = pl.BlockSpec(memory_space=pltpu.VMEM), pl.BlockSpec(memory_space=pl.ANY)
    n_in = len(entries)
    sem = pltpu.SemaphoreType.DMA
    found = pl.pallas_call(
        functools.partial(front_kernel, entries, head_size, groups, rows // 4, sizes),
        out_shape=[jax.ShapeDtypeStruct(e.whole, BF16) for e in entries]
        + [
            jax.ShapeDtypeStruct((4 * sizes[0], 8 * sizes[1]), F32),
            jax.ShapeDtypeStruct((4 * sizes[2], 8 * sizes[3]), F32),
            jax.ShapeDtypeStruct((peers, padded, embed), BF16),
            jax.ShapeDtypeStruct((groups, -(-heads // 8) * 8, n), F32),
        ]
        + [jax.ShapeDtypeStruct(s, t) for s, t in kept],
        in_specs=[hbm] * n_in + [vm] * 3,
        out_specs=[hbm] * n_in + [vm, vm, hbm, vm] + [hbm] * 6,
        scratch_shapes=[pltpu.VMEM(s, t) for s, t in kept]
        + [pltpu.VMEM(by[k].whole, BF16) for k in range(6)]
        + [
            pltpu.VMEM((peers, padded, embed), BF16),
            sem((n_in, 10)),
            sem((n_in, 10)),
            sem((n_in,)),
            sem((6,)),
            sem((6,)),
            sem((8,)),
            sem((8,)),
            sem((1,)),
        ],
        compiler_params=pltpu.CompilerParams(
            collective_id=0, has_side_effects=True, vmem_limit_bytes=60 << 20
        ),
        name="front",
    )(*pieces, x, keys, own)
    whole, (norms_e, norms_d, table, totals) = found[:n_in], found[n_in : n_in + 4]
    qkv, mixed, x_one, act, slope, sent = found[n_in + 4 :]
    return whole, norms_e, norms_d, table, (x, keys, own), [qkv, totals, mixed, x_one, act, slope, sent]


def per_device(
    staged,
    patches,
    send_counts,
    dec_segment,
    source_index,
    cotangent,
    enc_norms,
    enc_qkv,
    enc_out,
    enc_up,
    enc_down,
    dec_norms,
    dec_embed,
    dec_qkv,
    dec_out,
    dec_up,
    dec_down,
):
    peers = lax.axis_size("dp")
    width = patches.shape[1]
    slot_rows = patches.shape[0] // peers
    counts = send_counts.reshape(peers)
    masters = (enc_qkv, enc_out, enc_up, dec_embed, enc_down, dec_qkv, dec_out, dec_up, dec_down)
    padded = slot_plan(peers, slot_rows)[0]

    def swap(table):
        slots = table.reshape(peers, padded, table.shape[1])
        return lax.all_to_all(slots, "dp", split_axis=0, concat_axis=0, tiled=True).reshape(table.shape)

    if staged:
        entries, pieces = staged_pieces(enc_norms, dec_norms, masters)
        sizes = (*enc_norms.shape, *dec_norms.shape)
        whole, norms_e, norms_d, table, enc_inputs, stored = front(
            entries, pieces, patches, counts, sizes, HEADS_E
        )
        whole = [w.reshape(-1, w.shape[-1]) for w in whole[1:]]
        table = table.reshape(-1, table.shape[-1])
    else:
        norms_e, norms_d, whole = gather_masters(enc_norms, dec_norms, masters)
    enc_weights, embed, dec_weights = [*whole[:3], whole[4]], whole[3], whole[5:]
    if not staged:
        embedded, enc_inputs, stored = encoder(
            patches, counts, norms_e, norms_d, enc_weights, embed, HEADS_E
        )
        table = swap(embedded)
    place_of = source_index // slot_rows * padded + source_index % slot_rows
    index = jnp.where(source_index >= 0, place_of, -1)
    decoded, d_table, g_dec_norms, *dec_grads = decoder(
        table, index, dec_segment, cotangent, norms_d, dec_weights, HEADS_D
    )
    d_patches, g_enc_norms, g_shift, *enc_grads = encoder_back(
        enc_inputs, norms_e, enc_weights, embed, swap(d_table), stored, HEADS_E
    )
    g_dec_norms = jnp.concatenate([g_dec_norms[:7], g_shift[:1]], axis=0)
    s_enc_norms, s_dec_norms, sums = reduce_masters(
        staged, g_enc_norms[:4], g_dec_norms, [*enc_grads, *dec_grads]
    )
    d_patches = d_patches.reshape(peers, padded, width)[:, :slot_rows]
    return (
        decoded,
        d_patches.reshape(-1, width),
        s_enc_norms,
        *sums[:4],
        s_dec_norms,
        *sums[4:],
    )


def solution(mesh):
    placed = (
        P(("dp", "fsdp"), None),
        P(("dp", "fsdp"), None),
        P(("dp", "fsdp"), None),
        P(("dp", "fsdp"), None),
        P(("dp", "fsdp"), None, None),
        P("fsdp", "dp"),
        P("fsdp", "dp"),
        P("fsdp", "dp"),
        P("fsdp", "dp"),
        P("fsdp", "dp"),
        P("fsdp", "dp"),
        P("fsdp", "dp"),
        P("fsdp", "dp"),
        P("fsdp", "dp"),
        P("fsdp", "dp"),
        P("fsdp", "dp"),
    )
    staged = (mesh.shape["dp"], mesh.shape["fsdp"]) == (8, 4)
    return jax.shard_map(
        functools.partial(per_device, staged),
        mesh=mesh,
        in_specs=placed,
        out_specs=(
            P(("dp", "fsdp"), None, None),
            P(("dp", "fsdp"), None),
            P("fsdp", "dp"),
            P("fsdp", "dp"),
            P("fsdp", "dp"),
            P("fsdp", "dp"),
            P("fsdp", "dp"),
            P("fsdp", "dp"),
            P("fsdp", "dp"),
            P("fsdp", "dp"),
            P("fsdp", "dp"),
            P("fsdp", "dp"),
            P("fsdp", "dp"),
        ),
        check_vma=False,
    )
```

```python
import dataclasses
import functools

import jax
import jax.numpy as jnp
from jax import lax
from jax.experimental import pallas as pl
from jax.experimental.pallas import tpu as pltpu
from jax.sharding import PartitionSpec as P

HEADS_E = 12
HEADS_D = 16


EPSILON = 1e-06
NEGATIVE = -1000000000.0
LANES = 128
MESH = pl.DeviceIdType.MESH
BF16 = jnp.bfloat16
F32 = jnp.float32


def in_blocks(value, dim, length):
    dims = value.shape
    pieces = value.reshape(*dims[:dim], length, dims[dim] // length, *dims[dim + 1 :])
    return jnp.moveaxis(pieces, dim, 0)


def sum_at_owner(value, axis, dim):
    length = lax.axis_size(axis)
    pieces = lax.all_to_all(in_blocks(value, dim, length), axis, 0, 0, tiled=True)
    return jnp.sum(pieces.astype(jnp.float32), axis=0)


@dataclasses.dataclass(frozen=True)
class Entry:
    rows: int
    width: int
    by_core: bool

    @property
    def q(self):
        return self.width // 2 if self.by_core else self.width // 4

    @property
    def part(self):
        return self.rows // 2 if self.by_core else self.rows

    @property
    def whole(self):
        if self.by_core:
            return (4, 2, 2, self.part, self.width)
        return (4, 2, self.part, self.width)

    @property
    def cut(self):
        return -(-self.part // 32) * 16


def entry_of(rows, width):
    return Entry(rows, width, (width // 4) % 128 != 0)


def region(e, ref, zs, xs, rows, y, c):
    if e.by_core:
        return ref.at[zs, xs, c, rows, pl.ds(pl.multiple_of(y * e.q, 128), e.q)]
    return ref.at[zs, xs, rows, pl.ds(pl.multiple_of((2 * y + c) * e.q, 128), e.q)]


def region_pair(e, ref, zs, xs, rows, c):
    if e.by_core:
        return [ref.at[zs, xs, c, rows, :]]
    return [region(e, ref, zs, xs, rows, y, c) for y in range(2)]


def place():
    d, s = lax.axis_index("dp"), lax.axis_index("fsdp")
    return d // 2, lax.rem(d, 2), s // 2, lax.rem(s, 2)


def at(z, x, y, c):
    return (z * 2 + x, y * 2 + c)


def send(src, dst, sems, i, k, peer):
    return pltpu.make_async_remote_copy(
        src_ref=src,
        dst_ref=dst,
        send_sem=sems[0].at[i, k],
        recv_sem=sems[1].at[i, k],
        device_id=peer,
        device_id_type=MESH,
    )


ALL = slice(None)


def gather_stages(e, i, piece, out, sems, local_sem):
    z, x, y, c = place()
    top, bottom = slice(0, e.cut), slice(e.cut, e.part)

    def first():
        here = region(e, out, z, x, ALL, y, c)
        return [
            send(piece, here, sems, i, k - 1, at(lax.rem(z + k, 4), x, y, c)) for k in (1, 2, 3)
        ]

    def local():
        return pltpu.make_async_copy(piece, region(e, out, z, x, ALL, y, c), local_sem.at[i])

    def second():
        a = region(e, out, ALL, x, top, y, c)
        b = region(e, out, ALL, x, bottom, y, c)
        return [
            send(a, a, sems, i, 3, at(z, 1 - x, y, c)),
            send(b, b, sems, i, 4, at(z, x, 1 - y, c)),
        ]

    def third():
        a = region(e, out, ALL, ALL, top, y, c)
        found = [send(a, a, sems, i, 5, at(z, x, 1 - y, c))]
        for k, b in enumerate(region_pair(e, out, ALL, x, bottom, c)):
            found.append(send(b, b, sems, i, 6 + k, at(z, 1 - x, y, c)))
        return found

    def fourth():
        return [
            send(b, b, sems, i, 8 + k, at(z, x, y, 1 - c))
            for k, b in enumerate(region_pair(e, out, ALL, ALL, ALL, c))
        ]

    return local, [first, second, third, fourth]


def reduce_stages(e, i, grad, out, buf, sems, local_sem):
    z, x, y, c = place()
    acc, r4, r3a, r3b, r2a, r2b, r1 = buf
    q, cut, part = e.q, e.cut, e.part
    top, bottom = slice(0, cut), slice(cut, part)

    def lanes(y):
        return pl.ds(pl.multiple_of(y * q, 128), q)

    def share(core, ref):
        if len(grad.shape) > 2:
            into = [ref] if e.by_core else [ref.at[:, :, :, pl.ds(k * q, q)] for k in range(2)]
            return list(zip(region_pair(e, grad, ALL, ALL, ALL, core), into))
        found = []
        for b in range(8):
            to = ref.at[b // 2, b % 2]
            if e.by_core:
                found.append((grad.at[pl.ds(pl.multiple_of((2 * b + core) * part, 16), part), :], to))
                continue
            for k in range(2):
                cols = pl.ds(pl.multiple_of((2 * k + core) * q, 128), q)
                found.append((grad.at[pl.ds(b * part, part), cols], to.at[:, pl.ds(k * q, q)]))
        return found

    def local():
        copies = [pltpu.make_async_copy(src, dst, local_sem.at[i]) for src, dst in share(c, acc)]
        return copies, [pltpu.make_async_copy(acc, acc, local_sem.at[i])]

    def first():
        peer = at(z, x, y, 1 - c)
        copies = [send(src, dst, sems, i, 0, peer) for src, dst in share(1 - c, r4)]
        return copies, [send(r4, r4, sems, i, 0, peer)]

    def add_first():
        def step(k, carry):
            a, b = k // 2, lax.rem(k, 2)
            acc[a, b] = (acc[a, b].astype(F32) + r4[a, b].astype(F32)).astype(BF16)
            return carry

        lax.fori_loop(0, 8, step, 0)

    def second():
        found = [
            send(acc.at[:, :, top, lanes(1 - y)], r3a, sems, i, 2, at(z, x, 1 - y, c)),
            send(acc.at[:, 1 - x, bottom, :], r3b, sems, i, 3, at(z, 1 - x, y, c)),
        ]
        return found, found

    def add_second():
        def step(k, carry):
            for b in range(2):
                acc[k, b, top, lanes(y)] = (
                    acc[k, b, top, lanes(y)].astype(F32) + r3a[k, b].astype(F32)
                ).astype(BF16)
            acc[k, x, bottom, :] = (
                acc[k, x, bottom, :].astype(F32) + r3b[k].astype(F32)
            ).astype(BF16)
            return carry

        lax.fori_loop(0, 4, step, 0)

    def third():
        found = [
            send(acc.at[:, 1 - x, top, lanes(y)], r2a, sems, i, 4, at(z, 1 - x, y, c)),
            send(acc.at[:, x, bottom, lanes(1 - y)], r2b, sems, i, 5, at(z, x, 1 - y, c)),
        ]
        return found, found

    def add_third():
        def step(k, carry):
            acc[k, x, top, lanes(y)] = (
                acc[k, x, top, lanes(y)].astype(F32) + r2a[k].astype(F32)
            ).astype(BF16)
            acc[k, x, bottom, lanes(y)] = (
                acc[k, x, bottom, lanes(y)].astype(F32) + r2b[k].astype(F32)
            ).astype(BF16)
            return carry

        lax.fori_loop(0, 4, step, 0)

    def fourth():
        found = []
        for k in (1, 2, 3):
            there = lax.rem(z + k, 4)
            found.append(
                send(acc.at[there, x, :, lanes(y)], r1.at[k - 1], sems, i, 5 + k, at(there, x, y, c))
            )
        return found, found

    def add_fourth():
        total = acc[z, x, :, lanes(y)].astype(F32)
        for k in range(3):
            total = total + r1[k].astype(F32)
        out[...] = total

    return local, [(first, add_first), (second, add_second), (third, add_third), (fourth, add_fourth)]


def reduce_buffers(e):
    return [
        (4, 2, e.part, 2 * e.q),
        (4, 2, e.part, 2 * e.q),
        (4, 2, e.cut, e.q),
        (4, e.part - e.cut, 2 * e.q),
        (4, e.cut, e.q),
        (4, e.part - e.cut, e.q),
        (3, e.part, e.q),
    ]


CORE_SWAP = [(0, 1), (1, 0), (2, 3), (3, 2)]
NORM_ROWS = 32


def halves_to_pieces(blocks):
    c = lax.rem(lax.axis_index("fsdp"), 2)
    both = jnp.concatenate([b.reshape(2, b.shape[0] // 2, b.shape[1]) for b in blocks], axis=1)
    mine = lax.dynamic_index_in_dim(both, c, 0, keepdims=False)
    other = lax.dynamic_index_in_dim(both, 1 - c, 0, keepdims=False)
    came = lax.ppermute(other, "fsdp", CORE_SWAP)
    left, right = jnp.where(c == 0, mine, came), jnp.where(c == 0, came, mine)
    return jnp.concatenate([left, right], axis=1)


def pieces_to_halves(pieces):
    c = lax.rem(lax.axis_index("fsdp"), 2)
    whole = jnp.concatenate(pieces, axis=0)
    q = whole.shape[1] // 2
    left, right = whole[:, :q], whole[:, q:]
    mine, other = jnp.where(c == 0, left, right), jnp.where(c == 0, right, left)
    came = lax.ppermute(other, "fsdp", CORE_SWAP)
    first, second = jnp.where(c == 0, mine, came), jnp.where(c == 0, came, mine)
    sizes = [p.shape[0] for p in pieces]
    ends = [sum(sizes[:k]) for k in range(1, len(sizes))]
    return [
        jnp.concatenate([a, b], axis=0)
        for a, b in zip(jnp.split(first, ends, axis=0), jnp.split(second, ends, axis=0))
    ]


def gather_masters(enc_norms, dec_norms, weights):
    whole = []
    for w in weights:
        tall = lax.all_gather(w.astype(BF16).T, "dp", axis=0, tiled=True)
        whole.append(lax.all_gather(tall, "fsdp", axis=1, tiled=True))
    norms = []
    for rows in (enc_norms, dec_norms):
        wide = lax.all_gather(rows.astype(BF16), "dp", axis=1, tiled=True)
        norms.append(lax.all_gather(wide, "fsdp", axis=0, tiled=True))
    return norms[0], norms[1], whole


def staged_pieces(enc_norms, dec_norms, weights):
    blocks = [w.astype(BF16).T for w in weights]
    entries = [entry_of(b.shape[0], 4 * b.shape[1]) for b in blocks]
    pieces = list(blocks)
    cores = [k for k, e in enumerate(entries) if e.by_core]
    joined = halves_to_pieces([blocks[k] for k in cores])
    start = 0
    for k in cores:
        pieces[k] = lax.slice_in_dim(joined, start, start + entries[k].part, axis=0)
        start += entries[k].part
    small = jnp.zeros((NORM_ROWS, 128), BF16)
    small = small.at[: enc_norms.shape[0], : enc_norms.shape[1]].set(enc_norms.astype(BF16))
    half = NORM_ROWS // 2
    small = small.at[half : half + dec_norms.shape[0], : dec_norms.shape[1]].set(
        dec_norms.astype(BF16)
    )
    entries = [entry_of(NORM_ROWS, 512)] + entries
    return entries, [small] + pieces


def reduce_masters(g_enc_norms, g_dec_norms, grads):
    def owner(value, rows, lanes):
        part = lax.psum_scatter(value.astype(BF16), "fsdp", scatter_dimension=lanes, tiled=True)
        return sum_at_owner(part, "dp", rows)

    return (
        owner(g_enc_norms, 1, 0),
        owner(g_dec_norms, 1, 0),
        [owner(g, 0, 1).T for g in grads],
    )


def own_blocks(sums, like):
    blocks = list(sums)
    cores = [k for k, b in enumerate(blocks) if b.shape[0] != like[k].shape[1]]
    for k, b in zip(cores, pieces_to_halves([blocks[k] for k in cores])):
        blocks[k] = b
    return [b.T for b in blocks]


def nn(a, b):
    return lax.dot_general(a, b, (((1,), (0,)), ((), ())), preferred_element_type=F32)


def nt(a, b):
    return lax.dot_general(a, b, (((1,), (1,)), ((), ())), preferred_element_type=F32)


def tn(a, b):
    return lax.dot_general(a, b, (((0,), (0,)), ((), ())), preferred_element_type=F32)


def unit(values):
    centred = values - jnp.mean(values, axis=-1, keepdims=True)
    scale = lax.rsqrt(jnp.mean(centred * centred, axis=-1, keepdims=True) + EPSILON)
    return centred * scale, scale


def unit_back(d_hat, hat, scale):
    along = jnp.mean(d_hat * hat, axis=-1, keepdims=True)
    return scale * (d_hat - jnp.mean(d_hat, axis=-1, keepdims=True) - hat * along)


def column_sum(values):
    return jnp.sum(values, axis=0, keepdims=True)


def gelu_pair(u):
    phi = 0.5 + 0.5 * lax.erf(u * 0.7071067811865476)
    return u * phi, phi + u * (0.3989422804014327 * jnp.exp(-0.5 * u * u))


def head_lanes(shape, head_size, h):
    return lax.broadcasted_iota(jnp.int32, shape, 1) // head_size == h


def pick(values, head_size, h):
    return jnp.where(head_lanes(values.shape, head_size, h), values, jnp.zeros_like(values))


def attend_tile(q, k, v, bias, head_size):
    v_t = v.astype(F32).T.astype(BF16)
    mixed, totals = [], []
    for h in range(LANES // head_size):
        scores = nt(pick(k, head_size, h), q) * head_size**-0.5 + bias
        top = jnp.max(scores, axis=0, keepdims=True)
        weight = jnp.exp(scores - top)
        total = jnp.sum(weight, axis=0, keepdims=True)
        part = nn(v_t[h * head_size : (h + 1) * head_size], weight.astype(BF16))
        mixed.append(part * (1.0 / total))
        totals.append(top + jnp.log(total))
    return jnp.concatenate(mixed, axis=0).T, totals


def attend_tile_back(q, k, v, d_mixed, bias, totals, head_size):
    k_t = k.astype(F32).T.astype(BF16)
    d_q, d_k, d_v = [], 0.0, 0.0
    for h in range(LANES // head_size):
        scores = nt(pick(k, head_size, h), q) * head_size**-0.5 + bias
        prob = jnp.exp(scores - totals[h])
        d_prob = nt(pick(v, head_size, h), d_mixed)
        centre = jnp.sum(d_prob * prob, axis=0, keepdims=True)
        d_score = (prob * (d_prob - centre)).astype(BF16)
        d_v = d_v + nn(prob.astype(BF16), pick(d_mixed, head_size, h))
        d_k = d_k + nn(d_score, pick(q, head_size, h))
        d_q.append(nn(k_t[h * head_size : (h + 1) * head_size], d_score))
    d_q = jnp.concatenate(d_q, axis=0).T
    return d_q * head_size**-0.5, d_k * head_size**-0.5, d_v


def lane_tile(t):
    return pl.ds(pl.multiple_of(t * LANES, LANES), LANES)


def rows_of(i, n):
    return pl.ds(pl.multiple_of(i * n, 16), n)


def mask_bias(own, keys):
    return jnp.where(keys == own, 0.0, NEGATIVE).astype(F32)


def outer_loop(count, body):
    def step(i, carry):
        body(i)
        return carry

    lax.fori_loop(0, count, step, 0)


def weight_sum(dst, left, right, stage, sem):
    _, tile, width = stage.shape
    count = left.shape[1] // tile

    def off(t):
        slot = lax.rem(t, 2)
        rows = pl.ds(pl.multiple_of(t * tile, LANES), tile)
        return pltpu.make_async_copy(stage.at[slot], dst.at[rows, :], sem.at[slot])

    def one(t):
        @pl.when(t >= 2)
        def _():
            off(t - 2).wait()

        cols = pl.ds(pl.multiple_of(t * tile, LANES), tile)
        stage[lax.rem(t, 2)] = tn(left[:, cols], right[...]).astype(BF16)
        off(t).start()

    outer_loop(count, one)
    for t in range(max(0, count - 2), count):
        off(t).wait()


def decoder_body(
    hooks,
    head_size,
    chunk,
    table,
    index_col,
    index_row,
    seg_col,
    seg_row,
    cot,
    norms,
    w_qkv,
    w_out,
    w_up,
    w_down,
    decoded,
    d_table,
    g_norms,
    g_qkv,
    g_out,
    g_up,
    g_down,
    x,
    h_one,
    qkv,
    mixed,
    totals,
    h_two,
    act,
    slope,
    d_up,
    e_two,
    e_one,
    bias,
    d_x,
    stage,
    stage_wide,
    sem,
):
    groups, n, width = cot.shape
    real = decoded.shape[1]
    rows = groups * n
    per_group = n // chunk
    tiles = width // LANES
    per_tile = LANES // head_size
    gain = [norms[k : k + 1, :].astype(F32) for k in range(8)]
    g_norms[...] = jnp.zeros_like(g_norms)

    def start(i):
        r = rows_of(i, chunk)
        slots = lax.broadcasted_iota(jnp.int32, (chunk, table.shape[0]), 1)
        named = index_col[r, :]
        chosen = jnp.where(slots == named, 1.0, 0.0).astype(BF16)
        picked = nn(chosen, table[...])
        begin = jnp.where(named >= 0, picked, gain[6])
        x[r, :] = begin
        hat, _ = unit(begin)
        h = (hat * gain[0] + gain[1]).astype(BF16)
        h_one[r, :] = h
        qkv[r, :] = nt(h, w_qkv[...]).astype(BF16)

    outer_loop(rows // chunk, start)

    def attend(g):
        bias[...] = mask_bias(seg_row[g], seg_col[rows_of(g, n), :])
        r = rows_of(g, n)

        def one(t):
            q, k, v = [qkv[r, lane_tile(t + j * tiles)] for j in range(3)]
            out, logs = attend_tile(q, k, v, bias[...], head_size)
            mixed[r, lane_tile(t)] = out.astype(BF16)
            for h in range(per_tile):
                totals[g * tiles + t, h : h + 1, :] = logs[h]

        outer_loop(tiles, one)

    outer_loop(groups, attend)

    def middle(i):
        g, j = i // per_group, lax.rem(i, per_group)
        r = rows_of(i, chunk)
        one = x[r, :] + nt(mixed[r, :], w_out[...])
        hat_two, scale_two = unit(one)
        h = (hat_two * gain[2] + gain[3]).astype(BF16)
        h_two[r, :] = h
        step = 512
        for t in range(w_up.shape[0] // step):
            u = nt(h, w_up[t * step : (t + 1) * step, :])
            a, s = gelu_pair(u)
            act[r, t * step : (t + 1) * step] = a.astype(BF16)
            slope[:, t * step : (t + 1) * step] = s.astype(BF16)
        two = one + nt(act[r, :], w_down[...])
        hat, scale = unit(two)
        result = hat * gain[4] + gain[5]
        for b in range(groups):
            for c in range(per_group):
                lo = c * chunk
                hi = min(lo + chunk, real)

                @pl.when(i == b * per_group + c)
                def _(b=b, lo=lo, hi=hi):
                    decoded[b, lo:hi, :] = result[: hi - lo]

        cr = rows_of(j, chunk)
        d = cot[g, cr, :]
        g_norms[4:5, :] += column_sum(d * hat)
        g_norms[5:6, :] += column_sum(d)
        d_two = unit_back(d * gain[4], hat, scale)
        e = d_two.astype(BF16)
        e_two[r, :] = e
        for t in range(w_up.shape[0] // step):
            cols = slice(t * step, (t + 1) * step)
            d_act = nn(e, w_down[:, cols])
            d_up[r, cols] = (d_act * slope[:, cols].astype(F32)).astype(BF16)
        d_h = nn(d_up[r, :], w_up[...])
        g_norms[2:3, :] += column_sum(d_h * hat_two)
        g_norms[3:4, :] += column_sum(d_h)
        d_one = d_two + unit_back(d_h * gain[2], hat_two, scale_two)
        d_x[g, cr, :] = d_one
        e_one[r, :] = d_one.astype(BF16)

    outer_loop(rows // chunk, middle)

    weight_sum(g_down, e_two, act, stage_wide, sem)
    hooks.summed(0)
    weight_sum(g_up, d_up, h_two, stage, sem)
    hooks.summed(1)
    weight_sum(g_out, e_one, mixed, stage, sem)
    hooks.summed(2)

    def mix_back(i):
        r = rows_of(i, chunk)
        mixed[r, :] = nn(e_one[r, :], w_out[...]).astype(BF16)

    outer_loop(rows // chunk, mix_back)
    d_qkv = act

    for g in range(groups):
        bias[...] = mask_bias(seg_row[g], seg_col[rows_of(g, n), :])
        r = rows_of(g, n)

        def one(t, g=g, r=r):
            q, k, v = [qkv[r, lane_tile(t + j * tiles)] for j in range(3)]
            logs = [totals[g * tiles + t, h : h + 1, :] for h in range(per_tile)]
            found = attend_tile_back(q, k, v, mixed[r, lane_tile(t)], bias[...], logs, head_size)
            for j in range(3):
                d_qkv[r, lane_tile(t + j * tiles)] = found[j].astype(BF16)

        for half in range(2):
            some(half * tiles // 2, (half + 1) * tiles // 2, one)
            hooks.pause(2 * g + half)

    def finish(i):
        g, j = i // per_group, lax.rem(i, per_group)
        r, cr = rows_of(i, chunk), rows_of(j, chunk)
        d_h = nn(d_qkv[r, : 3 * width], w_qkv[...])
        hat, scale = unit(x[r, :])
        g_norms[0:1, :] += column_sum(d_h * hat)
        g_norms[1:2, :] += column_sum(d_h)
        d_start = d_x[g, cr, :] + unit_back(d_h * gain[0], hat, scale)
        seen = index_col[r, :] >= 0
        g_norms[6:7, :] += column_sum(jnp.where(seen, 0.0, d_start))
        e_two[r, :] = jnp.where(seen, d_start, 0.0).astype(BF16)

    outer_loop(rows // chunk, finish)

    slots, slot_rows, _ = d_table.shape

    def back(s):
        line = lax.broadcasted_iota(jnp.int32, (slot_rows, rows), 0) + s * slot_rows
        chosen = jnp.where(line == index_row[...], 1.0, 0.0).astype(BF16)
        d_table[s] = nn(chosen, e_two[...]).astype(BF16)

    hooks.slots(back, slots)
    weight_sum(g_qkv, d_qkv.at[:, : 3 * width], h_one, stage, sem)
    hooks.end()


def some(lo, hi, body):
    def step(i, carry):
        body(i)
        return carry

    lax.fori_loop(lo, hi, step, 0)


class NoHooks:
    def summed(self, k):
        pass

    def pause(self, k):
        pass

    def slots(self, body, count):
        outer_loop(count, body)

    def end(self):
        pass


class MiddleHooks:
    def __init__(self, reducer, d_table, returned, swap_send, swap_recv, swap_local):
        self.reducer = reducer
        self.d_table, self.returned = d_table, returned
        self.swap = (swap_send, swap_recv, swap_local)

    def summed(self, k):
        self.reducer.begin(k)
        for i in range(k):
            self.reducer.step(i)

    def pause(self, k):
        for i in range(3):
            self.reducer.step(i)

    def slots(self, body, count):
        z, x, y, c = place()
        d, f = z * 2 + x, y * 2 + c
        send_sem, recv_sem, local_sem = self.swap
        for s in range(count):
            some(s, s + 1, body)

            @pl.when(s != d)
            def _(s=s):
                send_slot(self.d_table, self.returned, s, d, send_sem, recv_sem, f).start()

            @pl.when(s == d)
            def _(s=s):
                pltpu.make_async_copy(
                    self.d_table.at[s], self.returned.at[s], local_sem.at[0]
                ).start()

    def end(self):
        z, x, y, c = place()
        for i in range(3):
            self.reducer.finish(i)
        finish_swap(self.d_table, self.returned, z * 2 + x, *self.swap, y * 2 + c)
        self.reducer.drain()


def decoder_kernel(head_size, chunk, *refs):
    decoder_body(NoHooks(), head_size, chunk, *refs)


def middle_kernel(entries, head_size, chunk, *refs):
    ins, refs = refs[:11], refs[11:]
    decoded, returned, g_norms, *refs = refs
    grads, refs = refs[:4], refs[4:]
    outs, refs = refs[:3], refs[3:]
    scratch, refs = refs[:16], refs[16:]
    d_table, *refs = refs
    bufs, refs = refs[:21], refs[21:]
    send_sem, recv_sem, local_sem, swap_send, swap_recv, swap_local = refs
    z, x, y, c = place()
    meet(z, x, y, c)
    by_entry = [grads[3], grads[2], grads[1]]
    reducer = Reducer(
        [
            reduce_stages(e, i, by_entry[i], outs[i], bufs[7 * i : 7 * i + 7], (send_sem, recv_sem), local_sem)
            for i, e in enumerate(entries)
        ]
    )
    hooks = MiddleHooks(reducer, d_table, returned, swap_send, swap_recv, swap_local)
    decoder_body(hooks, head_size, chunk, *ins, decoded, d_table, g_norms, *grads, *scratch)


def decoder(staged, table, index, segment, cotangent, norms, weights, heads):
    groups, real, width = cotangent.shape
    n = -(-real // 32) * 32
    chunk = n // 2
    rows = groups * n
    head_size = width // heads
    pad = n - real
    index = jnp.pad(index, ((0, 0), (0, pad)), constant_values=-1).reshape(rows)
    segment = jnp.pad(segment, ((0, 0), (0, pad)), constant_values=-1)
    cot = jnp.pad(cotangent, ((0, 0), (0, pad), (0, 0)))
    tiles = width // LANES
    ff = weights[2].shape[0]
    vm = pl.BlockSpec(memory_space=pltpu.VMEM)
    hbm = pl.BlockSpec(memory_space=pl.ANY)
    scratch = [
        pltpu.VMEM((rows, width), F32),
        pltpu.VMEM((rows, width), BF16),
        pltpu.VMEM((rows, 3 * width), BF16),
        pltpu.VMEM((rows, width), BF16),
        pltpu.VMEM((groups * tiles, LANES // head_size, n), F32),
        pltpu.VMEM((rows, width), BF16),
        pltpu.VMEM((rows, ff), BF16),
        pltpu.VMEM((chunk, ff), BF16),
        pltpu.VMEM((rows, ff), BF16),
        pltpu.VMEM((rows, width), BF16),
        pltpu.VMEM((rows, width), BF16),
        pltpu.VMEM((n, n), F32),
        pltpu.VMEM(cot.shape, F32),
        pltpu.VMEM((2, 256, width), BF16),
        pltpu.VMEM((2, LANES, ff), BF16),
        pltpu.SemaphoreType.DMA((2,)),
    ]
    args = (
        table,
        index[:, None],
        index[None, :],
        segment.reshape(rows, 1),
        segment[:, None, :],
        cot,
        norms,
        *weights,
    )
    slots = (8, table.shape[0] // 8, width)
    shapes = [
        jax.ShapeDtypeStruct(cotangent.shape, F32),
        jax.ShapeDtypeStruct(slots, BF16),
        jax.ShapeDtypeStruct((8, width), F32),
    ] + [jax.ShapeDtypeStruct(w.shape, BF16) for w in weights]
    if not staged:
        return pl.pallas_call(
            functools.partial(decoder_kernel, head_size, chunk),
            out_shape=shapes,
            in_specs=[vm] * 11,
            out_specs=[vm] * 3 + [hbm] * 4,
            scratch_shapes=scratch,
            compiler_params=pltpu.CompilerParams(vmem_limit_bytes=60 << 20),
            name="decoder",
        )(*args)
    entries = [entry_of(w.shape[0] // 8, w.shape[1]) for w in (weights[3], weights[2], weights[1])]
    sem = pltpu.SemaphoreType.DMA
    return pl.pallas_call(
        functools.partial(middle_kernel, entries, head_size, chunk),
        out_shape=shapes + [jax.ShapeDtypeStruct((e.part, e.q), F32) for e in entries],
        in_specs=[vm] * 11,
        out_specs=[vm, hbm, vm] + [hbm] * 4 + [vm] * 3,
        scratch_shapes=scratch
        + [pltpu.VMEM(slots, BF16)]
        + [pltpu.VMEM(shape, BF16) for e in entries for shape in reduce_buffers(e)]
        + [sem((3, 9)), sem((3, 9)), sem((3,)), sem((8,)), sem((8,)), sem((1,))],
        compiler_params=pltpu.CompilerParams(
            collective_id=1, has_side_effects=True, vmem_limit_bytes=62 << 20
        ),
        name="middle",
    )(*args)


def encoder_kernel(
    head_size,
    groups,
    chunk,
    patches,
    key_col,
    own_row,
    norms,
    shift,
    w_qkv,
    w_out,
    w_up,
    w_down,
    w_embed,
    embedded,
    qkv,
    totals,
    mixed,
    x_one,
    act,
    slope,
    sent,
):
    rows, width = patches.shape
    n = rows // groups
    tiles = width // LANES
    per_tile = LANES // head_size
    gain = [norms[k : k + 1, :].astype(F32) for k in range(4)]
    add = shift[7:8, :].astype(F32)

    def start(i):
        r = rows_of(i, chunk)
        hat, _ = unit(patches[r, :].astype(F32))
        qkv[r, :] = nt((hat * gain[0] + gain[1]).astype(BF16), w_qkv[...]).astype(BF16)

    outer_loop(rows // chunk, start)

    def attend(g):
        r = rows_of(g, n)
        bias = mask_bias(own_row[g], key_col[r, :])
        for t in range(tiles):
            q, k, v = [qkv[r, (t + j * tiles) * LANES : (t + j * tiles + 1) * LANES] for j in range(3)]
            out, logs = attend_tile(q, k, v, bias, head_size)
            mixed[r, t * LANES : (t + 1) * LANES] = out.astype(BF16)
            for h in range(per_tile):
                totals[g, t * per_tile + h : t * per_tile + h + 1, :] = logs[h]

    outer_loop(groups, attend)

    def middle(i):
        r = rows_of(i, chunk)
        one = patches[r, :].astype(F32) + nt(mixed[r, :], w_out[...])
        x_one[r, :] = one
        hat, _ = unit(one)
        h = (hat * gain[2] + gain[3]).astype(BF16)
        step = 512
        for t in range(w_up.shape[0] // step):
            u = nt(h, w_up[t * step : (t + 1) * step, :])
            a, s = gelu_pair(u)
            act[r, t * step : (t + 1) * step] = a.astype(BF16)
            slope[r, t * step : (t + 1) * step] = s.astype(BF16)
        two = (one + nt(act[r, :], w_down[...])).astype(BF16)
        sent[r, :] = two
        embedded[r, :] = (nt(two, w_embed[...]) + add).astype(BF16)

    outer_loop(rows // chunk, middle)


def encoder_back_kernel(
    head_size,
    groups,
    chunk,
    patches,
    key_col,
    own_row,
    norms,
    w_qkv,
    w_out,
    w_up,
    w_down,
    w_embed,
    d_table,
    qkv,
    totals,
    mixed,
    x_one,
    act,
    slope,
    sent,
    d_patches,
    g_norms,
    g_shift,
    g_qkv,
    g_out,
    g_up,
    g_down,
    g_embed,
    e_two,
    e_one,
    stage,
    stage_wide,
    sem,
):
    rows, width = patches.shape
    n = rows // groups
    tiles = width // LANES
    per_tile = LANES // head_size
    gain = [norms[k : k + 1, :].astype(F32) for k in range(4)]
    g_norms[...] = jnp.zeros_like(g_norms)
    g_shift[...] = jnp.zeros_like(g_shift)
    step = 512
    weight_sum(g_embed, d_table, sent, stage, sem)
    h_two = sent

    def middle(i):
        r = rows_of(i, chunk)
        d_emb = d_table[r, :]
        g_shift[0:1, :] += column_sum(d_emb.astype(F32))
        e = nn(d_emb, w_embed[...]).astype(BF16)
        e_two[r, :] = e
        for t in range(w_up.shape[0] // step):
            cols = slice(t * step, (t + 1) * step)
            d_act = nn(e, w_down[:, cols])
            slope[r, cols] = (d_act * slope[r, cols].astype(F32)).astype(BF16)
        d_h = nn(slope[r, :], w_up[...])
        hat, scale = unit(x_one[r, :])
        h_two[r, :] = (hat * gain[2] + gain[3]).astype(BF16)
        g_norms[2:3, :] += column_sum(d_h * hat)
        g_norms[3:4, :] += column_sum(d_h)
        d_one = e.astype(F32) + unit_back(d_h * gain[2], hat, scale)
        d_patches[r, :] = d_one
        e_one[r, :] = d_one.astype(BF16)

    outer_loop(rows // chunk, middle)
    weight_sum(g_down, e_two, act, stage_wide, sem)
    weight_sum(g_up, slope, h_two, stage, sem)
    weight_sum(g_out, e_one, mixed, stage, sem)

    def mix_back(i):
        r = rows_of(i, chunk)
        mixed[r, :] = nn(e_one[r, :], w_out[...]).astype(BF16)

    outer_loop(rows // chunk, mix_back)

    def attend_back(g):
        r = rows_of(g, n)
        bias = mask_bias(own_row[g], key_col[r, :])
        for t in range(tiles):
            cols = [slice((t + j * tiles) * LANES, (t + j * tiles + 1) * LANES) for j in range(3)]
            q, k, v = [qkv[r, col] for col in cols]
            logs = [totals[g, t * per_tile + h : t * per_tile + h + 1, :] for h in range(per_tile)]
            found = attend_tile_back(q, k, v, mixed[r, cols[0]], bias, logs, head_size)
            for j in range(3):
                act[r, cols[j]] = found[j].astype(BF16)

    outer_loop(groups, attend_back)
    h_one = h_two

    def finish(i):
        r = rows_of(i, chunk)
        d_h = nn(act[r, : 3 * width], w_qkv[...])
        hat, scale = unit(patches[r, :].astype(F32))
        h_one[r, :] = (hat * gain[0] + gain[1]).astype(BF16)
        g_norms[0:1, :] += column_sum(d_h * hat)
        g_norms[1:2, :] += column_sum(d_h)
        d_patches[r, :] += unit_back(d_h * gain[0], hat, scale)

    outer_loop(rows // chunk, finish)
    weight_sum(g_qkv, act.at[:, : 3 * width], h_one, stage, sem)


def slot_plan(peers, slot_rows):
    padded = -(-slot_rows // 16) * 16
    joined = max(1, 128 // padded)
    return padded, joined


def encoder_inputs(patches, counts):
    peers = counts.shape[0]
    width = patches.shape[1]
    slot_rows = patches.shape[0] // peers
    padded, joined = slot_plan(peers, slot_rows)
    rows, groups = peers * padded, peers // joined
    n = rows // groups
    x = jnp.pad(patches.reshape(peers, slot_rows, width), ((0, 0), (0, padded - slot_rows), (0, 0)))
    x = x.reshape(rows, width)
    row = jnp.arange(padded, dtype=jnp.int32)[None, :]
    slot = jnp.arange(peers, dtype=jnp.int32)[:, None]
    live = (row >= slot_rows - counts[:, None]) & (row < slot_rows)
    keys = jnp.where(live, slot, -1).reshape(rows, 1)
    own = jnp.broadcast_to(slot, (peers, padded)).reshape(groups, 1, n)
    return x, keys, own, padded


def encoder(patches, counts, norms, shift, weights, embed, heads):
    x, keys, own, _ = encoder_inputs(patches, counts)
    rows, width = x.shape
    groups, _, n = own.shape
    head_size = width // heads
    ff = weights[2].shape[0]
    vm = pl.BlockSpec(memory_space=pltpu.VMEM)
    shapes = [
        ((rows, weights[0].shape[0]), BF16),
        ((groups, -(-heads // 8) * 8, n), F32),
        ((rows, width), BF16),
        ((rows, width), F32),
        ((rows, ff), BF16),
        ((rows, ff), BF16),
        ((rows, width), BF16),
    ]
    shapes = [jax.ShapeDtypeStruct(s, t) for s, t in shapes]
    embedded, *stored = pl.pallas_call(
        functools.partial(encoder_kernel, head_size, groups, 2 * n),
        out_shape=[jax.ShapeDtypeStruct((rows, embed.shape[0]), BF16)] + shapes,
        in_specs=[vm] * 10,
        out_specs=[vm] * 8,
        compiler_params=pltpu.CompilerParams(vmem_limit_bytes=60 << 20),
        name="encoder",
    )(x, keys, own, norms, shift, *weights, embed)
    return embedded, (x, keys, own), stored


def encoder_back(rows_in, norms, weights, embed, d_table, stored, heads):
    x, keys, own = rows_in
    rows, width = x.shape
    groups, _, n = own.shape
    head_size = width // heads
    vm = pl.BlockSpec(memory_space=pltpu.VMEM)
    return pl.pallas_call(
        functools.partial(encoder_back_kernel, head_size, groups, 2 * n),
        out_shape=[
            jax.ShapeDtypeStruct((rows, width), F32),
            jax.ShapeDtypeStruct((8, width), F32),
            jax.ShapeDtypeStruct((8, embed.shape[0]), F32),
        ]
        + [jax.ShapeDtypeStruct(w.shape, BF16) for w in weights]
        + [jax.ShapeDtypeStruct(embed.shape, BF16)],
        in_specs=[vm] * 17,
        out_specs=[vm] * 3 + [pl.BlockSpec(memory_space=pl.ANY)] * 5,
        scratch_shapes=[pltpu.VMEM((rows, width), BF16)] * 2
        + [
            pltpu.VMEM((2, 256, width), BF16),
            pltpu.VMEM((2, LANES, weights[2].shape[0]), BF16),
            pltpu.SemaphoreType.DMA((2,)),
        ],
        compiler_params=pltpu.CompilerParams(vmem_limit_bytes=62 << 20),
        name="encoder_back",
    )(x, keys, own, norms, *weights, embed, d_table, *stored)


class Ticker:
    def __init__(self, plans, locals_):
        self.plans, self.locals_, self.moving, self.t = plans, locals_, {}, 0

    def tick(self, count=1):
        for _ in range(count):
            for stage in (3, 2, 1, 0):
                i = self.t - stage
                if 0 <= i < len(self.plans):
                    self.advance(i, stage)
            self.t += 1

    def advance(self, i, stage):
        if stage > 0:
            for copy in self.moving[i, stage - 1]:
                copy.wait_recv()
            if stage == 1:
                self.locals_[i].wait()
        self.moving[i, stage] = self.plans[i][stage]()
        for copy in self.moving[i, stage]:
            copy.start()

    def arrived(self, i):
        for copy in self.moving[i, 3]:
            copy.wait_recv()

    def drain(self):
        for copies in self.moving.values():
            for copy in copies:
                copy.wait_send()


def flat(ref):
    value = ref[...]
    return value.reshape(-1, value.shape[-1])


def spread_norms(tiles, start, count, part, out):
    width = 8 * part
    lane = lax.broadcasted_iota(jnp.int32, (LANES, width), 1)
    line = lax.broadcasted_iota(jnp.int32, (LANES, width), 0)
    for f in range(4):
        total = 0.0
        for d in range(8):
            put = jnp.where((lane == line + d * part) & (line < part), 1.0, 0.0).astype(BF16)
            rows = tiles[d // 2, d % 2, start : start + 16, f * LANES : (f + 1) * LANES]
            total = total + nn(rows, put)
        out[f * count : (f + 1) * count, :] = total[:count]


def front_kernel(entries, head_size, groups, chunk, sizes, *refs):
    n_in = len(entries)
    pieces, refs = refs[:n_in], refs[n_in:]
    patches, key_col, own_row, *refs = refs
    whole, refs = refs[:n_in], refs[n_in:]
    norms_e, norms_d, table, totals, *refs = refs
    kept_out, refs = refs[:6], refs[6:]
    kept, refs = refs[:6], refs[6:]
    qkv, mixed, x_one, act, slope, sent = kept
    loaded, refs = refs[:6], refs[6:]
    tiles_v, w_qkv, w_out, w_up, w_embed, w_down = loaded
    embedded, send_sem, recv_sem, local_sem, load_sem, keep_sem, swap_send, swap_recv, swap_local = refs
    rows, width = patches.shape
    n = rows // groups
    tiles = width // LANES
    per_tile = LANES // head_size
    z, x, y, c = place()
    d = z * 2 + x

    plans, locals_ = [], []
    for i, e in enumerate(entries):
        local, stages = gather_stages(e, i, pieces[i], whole[i], (send_sem, recv_sem), local_sem)
        plans.append(stages)
        locals_.append(local())
    for copy in locals_:
        copy.start()
    meet(z, x, y, c)
    ticker = Ticker(plans, locals_)

    def load(i):
        ticker.arrived(i)
        copy = pltpu.make_async_copy(whole[i], loaded[i], load_sem.at[i])
        copy.start()
        return copy

    keeping = []

    def keep(k):
        copy = pltpu.make_async_copy(kept[k], kept_out[k], keep_sem.at[k])
        copy.start()
        keeping.append(copy)

    ticker.tick(5)
    copies = [load(0), load(1)]
    for copy in copies:
        copy.wait()
    spread_norms(tiles_v, 0, sizes[0], sizes[1], norms_e)
    spread_norms(tiles_v, NORM_ROWS // 2, sizes[2], sizes[3], norms_d)
    gain = [norms_e[k : k + 1, :] for k in range(4)]
    add = norms_d[7:8, :]

    def start(i):
        r = rows_of(i, chunk)
        hat, _ = unit(patches[r, :].astype(F32))
        qkv[r, :] = nt((hat * gain[0] + gain[1]).astype(BF16), flat(w_qkv)).astype(BF16)

    some(0, 2, start)
    ticker.tick()
    some(2, 4, start)
    keep(0)

    def attend(g):
        r = rows_of(g, n)
        bias = mask_bias(own_row[g], key_col[r, :])
        for t in range(tiles):
            q, k, v = [qkv[r, (t + j * tiles) * LANES : (t + j * tiles + 1) * LANES] for j in range(3)]
            out, logs = attend_tile(q, k, v, bias, head_size)
            mixed[r, t * LANES : (t + 1) * LANES] = out.astype(BF16)
            for h in range(per_tile):
                totals[g, t * per_tile + h : t * per_tile + h + 1, :] = logs[h]

    some(0, groups // 2, attend)
    ticker.tick()
    some(groups // 2, groups, attend)
    keep(1)
    copies = [load(2), load(3)]
    ticker.tick()
    for copy in copies:
        copy.wait()
    step = w_up.shape[-2] * (2 if len(w_up.shape) == 5 else 1)

    def lift(i):
        r = rows_of(i, chunk)
        one = patches[r, :].astype(F32) + nt(mixed[r, :], flat(w_out))
        x_one[r, :] = one
        hat, _ = unit(one)
        h = (hat * gain[2] + gain[3]).astype(BF16)
        for t in range(8):
            u = nt(h, w_up[t // 2, t % 2].reshape(step, width))
            a, s = gelu_pair(u)
            act[r, t * step : (t + 1) * step] = a.astype(BF16)
            slope[r, t * step : (t + 1) * step] = s.astype(BF16)

    some(0, 1, lift)
    copies = [load(4)]
    some(1, 2, lift)
    ticker.tick()
    some(2, 3, lift)
    copies.append(load(5))
    some(3, 4, lift)
    for k in (2, 3, 4):
        keep(k)
    for copy in copies:
        copy.wait()
    per_chunk = chunk // embedded.shape[1]
    for i in range(4):

        def lower(i):
            r = rows_of(i, chunk)
            two = (x_one[r, :] + nt(act[r, :], flat(w_down))).astype(BF16)
            sent[r, :] = two
            out = (nt(two, flat(w_embed)) + add).astype(BF16)
            for k in range(per_chunk):
                embedded[i * per_chunk + k] = out[k * embedded.shape[1] : (k + 1) * embedded.shape[1]]

        some(i, i + 1, lower)
        for k in range(per_chunk):
            s = i * per_chunk + k

            @pl.when(s != d)
            def _(s=s):
                send_slot(embedded, table, s, d, swap_send, swap_recv, y * 2 + c).start()

            @pl.when(s == d)
            def _(s=s):
                pltpu.make_async_copy(embedded.at[s], table.at[s], swap_local.at[0]).start()

        ticker.tick()
    keep(5)
    while ticker.t < n_in + 3:
        ticker.tick()
    for i in range(6, n_in):
        ticker.arrived(i)
    finish_swap(embedded, table, d, swap_send, swap_recv, swap_local, y * 2 + c)
    ticker.drain()
    for copy in keeping:
        copy.wait()


def send_slot(src, dst, s, d, sends, recvs, f):
    return pltpu.make_async_remote_copy(
        src_ref=src.at[s],
        dst_ref=dst.at[d],
        send_sem=sends.at[s],
        recv_sem=recvs.at[d],
        device_id=(s, f),
        device_id_type=MESH,
    )


def finish_swap(src, dst, d, sends, recvs, local, f):
    for s in range(8):

        @pl.when(s != d)
        def _(s=s):
            came = pltpu.make_async_remote_copy(
                src_ref=src.at[s],
                dst_ref=dst.at[s],
                send_sem=sends.at[s],
                recv_sem=recvs.at[s],
                device_id=(s, f),
                device_id_type=MESH,
            )
            came.wait_send()
            came.wait_recv()

    pltpu.make_async_copy(src.at[d], dst.at[d], local.at[0]).wait()


def front(entries, pieces, patches, counts, sizes, heads):
    peers = 8
    width = patches.shape[1]
    x, keys, own, padded = encoder_inputs(patches, counts)
    rows = x.shape[0]
    groups, _, n = own.shape
    head_size = width // heads
    by = {k: e for k, e in enumerate(entries)}
    wide, ff = 3 * width, 8 * entries[3].rows
    embed = 8 * entries[4].rows
    kept = [
        ((rows, wide), BF16),
        ((rows, width), BF16),
        ((rows, width), F32),
        ((rows, ff), BF16),
        ((rows, ff), BF16),
        ((rows, width), BF16),
    ]
    vm, hbm = pl.BlockSpec(memory_space=pltpu.VMEM), pl.BlockSpec(memory_space=pl.ANY)
    n_in = len(entries)
    sem = pltpu.SemaphoreType.DMA
    found = pl.pallas_call(
        functools.partial(front_kernel, entries, head_size, groups, rows // 4, sizes),
        out_shape=[jax.ShapeDtypeStruct(e.whole, BF16) for e in entries]
        + [
            jax.ShapeDtypeStruct((4 * sizes[0], 8 * sizes[1]), F32),
            jax.ShapeDtypeStruct((4 * sizes[2], 8 * sizes[3]), F32),
            jax.ShapeDtypeStruct((peers, padded, embed), BF16),
            jax.ShapeDtypeStruct((groups, -(-heads // 8) * 8, n), F32),
        ]
        + [jax.ShapeDtypeStruct(s, t) for s, t in kept],
        in_specs=[hbm] * n_in + [vm] * 3,
        out_specs=[hbm] * n_in + [vm, vm, hbm, vm] + [hbm] * 6,
        scratch_shapes=[pltpu.VMEM(s, t) for s, t in kept]
        + [pltpu.VMEM(by[k].whole, BF16) for k in range(6)]
        + [
            pltpu.VMEM((peers, padded, embed), BF16),
            sem((n_in, 10)),
            sem((n_in, 10)),
            sem((n_in,)),
            sem((6,)),
            sem((6,)),
            sem((8,)),
            sem((8,)),
            sem((1,)),
        ],
        compiler_params=pltpu.CompilerParams(
            collective_id=0, has_side_effects=True, vmem_limit_bytes=60 << 20
        ),
        name="front",
    )(*pieces, x, keys, own)
    whole, (norms_e, norms_d, table, totals) = found[:n_in], found[n_in : n_in + 4]
    qkv, mixed, x_one, act, slope, sent = found[n_in + 4 :]
    return whole, norms_e, norms_d, table, (x, keys, own), [qkv, totals, mixed, x_one, act, slope, sent]


class Reducer:
    def __init__(self, plans):
        self.plans, self.stage, self.moving, self.waits = plans, {}, [], {}

    def start(self, i, copies, waits):
        for copy in copies:
            copy.start()
        self.waits[i] = waits
        self.moving += waits

    def begin(self, i):
        local, stages = self.plans[i]
        copies, self.local_waits = local()
        for copy in copies:
            copy.start()
        self.waits[i, 0] = self.local_waits
        self.start(i, *stages[0][0]())
        self.stage[i] = 0

    def step(self, i):
        k = self.stage[i]
        if k == 4:
            return
        _, stages = self.plans[i]
        for copy in self.waits[i]:
            copy.wait_recv()
        if k == 0:
            for copy in self.waits[i, 0]:
                copy.wait()
        stages[k][1]()
        if k < 3:
            self.start(i, *stages[k + 1][0]())
        self.stage[i] = k + 1

    def finish(self, i):
        while self.stage[i] < 4:
            self.step(i)

    def drain(self):
        for copy in self.moving:
            copy.wait_send()


def meet(z, x, y, c):
    d = z * 2 + x
    barrier = pltpu.get_barrier_semaphore()
    peers = [(lax.rem(d + k, 8), y * 2 + c) for k in range(1, 8)]
    peers += [at(z, x, 1 - y, c), at(z, x, y, 1 - c)]
    for peer in peers:
        pl.semaphore_signal(barrier, inc=1, device_id=peer, device_id_type=MESH)
    pl.semaphore_wait(barrier, len(peers))


def gather_norms(g, start, count, part, tiles):
    width = 8 * part
    lane = lax.broadcasted_iota(jnp.int32, (width, LANES), 1)
    line = lax.broadcasted_iota(jnp.int32, (width, LANES), 0)
    rows = g.astype(BF16)
    for d in range(8):
        put = jnp.where((line == lane + d * part) & (lane < part), 1.0, 0.0).astype(BF16)
        cut = nn(rows, put).astype(BF16)
        for f in range(4):
            tiles[d // 2, d % 2, start : start + count, f * LANES : (f + 1) * LANES] = cut[
                f * count : (f + 1) * count
            ]


def rear_kernel(entries, head_size, groups, chunk, sizes, *refs):
    patches, key_col, own_row, norms, g_dec, g_dec_qkv, *refs = refs
    weights, refs = refs[:5], refs[5:]
    d_table, *refs = refs
    stored, refs = refs[:7], refs[7:]
    d_patches, *refs = refs
    g_embed, g_down, g_up, g_out, g_qkv, *refs = refs
    n_in = len(entries)
    outs, refs = refs[:n_in], refs[n_in:]
    up_v, down_v, embed_v, act, slope, mixed, sent, e_two, e_one, d_emb, totals, small, *refs = refs
    stage, stage_wide, sem, g_norms, g_shift, *refs = refs
    bufs, refs = refs[: 7 * n_in], refs[7 * n_in :]
    send_sem, recv_sem, local_sem, load_sem = refs
    w_qkv, w_out, w_up, w_down, w_embed = weights
    s_qkv, s_totals, s_mixed, s_one, s_act, s_slope, s_sent = stored
    rows, width = patches.shape
    n = rows // groups
    tiles = width // LANES
    per_tile = LANES // head_size
    wide = 3 * width
    z, x, y, c = place()
    loads = {}

    def load(k, src, dst):
        loads[k] = pltpu.make_async_copy(src, dst, load_sem.at[k])
        loads[k].start()

    load(0, w_embed, embed_v)
    load(1, d_table, d_emb)
    load(2, s_act, act)
    load(3, s_sent, sent)
    load(4, w_down, down_v)
    load(5, s_slope, slope)
    load(6, w_up, up_v)
    load(7, s_one, d_patches)
    load(8, s_mixed, mixed)
    load(9, s_totals, totals)
    small[...] = jnp.zeros_like(small)
    g_norms[...] = jnp.zeros_like(g_norms)
    g_shift[...] = jnp.zeros_like(g_shift)
    meet(z, x, y, c)
    grads = [g_dec_qkv, g_down, g_embed, g_up, g_out, g_qkv, small]
    reducer = Reducer(
        [
            reduce_stages(e, i, grads[i], outs[i], bufs[7 * i : 7 * i + 7], (send_sem, recv_sem), local_sem)
            for i, e in enumerate(entries)
        ]
    )
    reducer.begin(0)
    gain = [norms[k : k + 1, :] for k in range(4)]

    def enter(i):
        r = rows_of(i, chunk)
        g_shift[0:1, :] += column_sum(d_emb[r, :].astype(F32))
        e_two[r, :] = nn(d_emb[r, :], embed_v[...]).astype(BF16)

    loads[0].wait()
    loads[1].wait()
    outer_loop(rows // chunk, enter)
    loads[2].wait()
    weight_sum(g_down, e_two, act, stage_wide, sem)
    reducer.begin(1)
    reducer.step(0)
    loads[3].wait()
    weight_sum(g_embed, d_emb, sent, stage, sem)
    reducer.begin(2)
    reducer.step(1)
    reducer.step(0)
    h_two = sent
    step = 512

    def middle(i):
        r = rows_of(i, chunk)
        e = e_two[r, :]
        for t in range(slope.shape[1] // step):
            cols = slice(t * step, (t + 1) * step)
            d_act = nn(e, down_v[:, cols])
            slope[r, cols] = (d_act * slope[r, cols].astype(F32)).astype(BF16)
        d_h = nn(slope[r, :], up_v[...])
        hat, scale = unit(d_patches[r, :])
        h_two[r, :] = (hat * gain[2] + gain[3]).astype(BF16)
        g_norms[2:3, :] += column_sum(d_h * hat)
        g_norms[3:4, :] += column_sum(d_h)
        d_one = e.astype(F32) + unit_back(d_h * gain[2], hat, scale)
        d_patches[r, :] = d_one
        e_one[r, :] = d_one.astype(BF16)

    for k in range(4, 8):
        loads[k].wait()
    for i, then in enumerate(((2, 0), (0, 2), (1, 2), (2,))):
        some(i, i + 1, middle)
        for k in then:
            reducer.step(k)
    load(10, w_qkv, up_v.at[:wide, :])
    load(11, w_out, up_v.at[wide:, :])
    weight_sum(g_up, slope, h_two, stage, sem)
    reducer.begin(3)
    reducer.step(1)
    qkv = slope.at[:, :wide]
    load(12, s_qkv, qkv)
    loads[8].wait()
    loads[9].wait()
    weight_sum(g_out, e_one, mixed, stage, sem)
    reducer.begin(4)

    def mix_back(i):
        r = rows_of(i, chunk)
        mixed[r, :] = nn(e_one[r, :], up_v[wide:, :]).astype(BF16)
        hat, _ = unit(patches[r, :].astype(F32))
        e_two[r, :] = (hat * gain[0] + gain[1]).astype(BF16)

    loads[11].wait()
    outer_loop(rows // chunk, mix_back)
    h_one = e_two
    reducer.step(3)
    reducer.step(4)
    loads[12].wait()

    def attend_back(g):
        r = rows_of(g, n)
        bias = mask_bias(own_row[g], key_col[r, :])
        for t in range(tiles):
            cols = [slice((t + j * tiles) * LANES, (t + j * tiles + 1) * LANES) for j in range(3)]
            q, k, v = [slope[r, col] for col in cols]
            logs = [totals[g, t * per_tile + h : t * per_tile + h + 1, :] for h in range(per_tile)]
            found = attend_tile_back(q, k, v, mixed[r, cols[0]], bias, logs, head_size)
            for j in range(3):
                act[r, cols[j]] = found[j].astype(BF16)

    some(0, groups // 2, attend_back)
    reducer.step(1)
    some(groups // 2, groups, attend_back)
    reducer.step(4)
    reducer.step(3)
    weight_sum(g_qkv, act.at[:, :wide], h_one, stage, sem)
    reducer.begin(5)
    reducer.step(4)
    reducer.step(3)
    loads[10].wait()

    def finish(i):
        r = rows_of(i, chunk)
        d_h = nn(act[r, :wide], up_v[:wide, :])
        hat, scale = unit(patches[r, :].astype(F32))
        g_norms[0:1, :] += column_sum(d_h * hat)
        g_norms[1:2, :] += column_sum(d_h)
        d_patches[r, :] += unit_back(d_h * gain[0], hat, scale)

    some(0, 2, finish)
    reducer.step(5)
    some(2, 4, finish)
    gather_norms(g_norms[0:4, :], 0, sizes[0], sizes[1], small)
    line = lax.broadcasted_iota(jnp.int32, g_dec.shape, 0)
    gather_norms(jnp.where(line == 7, g_shift[0:1, :], g_dec[...]), NORM_ROWS // 2, sizes[2], sizes[3], small)
    reducer.begin(6)
    reducer.step(4)
    reducer.step(6)
    reducer.step(5)
    reducer.step(6)
    reducer.step(3)
    reducer.step(6)
    for i in range(n_in):
        reducer.finish(i)
    reducer.drain()


def rear(rows_in, norms, g_dec, g_dec_qkv, weights, embed, d_table, stored, sizes):
    x, keys, own = rows_in
    rows, width = x.shape
    groups, _, n = own.shape
    head_size = width // HEADS_E
    ff = weights[2].shape[0]
    first = (8 * g_dec_qkv.shape[2], g_dec_qkv.shape[3])
    shapes = [first, weights[3].shape, embed.shape, weights[2].shape, weights[1].shape, weights[0].shape]
    entries = [entry_of(s[0] // 8, s[1]) for s in shapes] + [entry_of(NORM_ROWS, 512)]
    vm, hbm = pl.BlockSpec(memory_space=pltpu.VMEM), pl.BlockSpec(memory_space=pl.ANY)
    sem = pltpu.SemaphoreType.DMA
    n_in = len(entries)
    totals = stored[1]
    found = pl.pallas_call(
        functools.partial(rear_kernel, entries, head_size, groups, rows // 4, sizes),
        out_shape=[jax.ShapeDtypeStruct((rows, width), F32)]
        + [jax.ShapeDtypeStruct(s, BF16) for s in (shapes[2], shapes[1], *shapes[3:])]
        + [jax.ShapeDtypeStruct((e.part, e.q), F32) for e in entries],
        in_specs=[vm] * 5 + [hbm] * 14,
        out_specs=[vm] + [hbm] * 5 + [vm] * n_in,
        scratch_shapes=[
            pltpu.VMEM(weights[2].shape, BF16),
            pltpu.VMEM(weights[3].shape, BF16),
            pltpu.VMEM(embed.shape, BF16),
            pltpu.VMEM((rows, ff), BF16),
            pltpu.VMEM((rows, ff), BF16),
            pltpu.VMEM((rows, width), BF16),
            pltpu.VMEM((rows, width), BF16),
            pltpu.VMEM((rows, width), BF16),
            pltpu.VMEM((rows, width), BF16),
            pltpu.VMEM(d_table.shape, BF16),
            pltpu.VMEM(totals.shape, F32),
            pltpu.VMEM(entries[-1].whole, BF16),
            pltpu.VMEM((2, 256, width), BF16),
            pltpu.VMEM((2, LANES, ff), BF16),
            sem((2,)),
            pltpu.VMEM((8, width), F32),
            pltpu.VMEM((8, embed.shape[0]), F32),
        ]
        + [pltpu.VMEM(shape, BF16) for e in entries for shape in reduce_buffers(e)]
        + [sem((n_in, 9)), sem((n_in, 9)), sem((n_in,)), sem((13,))],
        compiler_params=pltpu.CompilerParams(
            collective_id=2, has_side_effects=True, vmem_limit_bytes=63 << 20
        ),
        name="rear",
    )(x, keys, own, norms, g_dec, g_dec_qkv, *weights, embed, d_table, *stored)
    return found[0], found[6:]


def per_device(
    staged,
    patches,
    send_counts,
    dec_segment,
    source_index,
    cotangent,
    enc_norms,
    enc_qkv,
    enc_out,
    enc_up,
    enc_down,
    dec_norms,
    dec_embed,
    dec_qkv,
    dec_out,
    dec_up,
    dec_down,
):
    peers = lax.axis_size("dp")
    width = patches.shape[1]
    slot_rows = patches.shape[0] // peers
    counts = send_counts.reshape(peers)
    masters = (enc_qkv, enc_out, enc_up, dec_embed, enc_down, dec_qkv, dec_out, dec_up, dec_down)
    padded = slot_plan(peers, slot_rows)[0]

    def swap(table):
        slots = table.reshape(peers, padded, table.shape[1])
        return lax.all_to_all(slots, "dp", split_axis=0, concat_axis=0, tiled=True).reshape(table.shape)

    if staged:
        entries, pieces = staged_pieces(enc_norms, dec_norms, masters)
        sizes = (*enc_norms.shape, *dec_norms.shape)
        whole, norms_e, norms_d, table, enc_inputs, stored = front(
            entries, pieces, patches, counts, sizes, HEADS_E
        )
        whole = [w.reshape(-1, w.shape[-1]) for w in whole[1:]]
        table = table.reshape(-1, table.shape[-1])
    else:
        norms_e, norms_d, whole = gather_masters(enc_norms, dec_norms, masters)
    enc_weights, embed, dec_weights = [*whole[:3], whole[4]], whole[3], whole[5:]
    if not staged:
        embedded, enc_inputs, stored = encoder(
            patches, counts, norms_e, norms_d, enc_weights, embed, HEADS_E
        )
        table = swap(embedded)
    place_of = source_index // slot_rows * padded + source_index % slot_rows
    index = jnp.where(source_index >= 0, place_of, -1)
    if staged:
        decoded, d_table, g_dec_norms, g_qkv, _, _, _, s_down, s_up, s_out = decoder(
            True, table, index, dec_segment, cotangent, norms_d, dec_weights, HEADS_D
        )
        e = entry_of(g_qkv.shape[0] // 8, g_qkv.shape[1])
        d_patches, sums = rear(
            enc_inputs,
            norms_e,
            g_dec_norms,
            g_qkv.reshape(e.whole),
            enc_weights,
            embed,
            d_table.reshape(table.shape),
            stored,
            sizes,
        )
        s_qkv, e_down, s_embed, e_up, e_out, e_qkv, small = sums
        half = NORM_ROWS // 2
        s_enc_norms = small[: sizes[0], : sizes[1]]
        s_dec_norms = small[half : half + sizes[2], : sizes[3]]
        sums = own_blocks(
            [e_qkv, e_out, e_up, e_down, s_embed, s_qkv, s_out, s_up, s_down],
            [enc_qkv, enc_out, enc_up, enc_down, dec_embed, dec_qkv, dec_out, dec_up, dec_down],
        )
    else:
        decoded, d_table, g_dec_norms, *dec_grads = decoder(
            False, table, index, dec_segment, cotangent, norms_d, dec_weights, HEADS_D
        )
        d_patches, g_enc_norms, g_shift, *enc_grads = encoder_back(
            enc_inputs,
            norms_e,
            enc_weights,
            embed,
            swap(d_table.reshape(table.shape)),
            stored,
            HEADS_E,
        )
        g_dec_norms = jnp.concatenate([g_dec_norms[:7], g_shift[:1]], axis=0)
        s_enc_norms, s_dec_norms, sums = reduce_masters(
            g_enc_norms[:4], g_dec_norms, [*enc_grads, *dec_grads]
        )
    d_patches = d_patches.reshape(peers, padded, width)[:, :slot_rows]
    return (
        decoded,
        d_patches.reshape(-1, width),
        s_enc_norms,
        *sums[:4],
        s_dec_norms,
        *sums[4:],
    )


def solution(mesh):
    placed = (
        P(("dp", "fsdp"), None),
        P(("dp", "fsdp"), None),
        P(("dp", "fsdp"), None),
        P(("dp", "fsdp"), None),
        P(("dp", "fsdp"), None, None),
        P("fsdp", "dp"),
        P("fsdp", "dp"),
        P("fsdp", "dp"),
        P("fsdp", "dp"),
        P("fsdp", "dp"),
        P("fsdp", "dp"),
        P("fsdp", "dp"),
        P("fsdp", "dp"),
        P("fsdp", "dp"),
        P("fsdp", "dp"),
        P("fsdp", "dp"),
    )
    staged = (mesh.shape["dp"], mesh.shape["fsdp"]) == (8, 4)
    return jax.shard_map(
        functools.partial(per_device, staged),
        mesh=mesh,
        in_specs=placed,
        out_specs=(
            P(("dp", "fsdp"), None, None),
            P(("dp", "fsdp"), None),
            P("fsdp", "dp"),
            P("fsdp", "dp"),
            P("fsdp", "dp"),
            P("fsdp", "dp"),
            P("fsdp", "dp"),
            P("fsdp", "dp"),
            P("fsdp", "dp"),
            P("fsdp", "dp"),
            P("fsdp", "dp"),
            P("fsdp", "dp"),
            P("fsdp", "dp"),
        ),
        check_vma=False,
    )
```

```python
import dataclasses
import functools

import jax
import jax.numpy as jnp
from jax import lax
from jax.experimental import pallas as pl
from jax.experimental.pallas import tpu as pltpu
from jax.sharding import PartitionSpec as P

HEADS_E = 12
HEADS_D = 16


EPSILON = 1e-06
NEGATIVE = -1000000000.0
LANES = 128
MESH = pl.DeviceIdType.MESH
BF16 = jnp.bfloat16
F32 = jnp.float32


def in_blocks(value, dim, length):
    dims = value.shape
    pieces = value.reshape(*dims[:dim], length, dims[dim] // length, *dims[dim + 1 :])
    return jnp.moveaxis(pieces, dim, 0)


def sum_at_owner(value, axis, dim):
    length = lax.axis_size(axis)
    pieces = lax.all_to_all(in_blocks(value, dim, length), axis, 0, 0, tiled=True)
    return jnp.sum(pieces.astype(jnp.float32), axis=0)


@dataclasses.dataclass(frozen=True)
class Entry:
    rows: int
    width: int
    by_core: bool
    share: int = 1

    @property
    def q(self):
        return self.width // 2 if self.by_core else self.width // 4

    @property
    def block(self):
        return self.rows // 2 if self.by_core else self.rows

    @property
    def part(self):
        return self.block // self.share

    @property
    def whole(self):
        if self.by_core:
            return (4, 2, 2, self.part, self.width)
        return (4, 2, self.part, self.width)

    @property
    def cut(self):
        return -(-self.part // 32) * 16


def entry_of(rows, width):
    return Entry(rows, width, (width // 4) % 128 != 0)


def region(e, ref, zs, xs, rows, y, c):
    if e.by_core:
        return ref.at[zs, xs, c, rows, pl.ds(pl.multiple_of(y * e.q, 128), e.q)]
    return ref.at[zs, xs, rows, pl.ds(pl.multiple_of((2 * y + c) * e.q, 128), e.q)]


def region_pair(e, ref, zs, xs, rows, c):
    if e.by_core:
        return [ref.at[zs, xs, c, rows, :]]
    return [region(e, ref, zs, xs, rows, y, c) for y in range(2)]


def place():
    d, s = lax.axis_index("dp"), lax.axis_index("fsdp")
    return d // 2, lax.rem(d, 2), s // 2, lax.rem(s, 2)


def at(z, x, y, c):
    return (z * 2 + x, y * 2 + c)


def send(src, dst, sems, i, k, peer):
    return pltpu.make_async_remote_copy(
        src_ref=src,
        dst_ref=dst,
        send_sem=sems[0].at[i, k],
        recv_sem=sems[1].at[i, k],
        device_id=peer,
        device_id_type=MESH,
    )


ALL = slice(None)


def gather_stages(e, i, piece, out, sems, local_sem):
    z, x, y, c = place()
    top, bottom = slice(0, e.cut), slice(e.cut, e.part)

    def first():
        here = region(e, out, z, x, ALL, y, c)
        return [
            send(piece, here, sems, i, k - 1, at(lax.rem(z + k, 4), x, y, c)) for k in (1, 2, 3)
        ]

    def local():
        return pltpu.make_async_copy(piece, region(e, out, z, x, ALL, y, c), local_sem.at[i])

    def second():
        a = region(e, out, ALL, x, top, y, c)
        b = region(e, out, ALL, x, bottom, y, c)
        return [
            send(a, a, sems, i, 3, at(z, 1 - x, y, c)),
            send(b, b, sems, i, 4, at(z, x, 1 - y, c)),
        ]

    def third():
        a = region(e, out, ALL, ALL, top, y, c)
        found = [send(a, a, sems, i, 5, at(z, x, 1 - y, c))]
        for k, b in enumerate(region_pair(e, out, ALL, x, bottom, c)):
            found.append(send(b, b, sems, i, 6 + k, at(z, 1 - x, y, c)))
        return found

    def fourth():
        return [
            send(b, b, sems, i, 8 + k, at(z, x, y, 1 - c))
            for k, b in enumerate(region_pair(e, out, ALL, ALL, ALL, c))
        ]

    return local, [first, second, third, fourth]


def reduce_stages(e, i, grad, out, buf, sems, local_sem, row=0):
    z, x, y, c = place()
    acc, r4, r3a, r3b, r2a, r2b, r1 = buf
    q, cut, part = e.q, e.cut, e.part
    top, bottom = slice(0, cut), slice(cut, part)

    def lanes(y):
        return pl.ds(pl.multiple_of(y * q, 128), q)

    def share(core, ref):
        if len(grad.shape) > 2:
            into = [ref] if e.by_core else [ref.at[:, :, :, pl.ds(k * q, q)] for k in range(2)]
            return list(zip(region_pair(e, grad, ALL, ALL, slice(row, row + part), core), into))
        found = []
        for b in range(8):
            to = ref.at[b // 2, b % 2]
            if e.by_core:
                first = pl.multiple_of((2 * b + core) * e.block + row, 16)
                found.append((grad.at[pl.ds(first, part), :], to))
                continue
            for k in range(2):
                cols = pl.ds(pl.multiple_of((2 * k + core) * q, 128), q)
                found.append((grad.at[pl.ds(b * e.block + row, part), cols], to.at[:, pl.ds(k * q, q)]))
        return found

    def local():
        copies = [pltpu.make_async_copy(src, dst, local_sem.at[i]) for src, dst in share(c, acc)]
        return copies, [pltpu.make_async_copy(acc, acc, local_sem.at[i])]

    def first():
        peer = at(z, x, y, 1 - c)
        copies = [send(src, dst, sems, i, 0, peer) for src, dst in share(1 - c, r4)]
        return copies, [send(r4, r4, sems, i, 0, peer)]

    def add_first():
        def step(k, carry):
            a, b = k // 2, lax.rem(k, 2)
            acc[a, b] = (acc[a, b].astype(F32) + r4[a, b].astype(F32)).astype(BF16)
            return carry

        lax.fori_loop(0, 8, step, 0)

    def second():
        found = [
            send(acc.at[:, :, top, lanes(1 - y)], r3a, sems, i, 2, at(z, x, 1 - y, c)),
            send(acc.at[:, 1 - x, bottom, :], r3b, sems, i, 3, at(z, 1 - x, y, c)),
        ]
        return found, found

    def add_second():
        def step(k, carry):
            for b in range(2):
                acc[k, b, top, lanes(y)] = (
                    acc[k, b, top, lanes(y)].astype(F32) + r3a[k, b].astype(F32)
                ).astype(BF16)
            acc[k, x, bottom, :] = (
                acc[k, x, bottom, :].astype(F32) + r3b[k].astype(F32)
            ).astype(BF16)
            return carry

        lax.fori_loop(0, 4, step, 0)

    def third():
        found = [
            send(acc.at[:, 1 - x, top, lanes(y)], r2a, sems, i, 4, at(z, 1 - x, y, c)),
            send(acc.at[:, x, bottom, lanes(1 - y)], r2b, sems, i, 5, at(z, x, 1 - y, c)),
        ]
        return found, found

    def add_third():
        def step(k, carry):
            acc[k, x, top, lanes(y)] = (
                acc[k, x, top, lanes(y)].astype(F32) + r2a[k].astype(F32)
            ).astype(BF16)
            acc[k, x, bottom, lanes(y)] = (
                acc[k, x, bottom, lanes(y)].astype(F32) + r2b[k].astype(F32)
            ).astype(BF16)
            return carry

        lax.fori_loop(0, 4, step, 0)

    def fourth():
        found = []
        for k in (1, 2, 3):
            there = lax.rem(z + k, 4)
            found.append(
                send(acc.at[there, x, :, lanes(y)], r1.at[k - 1], sems, i, 5 + k, at(there, x, y, c))
            )
        return found, found

    def add_fourth():
        total = acc[z, x, :, lanes(y)].astype(F32)
        for k in range(3):
            total = total + r1[k].astype(F32)
        out[row : row + part, :] = total

    return local, [(first, add_first), (second, add_second), (third, add_third), (fourth, add_fourth)]


def reduce_buffers(e):
    return [
        (4, 2, e.part, 2 * e.q),
        (4, 2, e.part, 2 * e.q),
        (4, 2, e.cut, e.q),
        (4, e.part - e.cut, 2 * e.q),
        (4, e.cut, e.q),
        (4, e.part - e.cut, e.q),
        (3, e.part, e.q),
    ]


CORE_SWAP = [(0, 1), (1, 0), (2, 3), (3, 2)]
NORM_ROWS = 32


def halves_to_pieces(blocks):
    c = lax.rem(lax.axis_index("fsdp"), 2)
    both = jnp.concatenate([b.reshape(2, b.shape[0] // 2, b.shape[1]) for b in blocks], axis=1)
    mine = lax.dynamic_index_in_dim(both, c, 0, keepdims=False)
    other = lax.dynamic_index_in_dim(both, 1 - c, 0, keepdims=False)
    came = lax.ppermute(other, "fsdp", CORE_SWAP)
    left, right = jnp.where(c == 0, mine, came), jnp.where(c == 0, came, mine)
    return jnp.concatenate([left, right], axis=1)


def pieces_to_halves(pieces):
    c = lax.rem(lax.axis_index("fsdp"), 2)
    whole = jnp.concatenate(pieces, axis=0)
    q = whole.shape[1] // 2
    left, right = whole[:, :q], whole[:, q:]
    mine, other = jnp.where(c == 0, left, right), jnp.where(c == 0, right, left)
    came = lax.ppermute(other, "fsdp", CORE_SWAP)
    first, second = jnp.where(c == 0, mine, came), jnp.where(c == 0, came, mine)
    sizes = [p.shape[0] for p in pieces]
    ends = [sum(sizes[:k]) for k in range(1, len(sizes))]
    return [
        jnp.concatenate([a, b], axis=0)
        for a, b in zip(jnp.split(first, ends, axis=0), jnp.split(second, ends, axis=0))
    ]


def gather_masters(enc_norms, dec_norms, weights):
    whole = []
    for w in weights:
        tall = lax.all_gather(w.astype(BF16).T, "dp", axis=0, tiled=True)
        whole.append(lax.all_gather(tall, "fsdp", axis=1, tiled=True))
    norms = []
    for rows in (enc_norms, dec_norms):
        wide = lax.all_gather(rows.astype(BF16), "dp", axis=1, tiled=True)
        norms.append(lax.all_gather(wide, "fsdp", axis=0, tiled=True))
    return norms[0], norms[1], whole


def staged_pieces(enc_norms, dec_norms, weights):
    blocks = [w.astype(BF16).T for w in weights]
    entries = [entry_of(b.shape[0], 4 * b.shape[1]) for b in blocks]
    pieces = list(blocks)
    cores = [k for k, e in enumerate(entries) if e.by_core]
    joined = halves_to_pieces([blocks[k] for k in cores])
    start = 0
    for k in cores:
        pieces[k] = lax.slice_in_dim(joined, start, start + entries[k].part, axis=0)
        start += entries[k].part
    small = jnp.zeros((NORM_ROWS, 128), BF16)
    small = small.at[: enc_norms.shape[0], : enc_norms.shape[1]].set(enc_norms.astype(BF16))
    half = NORM_ROWS // 2
    small = small.at[half : half + dec_norms.shape[0], : dec_norms.shape[1]].set(
        dec_norms.astype(BF16)
    )
    entries = [entry_of(NORM_ROWS, 512)] + entries
    return entries, [small] + pieces


def reduce_masters(g_enc_norms, g_dec_norms, grads):
    def owner(value, rows, lanes):
        part = lax.psum_scatter(value.astype(BF16), "fsdp", scatter_dimension=lanes, tiled=True)
        return sum_at_owner(part, "dp", rows)

    return (
        owner(g_enc_norms, 1, 0),
        owner(g_dec_norms, 1, 0),
        [owner(g, 0, 1).T for g in grads],
    )


def own_blocks(sums, like):
    blocks = list(sums)
    cores = [k for k, b in enumerate(blocks) if b.shape[0] != like[k].shape[1]]
    for k, b in zip(cores, pieces_to_halves([blocks[k] for k in cores])):
        blocks[k] = b
    return [b.T for b in blocks]


def nn(a, b):
    return lax.dot_general(a, b, (((1,), (0,)), ((), ())), preferred_element_type=F32)


def nt(a, b):
    return lax.dot_general(a, b, (((1,), (1,)), ((), ())), preferred_element_type=F32)


def tn(a, b):
    return lax.dot_general(a, b, (((0,), (0,)), ((), ())), preferred_element_type=F32)


def unit(values):
    centred = values - jnp.mean(values, axis=-1, keepdims=True)
    scale = lax.rsqrt(jnp.mean(centred * centred, axis=-1, keepdims=True) + EPSILON)
    return centred * scale, scale


def unit_back(d_hat, hat, scale):
    along = jnp.mean(d_hat * hat, axis=-1, keepdims=True)
    return scale * (d_hat - jnp.mean(d_hat, axis=-1, keepdims=True) - hat * along)


def column_sum(values):
    return jnp.sum(values, axis=0, keepdims=True)


def gelu_pair(u):
    phi = 0.5 + 0.5 * lax.erf(u * 0.7071067811865476)
    return u * phi, phi + u * (0.3989422804014327 * jnp.exp(-0.5 * u * u))


def head_lanes(shape, head_size, h):
    return lax.broadcasted_iota(jnp.int32, shape, 1) // head_size == h


def pick(values, head_size, h):
    return jnp.where(head_lanes(values.shape, head_size, h), values, jnp.zeros_like(values))


def attend_tile(q, k, v, bias, head_size):
    v_t = v.astype(F32).T.astype(BF16)
    mixed, totals = [], []
    for h in range(LANES // head_size):
        scores = nt(pick(k, head_size, h), q) * head_size**-0.5 + bias
        top = jnp.max(scores, axis=0, keepdims=True)
        weight = jnp.exp(scores - top)
        total = jnp.sum(weight, axis=0, keepdims=True)
        part = nn(v_t[h * head_size : (h + 1) * head_size], weight.astype(BF16))
        mixed.append(part * (1.0 / total))
        totals.append(top + jnp.log(total))
    return jnp.concatenate(mixed, axis=0).T, totals


def attend_tile_back(q, k, v, d_mixed, bias, totals, head_size):
    k_t = k.astype(F32).T.astype(BF16)
    d_q, d_k, d_v = [], 0.0, 0.0
    for h in range(LANES // head_size):
        scores = nt(pick(k, head_size, h), q) * head_size**-0.5 + bias
        prob = jnp.exp(scores - totals[h])
        d_prob = nt(pick(v, head_size, h), d_mixed)
        centre = jnp.sum(d_prob * prob, axis=0, keepdims=True)
        d_score = (prob * (d_prob - centre)).astype(BF16)
        d_v = d_v + nn(prob.astype(BF16), pick(d_mixed, head_size, h))
        d_k = d_k + nn(d_score, pick(q, head_size, h))
        d_q.append(nn(k_t[h * head_size : (h + 1) * head_size], d_score))
    d_q = jnp.concatenate(d_q, axis=0).T
    return d_q * head_size**-0.5, d_k * head_size**-0.5, d_v


def lane_tile(t):
    return pl.ds(pl.multiple_of(t * LANES, LANES), LANES)


def rows_of(i, n):
    return pl.ds(pl.multiple_of(i * n, 16), n)


def mask_bias(own, keys):
    return jnp.where(keys == own, 0.0, NEGATIVE).astype(F32)


def outer_loop(count, body):
    def step(i, carry):
        body(i)
        return carry

    lax.fori_loop(0, count, step, 0)


def weight_sum(dst, left, right, stage, sem):
    _, tile, width = stage.shape
    count = left.shape[1] // tile

    def off(t):
        slot = lax.rem(t, 2)
        rows = pl.ds(pl.multiple_of(t * tile, LANES), tile)
        return pltpu.make_async_copy(stage.at[slot], dst.at[rows, :], sem.at[slot])

    def one(t):
        @pl.when(t >= 2)
        def _():
            off(t - 2).wait()

        cols = pl.ds(pl.multiple_of(t * tile, LANES), tile)
        stage[lax.rem(t, 2)] = tn(left[:, cols], right[...]).astype(BF16)
        off(t).start()

    outer_loop(count, one)
    for t in range(max(0, count - 2), count):
        off(t).wait()


def decoder_body(
    hooks,
    head_size,
    chunk,
    table,
    index_col,
    index_row,
    seg_col,
    seg_row,
    cot,
    norms,
    w_qkv,
    w_out,
    w_up,
    w_down,
    decoded,
    d_table,
    g_norms,
    g_qkv,
    g_out,
    g_up,
    g_down,
    x,
    h_one,
    qkv,
    mixed,
    totals,
    h_two,
    act,
    slope,
    d_up,
    e_two,
    e_one,
    bias,
    d_x,
    stage,
    stage_wide,
    sem,
):
    groups, n, width = cot.shape
    real = decoded.shape[1]
    rows = groups * n
    per_group = n // chunk
    tiles = width // LANES
    per_tile = LANES // head_size
    gain = [norms[k : k + 1, :].astype(F32) for k in range(8)]
    g_norms[...] = jnp.zeros_like(g_norms)

    def start(i):
        r = rows_of(i, chunk)
        slots = lax.broadcasted_iota(jnp.int32, (chunk, table.shape[0]), 1)
        named = index_col[r, :]
        chosen = jnp.where(slots == named, 1.0, 0.0).astype(BF16)
        picked = nn(chosen, table[...])
        begin = jnp.where(named >= 0, picked, gain[6])
        x[r, :] = begin
        hat, _ = unit(begin)
        h = (hat * gain[0] + gain[1]).astype(BF16)
        h_one[r, :] = h
        qkv[r, :] = nt(h, w_qkv[...]).astype(BF16)

    outer_loop(rows // chunk, start)

    def attend(g):
        bias[...] = mask_bias(seg_row[g], seg_col[rows_of(g, n), :])
        r = rows_of(g, n)

        def one(t):
            q, k, v = [qkv[r, lane_tile(t + j * tiles)] for j in range(3)]
            out, logs = attend_tile(q, k, v, bias[...], head_size)
            mixed[r, lane_tile(t)] = out.astype(BF16)
            for h in range(per_tile):
                totals[g * tiles + t, h : h + 1, :] = logs[h]

        outer_loop(tiles, one)

    outer_loop(groups, attend)

    def middle(i):
        g, j = i // per_group, lax.rem(i, per_group)
        r = rows_of(i, chunk)
        one = x[r, :] + nt(mixed[r, :], w_out[...])
        hat_two, scale_two = unit(one)
        h = (hat_two * gain[2] + gain[3]).astype(BF16)
        h_two[r, :] = h
        step = 512
        for t in range(w_up.shape[0] // step):
            u = nt(h, w_up[t * step : (t + 1) * step, :])
            a, s = gelu_pair(u)
            act[r, t * step : (t + 1) * step] = a.astype(BF16)
            slope[:, t * step : (t + 1) * step] = s.astype(BF16)
        two = one + nt(act[r, :], w_down[...])
        hat, scale = unit(two)
        result = hat * gain[4] + gain[5]
        for b in range(groups):
            for c in range(per_group):
                lo = c * chunk
                hi = min(lo + chunk, real)

                @pl.when(i == b * per_group + c)
                def _(b=b, lo=lo, hi=hi):
                    decoded[b, lo:hi, :] = result[: hi - lo]

        cr = rows_of(j, chunk)
        d = cot[g, cr, :]
        g_norms[4:5, :] += column_sum(d * hat)
        g_norms[5:6, :] += column_sum(d)
        d_two = unit_back(d * gain[4], hat, scale)
        e = d_two.astype(BF16)
        e_two[r, :] = e
        for t in range(w_up.shape[0] // step):
            cols = slice(t * step, (t + 1) * step)
            d_act = nn(e, w_down[:, cols])
            d_up[r, cols] = (d_act * slope[:, cols].astype(F32)).astype(BF16)
        d_h = nn(d_up[r, :], w_up[...])
        g_norms[2:3, :] += column_sum(d_h * hat_two)
        g_norms[3:4, :] += column_sum(d_h)
        d_one = d_two + unit_back(d_h * gain[2], hat_two, scale_two)
        d_x[g, cr, :] = d_one
        e_one[r, :] = d_one.astype(BF16)

    outer_loop(rows // chunk, middle)

    weight_sum(g_down, e_two, act, stage_wide, sem)
    hooks.summed(0)
    weight_sum(g_up, d_up, h_two, stage, sem)
    hooks.summed(1)
    weight_sum(g_out, e_one, mixed, stage, sem)
    hooks.summed(2)

    def mix_back(i):
        r = rows_of(i, chunk)
        mixed[r, :] = nn(e_one[r, :], w_out[...]).astype(BF16)

    outer_loop(rows // chunk, mix_back)
    d_qkv = act

    for g in range(groups):
        bias[...] = mask_bias(seg_row[g], seg_col[rows_of(g, n), :])
        r = rows_of(g, n)

        def one(t, g=g, r=r):
            q, k, v = [qkv[r, lane_tile(t + j * tiles)] for j in range(3)]
            logs = [totals[g * tiles + t, h : h + 1, :] for h in range(per_tile)]
            found = attend_tile_back(q, k, v, mixed[r, lane_tile(t)], bias[...], logs, head_size)
            for j in range(3):
                d_qkv[r, lane_tile(t + j * tiles)] = found[j].astype(BF16)

        for half in range(2):
            some(half * tiles // 2, (half + 1) * tiles // 2, one)
            hooks.pause(2 * g + half)

    def finish(i):
        g, j = i // per_group, lax.rem(i, per_group)
        r, cr = rows_of(i, chunk), rows_of(j, chunk)
        d_h = nn(d_qkv[r, : 3 * width], w_qkv[...])
        hat, scale = unit(x[r, :])
        g_norms[0:1, :] += column_sum(d_h * hat)
        g_norms[1:2, :] += column_sum(d_h)
        d_start = d_x[g, cr, :] + unit_back(d_h * gain[0], hat, scale)
        seen = index_col[r, :] >= 0
        g_norms[6:7, :] += column_sum(jnp.where(seen, 0.0, d_start))
        e_two[r, :] = jnp.where(seen, d_start, 0.0).astype(BF16)

    outer_loop(rows // chunk, finish)

    slots, slot_rows, _ = d_table.shape

    def back(s):
        line = lax.broadcasted_iota(jnp.int32, (slot_rows, rows), 0) + s * slot_rows
        chosen = jnp.where(line == index_row[...], 1.0, 0.0).astype(BF16)
        d_table[s] = nn(chosen, e_two[...]).astype(BF16)

    hooks.slots(back, slots)
    weight_sum(g_qkv, d_qkv.at[:, : 3 * width], h_one, stage, sem)
    hooks.end()


def some(lo, hi, body):
    def step(i, carry):
        body(i)
        return carry

    lax.fori_loop(lo, hi, step, 0)


class NoHooks:
    def summed(self, k):
        pass

    def pause(self, k):
        pass

    def slots(self, body, count):
        outer_loop(count, body)

    def end(self):
        pass


class MiddleHooks:
    def __init__(self, reducer, d_table, returned, swap_send, swap_recv, swap_local):
        self.reducer = reducer
        self.d_table, self.returned = d_table, returned
        self.swap = (swap_send, swap_recv, swap_local)

    def summed(self, k):
        if k == 1:
            self.reducer.step(0)
        self.reducer.begin(k)

    def pause(self, k):
        for i in range(3):
            self.reducer.step(i)

    def slots(self, body, count):
        z, x, y, c = place()
        d, f = z * 2 + x, y * 2 + c
        send_sem, recv_sem, local_sem = self.swap
        for s in range(count):
            some(s, s + 1, body)

            @pl.when(s != d)
            def _(s=s):
                send_slot(self.d_table, self.returned, s, d, send_sem, recv_sem, f).start()

            @pl.when(s == d)
            def _(s=s):
                pltpu.make_async_copy(
                    self.d_table.at[s], self.returned.at[s], local_sem.at[0]
                ).start()

    def end(self):
        z, x, y, c = place()
        for i in range(3):
            self.reducer.finish(i)
        finish_swap(self.d_table, self.returned, z * 2 + x, *self.swap, y * 2 + c)
        self.reducer.drain()


def decoder_kernel(head_size, chunk, *refs):
    decoder_body(NoHooks(), head_size, chunk, *refs)


def middle_kernel(entries, head_size, chunk, *refs):
    ins, refs = refs[:11], refs[11:]
    decoded, returned, g_norms, *refs = refs
    grads, refs = refs[:4], refs[4:]
    outs, refs = refs[:3], refs[3:]
    scratch, refs = refs[:16], refs[16:]
    d_table, *refs = refs
    bufs, refs = refs[:21], refs[21:]
    send_sem, recv_sem, local_sem, swap_send, swap_recv, swap_local = refs
    z, x, y, c = place()
    meet(z, x, y, c)
    by_entry = [grads[3], grads[2], grads[1]]
    reducer = Reducer(
        [
            reduce_stages(e, i, by_entry[i], outs[i], bufs[7 * i : 7 * i + 7], (send_sem, recv_sem), local_sem)
            for i, e in enumerate(entries)
        ]
    )
    hooks = MiddleHooks(reducer, d_table, returned, swap_send, swap_recv, swap_local)
    decoder_body(hooks, head_size, chunk, *ins, decoded, d_table, g_norms, *grads, *scratch)


def decoder(staged, table, index, segment, cotangent, norms, weights, heads):
    groups, real, width = cotangent.shape
    n = -(-real // 32) * 32
    chunk = n // 2
    rows = groups * n
    head_size = width // heads
    pad = n - real
    index = jnp.pad(index, ((0, 0), (0, pad)), constant_values=-1).reshape(rows)
    segment = jnp.pad(segment, ((0, 0), (0, pad)), constant_values=-1)
    cot = jnp.pad(cotangent, ((0, 0), (0, pad), (0, 0)))
    tiles = width // LANES
    ff = weights[2].shape[0]
    vm = pl.BlockSpec(memory_space=pltpu.VMEM)
    hbm = pl.BlockSpec(memory_space=pl.ANY)
    scratch = [
        pltpu.VMEM((rows, width), F32),
        pltpu.VMEM((rows, width), BF16),
        pltpu.VMEM((rows, 3 * width), BF16),
        pltpu.VMEM((rows, width), BF16),
        pltpu.VMEM((groups * tiles, LANES // head_size, n), F32),
        pltpu.VMEM((rows, width), BF16),
        pltpu.VMEM((rows, ff), BF16),
        pltpu.VMEM((chunk, ff), BF16),
        pltpu.VMEM((rows, ff), BF16),
        pltpu.VMEM((rows, width), BF16),
        pltpu.VMEM((rows, width), BF16),
        pltpu.VMEM((n, n), F32),
        pltpu.VMEM(cot.shape, F32),
        pltpu.VMEM((2, 256, width), BF16),
        pltpu.VMEM((2, LANES, ff), BF16),
        pltpu.SemaphoreType.DMA((2,)),
    ]
    args = (
        table,
        index[:, None],
        index[None, :],
        segment.reshape(rows, 1),
        segment[:, None, :],
        cot,
        norms,
        *weights,
    )
    slots = (8, table.shape[0] // 8, width)
    shapes = [
        jax.ShapeDtypeStruct(cotangent.shape, F32),
        jax.ShapeDtypeStruct(slots, BF16),
        jax.ShapeDtypeStruct((8, width), F32),
    ] + [jax.ShapeDtypeStruct(w.shape, BF16) for w in weights]
    if not staged:
        return pl.pallas_call(
            functools.partial(decoder_kernel, head_size, chunk),
            out_shape=shapes,
            in_specs=[vm] * 11,
            out_specs=[vm] * 3 + [hbm] * 4,
            scratch_shapes=scratch,
            compiler_params=pltpu.CompilerParams(vmem_limit_bytes=60 << 20),
            name="decoder",
        )(*args)
    entries = [entry_of(w.shape[0] // 8, w.shape[1]) for w in (weights[3], weights[2], weights[1])]
    sem = pltpu.SemaphoreType.DMA
    return pl.pallas_call(
        functools.partial(middle_kernel, entries, head_size, chunk),
        out_shape=shapes + [jax.ShapeDtypeStruct((e.part, e.q), F32) for e in entries],
        in_specs=[vm] * 11,
        out_specs=[vm, hbm, vm] + [hbm] * 4 + [vm] * 3,
        scratch_shapes=scratch
        + [pltpu.VMEM(slots, BF16)]
        + [pltpu.VMEM(shape, BF16) for e in entries for shape in reduce_buffers(e)]
        + [sem((3, 9)), sem((3, 9)), sem((3,)), sem((8,)), sem((8,)), sem((1,))],
        compiler_params=pltpu.CompilerParams(
            collective_id=1, has_side_effects=True, vmem_limit_bytes=62 << 20
        ),
        name="middle",
    )(*args)


def encoder_kernel(
    head_size,
    groups,
    chunk,
    patches,
    key_col,
    own_row,
    norms,
    shift,
    w_qkv,
    w_out,
    w_up,
    w_down,
    w_embed,
    embedded,
    qkv,
    totals,
    mixed,
    x_one,
    act,
    slope,
    sent,
):
    rows, width = patches.shape
    n = rows // groups
    tiles = width // LANES
    per_tile = LANES // head_size
    gain = [norms[k : k + 1, :].astype(F32) for k in range(4)]
    add = shift[7:8, :].astype(F32)

    def start(i):
        r = rows_of(i, chunk)
        hat, _ = unit(patches[r, :].astype(F32))
        qkv[r, :] = nt((hat * gain[0] + gain[1]).astype(BF16), w_qkv[...]).astype(BF16)

    outer_loop(rows // chunk, start)

    def attend(g):
        r = rows_of(g, n)
        bias = mask_bias(own_row[g], key_col[r, :])
        for t in range(tiles):
            q, k, v = [qkv[r, (t + j * tiles) * LANES : (t + j * tiles + 1) * LANES] for j in range(3)]
            out, logs = attend_tile(q, k, v, bias, head_size)
            mixed[r, t * LANES : (t + 1) * LANES] = out.astype(BF16)
            for h in range(per_tile):
                totals[g, t * per_tile + h : t * per_tile + h + 1, :] = logs[h]

    outer_loop(groups, attend)

    def middle(i):
        r = rows_of(i, chunk)
        one = patches[r, :].astype(F32) + nt(mixed[r, :], w_out[...])
        x_one[r, :] = one
        hat, _ = unit(one)
        h = (hat * gain[2] + gain[3]).astype(BF16)
        step = 512
        for t in range(w_up.shape[0] // step):
            u = nt(h, w_up[t * step : (t + 1) * step, :])
            a, s = gelu_pair(u)
            act[r, t * step : (t + 1) * step] = a.astype(BF16)
            slope[r, t * step : (t + 1) * step] = s.astype(BF16)
        two = (one + nt(act[r, :], w_down[...])).astype(BF16)
        sent[r, :] = two
        embedded[r, :] = (nt(two, w_embed[...]) + add).astype(BF16)

    outer_loop(rows // chunk, middle)


def encoder_back_kernel(
    head_size,
    groups,
    chunk,
    patches,
    key_col,
    own_row,
    norms,
    w_qkv,
    w_out,
    w_up,
    w_down,
    w_embed,
    d_table,
    qkv,
    totals,
    mixed,
    x_one,
    act,
    slope,
    sent,
    d_patches,
    g_norms,
    g_shift,
    g_qkv,
    g_out,
    g_up,
    g_down,
    g_embed,
    e_two,
    e_one,
    stage,
    stage_wide,
    sem,
):
    rows, width = patches.shape
    n = rows // groups
    tiles = width // LANES
    per_tile = LANES // head_size
    gain = [norms[k : k + 1, :].astype(F32) for k in range(4)]
    g_norms[...] = jnp.zeros_like(g_norms)
    g_shift[...] = jnp.zeros_like(g_shift)
    step = 512
    weight_sum(g_embed, d_table, sent, stage, sem)
    h_two = sent

    def middle(i):
        r = rows_of(i, chunk)
        d_emb = d_table[r, :]
        g_shift[0:1, :] += column_sum(d_emb.astype(F32))
        e = nn(d_emb, w_embed[...]).astype(BF16)
        e_two[r, :] = e
        for t in range(w_up.shape[0] // step):
            cols = slice(t * step, (t + 1) * step)
            d_act = nn(e, w_down[:, cols])
            slope[r, cols] = (d_act * slope[r, cols].astype(F32)).astype(BF16)
        d_h = nn(slope[r, :], w_up[...])
        hat, scale = unit(x_one[r, :])
        h_two[r, :] = (hat * gain[2] + gain[3]).astype(BF16)
        g_norms[2:3, :] += column_sum(d_h * hat)
        g_norms[3:4, :] += column_sum(d_h)
        d_one = e.astype(F32) + unit_back(d_h * gain[2], hat, scale)
        d_patches[r, :] = d_one
        e_one[r, :] = d_one.astype(BF16)

    outer_loop(rows // chunk, middle)
    weight_sum(g_down, e_two, act, stage_wide, sem)
    weight_sum(g_up, slope, h_two, stage, sem)
    weight_sum(g_out, e_one, mixed, stage, sem)

    def mix_back(i):
        r = rows_of(i, chunk)
        mixed[r, :] = nn(e_one[r, :], w_out[...]).astype(BF16)

    outer_loop(rows // chunk, mix_back)

    def attend_back(g):
        r = rows_of(g, n)
        bias = mask_bias(own_row[g], key_col[r, :])
        for t in range(tiles):
            cols = [slice((t + j * tiles) * LANES, (t + j * tiles + 1) * LANES) for j in range(3)]
            q, k, v = [qkv[r, col] for col in cols]
            logs = [totals[g, t * per_tile + h : t * per_tile + h + 1, :] for h in range(per_tile)]
            found = attend_tile_back(q, k, v, mixed[r, cols[0]], bias, logs, head_size)
            for j in range(3):
                act[r, cols[j]] = found[j].astype(BF16)

    outer_loop(groups, attend_back)
    h_one = h_two

    def finish(i):
        r = rows_of(i, chunk)
        d_h = nn(act[r, : 3 * width], w_qkv[...])
        hat, scale = unit(patches[r, :].astype(F32))
        h_one[r, :] = (hat * gain[0] + gain[1]).astype(BF16)
        g_norms[0:1, :] += column_sum(d_h * hat)
        g_norms[1:2, :] += column_sum(d_h)
        d_patches[r, :] += unit_back(d_h * gain[0], hat, scale)

    outer_loop(rows // chunk, finish)
    weight_sum(g_qkv, act.at[:, : 3 * width], h_one, stage, sem)


def slot_plan(peers, slot_rows):
    padded = -(-slot_rows // 16) * 16
    joined = max(1, 128 // padded)
    return padded, joined


def encoder_inputs(patches, counts):
    peers = counts.shape[0]
    width = patches.shape[1]
    slot_rows = patches.shape[0] // peers
    padded, joined = slot_plan(peers, slot_rows)
    rows, groups = peers * padded, peers // joined
    n = rows // groups
    x = jnp.pad(patches.reshape(peers, slot_rows, width), ((0, 0), (0, padded - slot_rows), (0, 0)))
    x = x.reshape(rows, width)
    row = jnp.arange(padded, dtype=jnp.int32)[None, :]
    slot = jnp.arange(peers, dtype=jnp.int32)[:, None]
    live = (row >= slot_rows - counts[:, None]) & (row < slot_rows)
    keys = jnp.where(live, slot, -1).reshape(rows, 1)
    own = jnp.broadcast_to(slot, (peers, padded)).reshape(groups, 1, n)
    return x, keys, own, padded


def encoder(patches, counts, norms, shift, weights, embed, heads):
    x, keys, own, _ = encoder_inputs(patches, counts)
    rows, width = x.shape
    groups, _, n = own.shape
    head_size = width // heads
    ff = weights[2].shape[0]
    vm = pl.BlockSpec(memory_space=pltpu.VMEM)
    shapes = [
        ((rows, weights[0].shape[0]), BF16),
        ((groups, -(-heads // 8) * 8, n), F32),
        ((rows, width), BF16),
        ((rows, width), F32),
        ((rows, ff), BF16),
        ((rows, ff), BF16),
        ((rows, width), BF16),
    ]
    shapes = [jax.ShapeDtypeStruct(s, t) for s, t in shapes]
    embedded, *stored = pl.pallas_call(
        functools.partial(encoder_kernel, head_size, groups, 2 * n),
        out_shape=[jax.ShapeDtypeStruct((rows, embed.shape[0]), BF16)] + shapes,
        in_specs=[vm] * 10,
        out_specs=[vm] * 8,
        compiler_params=pltpu.CompilerParams(vmem_limit_bytes=60 << 20),
        name="encoder",
    )(x, keys, own, norms, shift, *weights, embed)
    return embedded, (x, keys, own), stored


def encoder_back(rows_in, norms, weights, embed, d_table, stored, heads):
    x, keys, own = rows_in
    rows, width = x.shape
    groups, _, n = own.shape
    head_size = width // heads
    vm = pl.BlockSpec(memory_space=pltpu.VMEM)
    return pl.pallas_call(
        functools.partial(encoder_back_kernel, head_size, groups, 2 * n),
        out_shape=[
            jax.ShapeDtypeStruct((rows, width), F32),
            jax.ShapeDtypeStruct((8, width), F32),
            jax.ShapeDtypeStruct((8, embed.shape[0]), F32),
        ]
        + [jax.ShapeDtypeStruct(w.shape, BF16) for w in weights]
        + [jax.ShapeDtypeStruct(embed.shape, BF16)],
        in_specs=[vm] * 17,
        out_specs=[vm] * 3 + [pl.BlockSpec(memory_space=pl.ANY)] * 5,
        scratch_shapes=[pltpu.VMEM((rows, width), BF16)] * 2
        + [
            pltpu.VMEM((2, 256, width), BF16),
            pltpu.VMEM((2, LANES, weights[2].shape[0]), BF16),
            pltpu.SemaphoreType.DMA((2,)),
        ],
        compiler_params=pltpu.CompilerParams(vmem_limit_bytes=62 << 20),
        name="encoder_back",
    )(x, keys, own, norms, *weights, embed, d_table, *stored)


class Ticker:
    def __init__(self, plans, locals_):
        self.plans, self.locals_, self.moving, self.t = plans, locals_, {}, 0

    def tick(self, count=1):
        for _ in range(count):
            for stage in (3, 2, 1, 0):
                i = self.t - 2 * stage
                if 0 <= i < len(self.plans):
                    self.advance(i, stage)
            self.t += 1

    def advance(self, i, stage):
        if stage > 0:
            for copy in self.moving[i, stage - 1]:
                copy.wait_recv()
            if stage == 1:
                self.locals_[i].wait()
        self.moving[i, stage] = self.plans[i][stage]()
        for copy in self.moving[i, stage]:
            copy.start()

    def arrived(self, i):
        for copy in self.moving[i, 3]:
            copy.wait_recv()

    def drain(self):
        for copies in self.moving.values():
            for copy in copies:
                copy.wait_send()


def flat(ref):
    value = ref[...]
    return value.reshape(-1, value.shape[-1])


def spread_norms(tiles, start, count, part, out):
    width = 8 * part
    lane = lax.broadcasted_iota(jnp.int32, (LANES, width), 1)
    line = lax.broadcasted_iota(jnp.int32, (LANES, width), 0)
    for f in range(4):
        total = 0.0
        for d in range(8):
            put = jnp.where((lane == line + d * part) & (line < part), 1.0, 0.0).astype(BF16)
            rows = tiles[d // 2, d % 2, start : start + 16, f * LANES : (f + 1) * LANES]
            total = total + nn(rows, put)
        out[f * count : (f + 1) * count, :] = total[:count]


def front_kernel(entries, head_size, groups, chunk, sizes, *refs):
    n_in = len(entries)
    pieces, refs = refs[:n_in], refs[n_in:]
    patches, key_col, own_row, *refs = refs
    whole, refs = refs[:n_in], refs[n_in:]
    norms_e, norms_d, table, totals, *refs = refs
    kept_out, refs = refs[:6], refs[6:]
    kept, refs = refs[:6], refs[6:]
    qkv, mixed, x_one, act, slope, sent = kept
    loaded, refs = refs[:6], refs[6:]
    tiles_v, w_qkv, w_out, w_up, w_embed, w_down = loaded
    embedded, send_sem, recv_sem, local_sem, load_sem, keep_sem, swap_send, swap_recv, swap_local = refs
    rows, width = patches.shape
    n = rows // groups
    tiles = width // LANES
    per_tile = LANES // head_size
    z, x, y, c = place()
    d = z * 2 + x

    plans, locals_ = [], []
    for i, e in enumerate(entries):
        local, stages = gather_stages(e, i, pieces[i], whole[i], (send_sem, recv_sem), local_sem)
        plans.append(stages)
        locals_.append(local())
    for copy in locals_:
        copy.start()
    meet(z, x, y, c)
    ticker = Ticker(plans, locals_)

    def load(i):
        ticker.arrived(i)
        copy = pltpu.make_async_copy(whole[i], loaded[i], load_sem.at[i])
        copy.start()
        return copy

    keeping = []

    def keep(k):
        copy = pltpu.make_async_copy(kept[k], kept_out[k], keep_sem.at[k])
        copy.start()
        keeping.append(copy)

    ticker.tick(8)
    copies = [load(0), load(1)]
    for copy in copies:
        copy.wait()
    spread_norms(tiles_v, 0, sizes[0], sizes[1], norms_e)
    spread_norms(tiles_v, NORM_ROWS // 2, sizes[2], sizes[3], norms_d)
    gain = [norms_e[k : k + 1, :] for k in range(4)]
    add = norms_d[7:8, :]

    def start(i):
        r = rows_of(i, chunk)
        hat, _ = unit(patches[r, :].astype(F32))
        qkv[r, :] = nt((hat * gain[0] + gain[1]).astype(BF16), flat(w_qkv)).astype(BF16)

    some(0, 2, start)
    ticker.tick()
    some(2, 4, start)
    keep(0)

    def attend(g):
        r = rows_of(g, n)
        bias = mask_bias(own_row[g], key_col[r, :])
        for t in range(tiles):
            q, k, v = [qkv[r, (t + j * tiles) * LANES : (t + j * tiles + 1) * LANES] for j in range(3)]
            out, logs = attend_tile(q, k, v, bias, head_size)
            mixed[r, t * LANES : (t + 1) * LANES] = out.astype(BF16)
            for h in range(per_tile):
                totals[g, t * per_tile + h : t * per_tile + h + 1, :] = logs[h]

    some(0, groups, attend)
    keep(1)
    ticker.tick()
    copies = [load(2), load(3)]
    ticker.tick()
    for copy in copies:
        copy.wait()
    step = w_up.shape[-2] * (2 if len(w_up.shape) == 5 else 1)

    def lift(i):
        r = rows_of(i, chunk)
        one = patches[r, :].astype(F32) + nt(mixed[r, :], flat(w_out))
        x_one[r, :] = one
        hat, _ = unit(one)
        h = (hat * gain[2] + gain[3]).astype(BF16)
        for t in range(8):
            u = nt(h, w_up[t // 2, t % 2].reshape(step, width))
            a, s = gelu_pair(u)
            act[r, t * step : (t + 1) * step] = a.astype(BF16)
            slope[r, t * step : (t + 1) * step] = s.astype(BF16)

    some(0, 4, lift)
    copies = [load(4)]
    ticker.tick()
    copies.append(load(5))
    for k in (2, 3, 4):
        keep(k)
    for copy in copies:
        copy.wait()
    per_chunk = chunk // embedded.shape[1]
    for i in range(4):

        def lower(i):
            r = rows_of(i, chunk)
            two = (x_one[r, :] + nt(act[r, :], flat(w_down))).astype(BF16)
            sent[r, :] = two
            out = (nt(two, flat(w_embed)) + add).astype(BF16)
            for k in range(per_chunk):
                embedded[i * per_chunk + k] = out[k * embedded.shape[1] : (k + 1) * embedded.shape[1]]

        some(i, i + 1, lower)
        for k in range(per_chunk):
            s = i * per_chunk + k

            @pl.when(s != d)
            def _(s=s):
                send_slot(embedded, table, s, d, swap_send, swap_recv, y * 2 + c).start()

            @pl.when(s == d)
            def _(s=s):
                pltpu.make_async_copy(embedded.at[s], table.at[s], swap_local.at[0]).start()

        if i == 1:
            ticker.tick()
    keep(5)
    while ticker.t < n_in + 6:
        ticker.tick()
    for i in range(6, n_in):
        ticker.arrived(i)
    finish_swap(embedded, table, d, swap_send, swap_recv, swap_local, y * 2 + c)
    ticker.drain()
    for copy in keeping:
        copy.wait()


def send_slot(src, dst, s, d, sends, recvs, f):
    return pltpu.make_async_remote_copy(
        src_ref=src.at[s],
        dst_ref=dst.at[d],
        send_sem=sends.at[s],
        recv_sem=recvs.at[d],
        device_id=(s, f),
        device_id_type=MESH,
    )


def finish_swap(src, dst, d, sends, recvs, local, f):
    for s in range(8):

        @pl.when(s != d)
        def _(s=s):
            came = pltpu.make_async_remote_copy(
                src_ref=src.at[s],
                dst_ref=dst.at[s],
                send_sem=sends.at[s],
                recv_sem=recvs.at[s],
                device_id=(s, f),
                device_id_type=MESH,
            )
            came.wait_send()
            came.wait_recv()

    pltpu.make_async_copy(src.at[d], dst.at[d], local.at[0]).wait()


def front(entries, pieces, patches, counts, sizes, heads):
    peers = 8
    width = patches.shape[1]
    x, keys, own, padded = encoder_inputs(patches, counts)
    rows = x.shape[0]
    groups, _, n = own.shape
    head_size = width // heads
    by = {k: e for k, e in enumerate(entries)}
    wide, ff = 3 * width, 8 * entries[3].rows
    embed = 8 * entries[4].rows
    kept = [
        ((rows, wide), BF16),
        ((rows, width), BF16),
        ((rows, width), F32),
        ((rows, ff), BF16),
        ((rows, ff), BF16),
        ((rows, width), BF16),
    ]
    vm, hbm = pl.BlockSpec(memory_space=pltpu.VMEM), pl.BlockSpec(memory_space=pl.ANY)
    n_in = len(entries)
    sem = pltpu.SemaphoreType.DMA
    found = pl.pallas_call(
        functools.partial(front_kernel, entries, head_size, groups, rows // 4, sizes),
        out_shape=[jax.ShapeDtypeStruct(e.whole, BF16) for e in entries]
        + [
            jax.ShapeDtypeStruct((4 * sizes[0], 8 * sizes[1]), F32),
            jax.ShapeDtypeStruct((4 * sizes[2], 8 * sizes[3]), F32),
            jax.ShapeDtypeStruct((peers, padded, embed), BF16),
            jax.ShapeDtypeStruct((groups, -(-heads // 8) * 8, n), F32),
        ]
        + [jax.ShapeDtypeStruct(s, t) for s, t in kept],
        in_specs=[hbm] * n_in + [vm] * 3,
        out_specs=[hbm] * n_in + [vm, vm, hbm, vm] + [hbm] * 6,
        scratch_shapes=[pltpu.VMEM(s, t) for s, t in kept]
        + [pltpu.VMEM(by[k].whole, BF16) for k in range(6)]
        + [
            pltpu.VMEM((peers, padded, embed), BF16),
            sem((n_in, 10)),
            sem((n_in, 10)),
            sem((n_in,)),
            sem((6,)),
            sem((6,)),
            sem((8,)),
            sem((8,)),
            sem((1,)),
        ],
        compiler_params=pltpu.CompilerParams(
            collective_id=0, has_side_effects=True, vmem_limit_bytes=60 << 20
        ),
        name="front",
    )(*pieces, x, keys, own)
    whole, (norms_e, norms_d, table, totals) = found[:n_in], found[n_in : n_in + 4]
    qkv, mixed, x_one, act, slope, sent = found[n_in + 4 :]
    return whole, norms_e, norms_d, table, (x, keys, own), [qkv, totals, mixed, x_one, act, slope, sent]


class Reducer:
    def __init__(self, plans):
        self.plans, self.stage, self.moving, self.waits = plans, {}, [], {}

    def start(self, i, copies, waits):
        for copy in copies:
            copy.start()
        self.waits[i] = waits
        self.moving += waits

    def begin(self, i):
        local, stages = self.plans[i]
        copies, self.local_waits = local()
        for copy in copies:
            copy.start()
        self.waits[i, 0] = self.local_waits
        self.start(i, *stages[0][0]())
        self.stage[i] = 0

    def step(self, i):
        k = self.stage[i]
        if k == 4:
            return
        _, stages = self.plans[i]
        for copy in self.waits[i]:
            copy.wait_recv()
        if k == 0:
            for copy in self.waits[i, 0]:
                copy.wait()
        stages[k][1]()
        if k < 3:
            self.start(i, *stages[k + 1][0]())
        self.stage[i] = k + 1

    def finish(self, i):
        while self.stage[i] < 4:
            self.step(i)

    def drain(self):
        for copy in self.moving:
            copy.wait_send()


def meet(z, x, y, c):
    d = z * 2 + x
    barrier = pltpu.get_barrier_semaphore()
    peers = [(lax.rem(d + k, 8), y * 2 + c) for k in range(1, 8)]
    peers += [at(z, x, 1 - y, c), at(z, x, y, 1 - c)]
    for peer in peers:
        pl.semaphore_signal(barrier, inc=1, device_id=peer, device_id_type=MESH)
    pl.semaphore_wait(barrier, len(peers))


def gather_norms(g, start, count, part, tiles):
    width = 8 * part
    lane = lax.broadcasted_iota(jnp.int32, (width, LANES), 1)
    line = lax.broadcasted_iota(jnp.int32, (width, LANES), 0)
    rows = g.astype(BF16)
    for d in range(8):
        put = jnp.where((line == lane + d * part) & (lane < part), 1.0, 0.0).astype(BF16)
        cut = nn(rows, put).astype(BF16)
        for f in range(4):
            tiles[d // 2, d % 2, start : start + count, f * LANES : (f + 1) * LANES] = cut[
                f * count : (f + 1) * count
            ]


def rear_kernel(parts, names, head_size, groups, chunk, sizes, *refs):
    patches, key_col, own_row, norms, g_dec, g_dec_qkv, *refs = refs
    weights, refs = refs[:5], refs[5:]
    d_table, *refs = refs
    stored, refs = refs[:7], refs[7:]
    d_patches, *refs = refs
    g_embed, g_down, g_up, g_out, g_qkv, *refs = refs
    outs, refs = refs[: len(names)], refs[len(names) :]
    up_v, down_v, embed_v, act, slope, mixed, sent, e_two, e_one, d_emb, totals, small, *refs = refs
    stage, stage_wide, sem, g_norms, g_shift, *refs = refs
    bufs, refs = refs[: 7 * len(parts)], refs[7 * len(parts) :]
    send_sem, recv_sem, local_sem, load_sem = refs
    w_qkv, w_out, w_up, w_down, w_embed = weights
    s_qkv, s_totals, s_mixed, s_one, s_act, s_slope, s_sent = stored
    rows, width = patches.shape
    n = rows // groups
    tiles = width // LANES
    per_tile = LANES // head_size
    wide = 3 * width
    z, x, y, c = place()
    loads = {}

    def load(k, src, dst):
        loads[k] = pltpu.make_async_copy(src, dst, load_sem.at[k])
        loads[k].start()

    load(0, w_embed, embed_v)
    load(1, d_table, d_emb)
    load(2, s_act, act)
    load(3, s_sent, sent)
    load(4, w_down, down_v)
    load(5, s_slope, slope)
    load(6, w_up, up_v)
    load(7, s_one, d_patches)
    load(8, s_mixed, mixed)
    load(9, s_totals, totals)
    small[...] = jnp.zeros_like(small)
    g_norms[...] = jnp.zeros_like(g_norms)
    g_shift[...] = jnp.zeros_like(g_shift)
    meet(z, x, y, c)
    sources = {"dq": g_dec_qkv, "do": g_down, "em": g_embed, "up": g_up, "ou": g_out, "qk": g_qkv, "sm": small}
    plans = {}
    for i, (name, e, row) in enumerate(parts):
        out = outs[names.index(name[:2])]
        plans[name] = reduce_stages(
            e, i, sources[name[:2]], out, bufs[7 * i : 7 * i + 7], (send_sem, recv_sem), local_sem, row
        )
    reducer = Reducer(plans)
    gain = [norms[k : k + 1, :] for k in range(4)]
    h_two, h_one = sent, e_two
    step = 512

    def enter():
        loads[0].wait()
        loads[1].wait()
        some(0, rows // chunk, enter_rows)
        loads[2].wait()

    def enter_rows(i):
        r = rows_of(i, chunk)
        g_shift[0:1, :] += column_sum(d_emb[r, :].astype(F32))
        e_two[r, :] = nn(d_emb[r, :], embed_v[...]).astype(BF16)

    def sum_down():
        weight_sum(g_down, e_two, act, stage_wide, sem)

    def sum_embed():
        loads[3].wait()
        weight_sum(g_embed, d_emb, sent, stage, sem)
        for k in range(4, 8):
            loads[k].wait()

    def middle_rows(i):
        r = rows_of(i, chunk)
        e = e_two[r, :]
        for t in range(slope.shape[1] // step):
            cols = slice(t * step, (t + 1) * step)
            d_act = nn(e, down_v[:, cols])
            slope[r, cols] = (d_act * slope[r, cols].astype(F32)).astype(BF16)
        d_h = nn(slope[r, :], up_v[...])
        hat, scale = unit(d_patches[r, :])
        h_two[r, :] = (hat * gain[2] + gain[3]).astype(BF16)
        g_norms[2:3, :] += column_sum(d_h * hat)
        g_norms[3:4, :] += column_sum(d_h)
        d_one = e.astype(F32) + unit_back(d_h * gain[2], hat, scale)
        d_patches[r, :] = d_one
        e_one[r, :] = d_one.astype(BF16)

    def middle(i):
        some(i, i + 1, middle_rows)

    def sum_up():
        load(10, w_qkv, up_v.at[:wide, :])
        load(11, w_out, up_v.at[wide:, :])
        weight_sum(g_up, slope, h_two, stage, sem)
        load(12, s_qkv, slope.at[:, :wide])

    def sum_out():
        loads[8].wait()
        loads[9].wait()
        weight_sum(g_out, e_one, mixed, stage, sem)

    def mix_rows(i):
        r = rows_of(i, chunk)
        mixed[r, :] = nn(e_one[r, :], up_v[wide:, :]).astype(BF16)
        hat, _ = unit(patches[r, :].astype(F32))
        h_one[r, :] = (hat * gain[0] + gain[1]).astype(BF16)

    def mix():
        loads[11].wait()
        some(0, rows // chunk, mix_rows)
        loads[12].wait()

    def attend_back(g):
        r = rows_of(g, n)
        bias = mask_bias(own_row[g], key_col[r, :])
        for t in range(tiles):
            cols = [slice((t + j * tiles) * LANES, (t + j * tiles + 1) * LANES) for j in range(3)]
            q, k, v = [slope[r, col] for col in cols]
            logs = [totals[g, t * per_tile + h : t * per_tile + h + 1, :] for h in range(per_tile)]
            found = attend_tile_back(q, k, v, mixed[r, cols[0]], bias, logs, head_size)
            for j in range(3):
                act[r, cols[j]] = found[j].astype(BF16)

    def attend(i):
        some(i * groups // 4, (i + 1) * groups // 4, attend_back)

    def sum_qkv():
        weight_sum(g_qkv, act.at[:, :wide], h_one, stage, sem)
        loads[10].wait()

    def finish_rows(i):
        r = rows_of(i, chunk)
        d_h = nn(act[r, :wide], up_v[:wide, :])
        hat, scale = unit(patches[r, :].astype(F32))
        g_norms[0:1, :] += column_sum(d_h * hat)
        g_norms[1:2, :] += column_sum(d_h)
        d_patches[r, :] += unit_back(d_h * gain[0], hat, scale)

    def finish(i):
        some(i, i + 1, finish_rows)

    def norms_of_all():
        gather_norms(g_norms[0:4, :], 0, sizes[0], sizes[1], small)

    def norms_of_decoder():
        line = lax.broadcasted_iota(jnp.int32, g_dec.shape, 0)
        joined = jnp.where(line == 7, g_shift[0:1, :], g_dec[...])
        gather_norms(joined, NORM_ROWS // 2, sizes[2], sizes[3], small)

    blocks = {
        "enter": enter,
        "down": sum_down,
        "embed": sum_embed,
        "up": sum_up,
        "out": sum_out,
        "mix": mix,
        "qkv": sum_qkv,
        "norms": norms_of_all,
        "dnorms": norms_of_decoder,
    }
    for i in range(4):
        blocks["mid" + str(i)] = functools.partial(middle, i)
        blocks["att" + str(i)] = functools.partial(attend, i)
        blocks["fin" + str(i)] = functools.partial(finish, i)
    for name, actions in REAR_PLAN:
        if name:
            blocks[name]()
        for action in actions:
            if action[0] == "+":
                reducer.begin(action[1:])
            else:
                reducer.step(action)
    for name, _, _ in parts:
        reducer.finish(name)
    reducer.drain()


REAR_SPLIT = {"qk": 3}
REAR_PLAN = (
    ("", ("+dq",)),
    ("enter", ()),
    ("down", ("+do", "dq")),
    ("dnorms", ()),
    ("embed", ("+em",)),
    ("mid0", ()),
    ("mid1", ("dq", "em", "do")),
    ("mid2", ()),
    ("mid3", ("dq",)),
    ("up", ("+up", "em", "dq")),
    ("out", ("+ou",)),
    ("mix", ()),
    ("att0", ("ou", "do", "up", "em")),
    ("att1", ()),
    ("att2", ("em", "ou")),
    ("att3", ("do",)),
    ("qkv", ("+qk0", "+qk1", "+qk2", "up")),
    ("fin0", ()),
    ("fin1", ("ou",)),
    ("fin2", ("qk0",)),
    ("fin3", ("qk1", "qk2")),
    ("norms", ("+sm", "up", "do", "sm", "qk0", "sm", "qk1", "qk0", "qk2", "sm", "qk1", "qk2", "ou", "up")),
)


def rear(rows_in, norms, g_dec, g_dec_qkv, weights, embed, d_table, stored, sizes):
    x, keys, own = rows_in
    rows, width = x.shape
    groups, _, n = own.shape
    head_size = width // HEADS_E
    ff = weights[2].shape[0]
    first = (8 * g_dec_qkv.shape[2], g_dec_qkv.shape[3])
    names = ("dq", "do", "em", "up", "ou", "qk", "sm")
    shapes = [first, weights[3].shape, embed.shape, weights[2].shape, weights[1].shape, weights[0].shape]
    entries = [entry_of(s[0] // 8, s[1]) for s in shapes] + [entry_of(NORM_ROWS, 512)]
    parts = []
    for name, e in zip(names, entries):
        count = REAR_SPLIT.get(name, 1)
        for k in range(count):
            cut = dataclasses.replace(e, share=count)
            parts.append((name + (str(k) if count > 1 else ""), cut, k * cut.part))
    vm, hbm = pl.BlockSpec(memory_space=pltpu.VMEM), pl.BlockSpec(memory_space=pl.ANY)
    sem = pltpu.SemaphoreType.DMA
    n_in = len(parts)
    totals = stored[1]
    found = pl.pallas_call(
        functools.partial(rear_kernel, parts, names, head_size, groups, rows // 4, sizes),
        out_shape=[jax.ShapeDtypeStruct((rows, width), F32)]
        + [jax.ShapeDtypeStruct(s, BF16) for s in (shapes[2], shapes[1], *shapes[3:])]
        + [jax.ShapeDtypeStruct((e.part, e.q), F32) for e in entries],
        in_specs=[vm] * 5 + [hbm] * 14,
        out_specs=[vm] + [hbm] * 5 + [vm] * len(names),
        scratch_shapes=[
            pltpu.VMEM(weights[2].shape, BF16),
            pltpu.VMEM(weights[3].shape, BF16),
            pltpu.VMEM(embed.shape, BF16),
            pltpu.VMEM((rows, ff), BF16),
            pltpu.VMEM((rows, ff), BF16),
            pltpu.VMEM((rows, width), BF16),
            pltpu.VMEM((rows, width), BF16),
            pltpu.VMEM((rows, width), BF16),
            pltpu.VMEM((rows, width), BF16),
            pltpu.VMEM(d_table.shape, BF16),
            pltpu.VMEM(totals.shape, F32),
            pltpu.VMEM(entries[-1].whole, BF16),
            pltpu.VMEM((2, 256, width), BF16),
            pltpu.VMEM((2, LANES, ff), BF16),
            sem((2,)),
            pltpu.VMEM((8, width), F32),
            pltpu.VMEM((8, embed.shape[0]), F32),
        ]
        + [pltpu.VMEM(shape, BF16) for _, e, _ in parts for shape in reduce_buffers(e)]
        + [sem((n_in, 9)), sem((n_in, 9)), sem((n_in,)), sem((13,))],
        compiler_params=pltpu.CompilerParams(
            collective_id=2, has_side_effects=True, vmem_limit_bytes=63 << 20
        ),
        name="rear",
    )(x, keys, own, norms, g_dec, g_dec_qkv, *weights, embed, d_table, *stored)
    return found[0], found[6:]


def per_device(
    staged,
    patches,
    send_counts,
    dec_segment,
    source_index,
    cotangent,
    enc_norms,
    enc_qkv,
    enc_out,
    enc_up,
    enc_down,
    dec_norms,
    dec_embed,
    dec_qkv,
    dec_out,
    dec_up,
    dec_down,
):
    peers = lax.axis_size("dp")
    width = patches.shape[1]
    slot_rows = patches.shape[0] // peers
    counts = send_counts.reshape(peers)
    masters = (enc_qkv, enc_out, enc_up, dec_embed, enc_down, dec_qkv, dec_out, dec_up, dec_down)
    padded = slot_plan(peers, slot_rows)[0]

    def swap(table):
        slots = table.reshape(peers, padded, table.shape[1])
        return lax.all_to_all(slots, "dp", split_axis=0, concat_axis=0, tiled=True).reshape(table.shape)

    if staged:
        entries, pieces = staged_pieces(enc_norms, dec_norms, masters)
        sizes = (*enc_norms.shape, *dec_norms.shape)
        whole, norms_e, norms_d, table, enc_inputs, stored = front(
            entries, pieces, patches, counts, sizes, HEADS_E
        )
        whole = [w.reshape(-1, w.shape[-1]) for w in whole[1:]]
        table = table.reshape(-1, table.shape[-1])
    else:
        norms_e, norms_d, whole = gather_masters(enc_norms, dec_norms, masters)
    enc_weights, embed, dec_weights = [*whole[:3], whole[4]], whole[3], whole[5:]
    if not staged:
        embedded, enc_inputs, stored = encoder(
            patches, counts, norms_e, norms_d, enc_weights, embed, HEADS_E
        )
        table = swap(embedded)
    place_of = source_index // slot_rows * padded + source_index % slot_rows
    index = jnp.where(source_index >= 0, place_of, -1)
    if staged:
        decoded, d_table, g_dec_norms, g_qkv, _, _, _, s_down, s_up, s_out = decoder(
            True, table, index, dec_segment, cotangent, norms_d, dec_weights, HEADS_D
        )
        e = entry_of(g_qkv.shape[0] // 8, g_qkv.shape[1])
        d_patches, sums = rear(
            enc_inputs,
            norms_e,
            g_dec_norms,
            g_qkv.reshape(e.whole),
            enc_weights,
            embed,
            d_table.reshape(table.shape),
            stored,
            sizes,
        )
        s_qkv, e_down, s_embed, e_up, e_out, e_qkv, small = sums
        half = NORM_ROWS // 2
        s_enc_norms = small[: sizes[0], : sizes[1]]
        s_dec_norms = small[half : half + sizes[2], : sizes[3]]
        sums = own_blocks(
            [e_qkv, e_out, e_up, e_down, s_embed, s_qkv, s_out, s_up, s_down],
            [enc_qkv, enc_out, enc_up, enc_down, dec_embed, dec_qkv, dec_out, dec_up, dec_down],
        )
    else:
        decoded, d_table, g_dec_norms, *dec_grads = decoder(
            False, table, index, dec_segment, cotangent, norms_d, dec_weights, HEADS_D
        )
        d_patches, g_enc_norms, g_shift, *enc_grads = encoder_back(
            enc_inputs,
            norms_e,
            enc_weights,
            embed,
            swap(d_table.reshape(table.shape)),
            stored,
            HEADS_E,
        )
        g_dec_norms = jnp.concatenate([g_dec_norms[:7], g_shift[:1]], axis=0)
        s_enc_norms, s_dec_norms, sums = reduce_masters(
            g_enc_norms[:4], g_dec_norms, [*enc_grads, *dec_grads]
        )
    d_patches = d_patches.reshape(peers, padded, width)[:, :slot_rows]
    return (
        decoded,
        d_patches.reshape(-1, width),
        s_enc_norms,
        *sums[:4],
        s_dec_norms,
        *sums[4:],
    )


def solution(mesh):
    placed = (
        P(("dp", "fsdp"), None),
        P(("dp", "fsdp"), None),
        P(("dp", "fsdp"), None),
        P(("dp", "fsdp"), None),
        P(("dp", "fsdp"), None, None),
        P("fsdp", "dp"),
        P("fsdp", "dp"),
        P("fsdp", "dp"),
        P("fsdp", "dp"),
        P("fsdp", "dp"),
        P("fsdp", "dp"),
        P("fsdp", "dp"),
        P("fsdp", "dp"),
        P("fsdp", "dp"),
        P("fsdp", "dp"),
        P("fsdp", "dp"),
    )
    staged = (mesh.shape["dp"], mesh.shape["fsdp"]) == (8, 4)
    return jax.shard_map(
        functools.partial(per_device, staged),
        mesh=mesh,
        in_specs=placed,
        out_specs=(
            P(("dp", "fsdp"), None, None),
            P(("dp", "fsdp"), None),
            P("fsdp", "dp"),
            P("fsdp", "dp"),
            P("fsdp", "dp"),
            P("fsdp", "dp"),
            P("fsdp", "dp"),
            P("fsdp", "dp"),
            P("fsdp", "dp"),
            P("fsdp", "dp"),
            P("fsdp", "dp"),
            P("fsdp", "dp"),
            P("fsdp", "dp"),
        ),
        check_vma=False,
    )
```

```python
import dataclasses
import functools

import jax
import jax.numpy as jnp
from jax import lax
from jax.experimental import pallas as pl
from jax.experimental.pallas import tpu as pltpu
from jax.sharding import PartitionSpec as P

HEADS_E = 12
HEADS_D = 16


EPSILON = 1e-06
NEGATIVE = -1000000000.0
LANES = 128
MESH = pl.DeviceIdType.MESH
BF16 = jnp.bfloat16
F32 = jnp.float32


def in_blocks(value, dim, length):
    dims = value.shape
    pieces = value.reshape(*dims[:dim], length, dims[dim] // length, *dims[dim + 1 :])
    return jnp.moveaxis(pieces, dim, 0)


def sum_at_owner(value, axis, dim):
    length = lax.axis_size(axis)
    pieces = lax.all_to_all(in_blocks(value, dim, length), axis, 0, 0, tiled=True)
    return jnp.sum(pieces.astype(jnp.float32), axis=0)


@dataclasses.dataclass(frozen=True)
class Entry:
    rows: int
    width: int
    by_core: bool
    share: int = 1

    @property
    def q(self):
        return self.width // 2 if self.by_core else self.width // 4

    @property
    def block(self):
        return self.rows // 2 if self.by_core else self.rows

    @property
    def part(self):
        return self.block // self.share

    @property
    def whole(self):
        if self.by_core:
            return (4, 2, 2, self.part, self.width)
        return (4, 2, self.part, self.width)

    @property
    def cut(self):
        return -(-self.part // 32) * 16


def entry_of(rows, width):
    return Entry(rows, width, (width // 4) % 128 != 0)


def region(e, ref, zs, xs, rows, y, c):
    if e.by_core:
        return ref.at[zs, xs, c, rows, pl.ds(pl.multiple_of(y * e.q, 128), e.q)]
    return ref.at[zs, xs, rows, pl.ds(pl.multiple_of((2 * y + c) * e.q, 128), e.q)]


def region_pair(e, ref, zs, xs, rows, c):
    if e.by_core:
        return [ref.at[zs, xs, c, rows, :]]
    return [region(e, ref, zs, xs, rows, y, c) for y in range(2)]


def place():
    d, s = lax.axis_index("dp"), lax.axis_index("fsdp")
    return d // 2, lax.rem(d, 2), s // 2, lax.rem(s, 2)


def at(z, x, y, c):
    return (z * 2 + x, y * 2 + c)


def send(src, dst, sems, i, k, peer):
    return pltpu.make_async_remote_copy(
        src_ref=src,
        dst_ref=dst,
        send_sem=sems[0].at[i, k],
        recv_sem=sems[1].at[i, k],
        device_id=peer,
        device_id_type=MESH,
    )


ALL = slice(None)


def gather_stages(e, i, piece, out, sems, local_sem):
    z, x, y, c = place()
    top, bottom = slice(0, e.cut), slice(e.cut, e.part)

    def first():
        here = region(e, out, z, x, ALL, y, c)
        return [
            send(piece, here, sems, i, k - 1, at(lax.rem(z + k, 4), x, y, c)) for k in (1, 2, 3)
        ]

    def local():
        return pltpu.make_async_copy(piece, region(e, out, z, x, ALL, y, c), local_sem.at[i])

    def second():
        a = region(e, out, ALL, x, top, y, c)
        b = region(e, out, ALL, x, bottom, y, c)
        return [
            send(a, a, sems, i, 3, at(z, 1 - x, y, c)),
            send(b, b, sems, i, 4, at(z, x, 1 - y, c)),
        ]

    def third():
        a = region(e, out, ALL, ALL, top, y, c)
        found = [send(a, a, sems, i, 5, at(z, x, 1 - y, c))]
        for k, b in enumerate(region_pair(e, out, ALL, x, bottom, c)):
            found.append(send(b, b, sems, i, 6 + k, at(z, 1 - x, y, c)))
        return found

    def fourth():
        return [
            send(b, b, sems, i, 8 + k, at(z, x, y, 1 - c))
            for k, b in enumerate(region_pair(e, out, ALL, ALL, ALL, c))
        ]

    return local, [first, second, third, fourth]


def reduce_stages(e, i, grad, out, buf, sems, local_sem, row=0, place_row=0):
    z, x, y, c = place()
    acc, r4, r3a, r3b, r2a, r2b, r1 = buf
    q, cut, part = e.q, e.cut, e.part
    top, bottom = slice(0, cut), slice(cut, part)

    def lanes(y):
        return pl.ds(pl.multiple_of(y * q, 128), q)

    def share(core, ref):
        if len(grad.shape) > 2:
            into = [ref] if e.by_core else [ref.at[:, :, :, pl.ds(k * q, q)] for k in range(2)]
            return list(zip(region_pair(e, grad, ALL, ALL, slice(row, row + part), core), into))
        found = []
        for b in range(8):
            to = ref.at[b // 2, b % 2]
            if e.by_core:
                first = pl.multiple_of((2 * b + core) * e.block + row, 16)
                found.append((grad.at[pl.ds(first, part), :], to))
                continue
            for k in range(2):
                cols = pl.ds(pl.multiple_of((2 * k + core) * q, 128), q)
                found.append((grad.at[pl.ds(b * e.block + row, part), cols], to.at[:, pl.ds(k * q, q)]))
        return found

    def local():
        copies = [pltpu.make_async_copy(src, dst, local_sem.at[i]) for src, dst in share(c, acc)]
        return copies, [pltpu.make_async_copy(acc, acc, local_sem.at[i])]

    def first():
        peer = at(z, x, y, 1 - c)
        copies = [send(src, dst, sems, i, 0, peer) for src, dst in share(1 - c, r4)]
        return copies, [send(r4, r4, sems, i, 0, peer)]

    def add_first():
        def step(k, carry):
            a, b = k // 2, lax.rem(k, 2)
            acc[a, b] = (acc[a, b].astype(F32) + r4[a, b].astype(F32)).astype(BF16)
            return carry

        lax.fori_loop(0, 8, step, 0)

    def second():
        found = [
            send(acc.at[:, :, top, lanes(1 - y)], r3a, sems, i, 2, at(z, x, 1 - y, c)),
            send(acc.at[:, 1 - x, bottom, :], r3b, sems, i, 3, at(z, 1 - x, y, c)),
        ]
        return found, found

    def add_second():
        def step(k, carry):
            for b in range(2):
                acc[k, b, top, lanes(y)] = (
                    acc[k, b, top, lanes(y)].astype(F32) + r3a[k, b].astype(F32)
                ).astype(BF16)
            acc[k, x, bottom, :] = (
                acc[k, x, bottom, :].astype(F32) + r3b[k].astype(F32)
            ).astype(BF16)
            return carry

        lax.fori_loop(0, 4, step, 0)

    def third():
        found = [
            send(acc.at[:, 1 - x, top, lanes(y)], r2a, sems, i, 4, at(z, 1 - x, y, c)),
            send(acc.at[:, x, bottom, lanes(1 - y)], r2b, sems, i, 5, at(z, x, 1 - y, c)),
        ]
        return found, found

    def add_third():
        def step(k, carry):
            acc[k, x, top, lanes(y)] = (
                acc[k, x, top, lanes(y)].astype(F32) + r2a[k].astype(F32)
            ).astype(BF16)
            acc[k, x, bottom, lanes(y)] = (
                acc[k, x, bottom, lanes(y)].astype(F32) + r2b[k].astype(F32)
            ).astype(BF16)
            return carry

        lax.fori_loop(0, 4, step, 0)

    def fourth():
        found = []
        for k in (1, 2, 3):
            there = lax.rem(z + k, 4)
            found.append(
                send(acc.at[there, x, :, lanes(y)], r1.at[k - 1], sems, i, 5 + k, at(there, x, y, c))
            )
        return found, found

    def add_fourth():
        total = acc[z, x, :, lanes(y)].astype(F32)
        for k in range(3):
            total = total + r1[k].astype(F32)
        out[place_row + row : place_row + row + part, :] = total

    return local, [(first, add_first), (second, add_second), (third, add_third), (fourth, add_fourth)]


def reduce_buffers(e):
    return [
        (4, 2, e.part, 2 * e.q),
        (4, 2, e.part, 2 * e.q),
        (4, 2, e.cut, e.q),
        (4, e.part - e.cut, 2 * e.q),
        (4, e.cut, e.q),
        (4, e.part - e.cut, e.q),
        (3, e.part, e.q),
    ]


CORE_SWAP = [(0, 1), (1, 0), (2, 3), (3, 2)]
NORM_ROWS = 32


def halves_to_pieces(blocks):
    c = lax.rem(lax.axis_index("fsdp"), 2)
    both = jnp.concatenate([b.reshape(2, b.shape[0] // 2, b.shape[1]) for b in blocks], axis=1)
    mine = lax.dynamic_index_in_dim(both, c, 0, keepdims=False)
    other = lax.dynamic_index_in_dim(both, 1 - c, 0, keepdims=False)
    came = lax.ppermute(other, "fsdp", CORE_SWAP)
    left, right = jnp.where(c == 0, mine, came), jnp.where(c == 0, came, mine)
    return jnp.concatenate([left, right], axis=1)


def pieces_to_halves(whole):
    c = lax.rem(lax.axis_index("fsdp"), 2)
    q = whole.shape[1] // 2
    left, right = whole[:, :q], whole[:, q:]
    mine, other = jnp.where(c == 0, left, right), jnp.where(c == 0, right, left)
    came = lax.ppermute(other, "fsdp", CORE_SWAP)
    return jnp.where(c == 0, mine, came), jnp.where(c == 0, came, mine)


def gather_masters(enc_norms, dec_norms, weights):
    whole = []
    for w in weights:
        tall = lax.all_gather(w.astype(BF16).T, "dp", axis=0, tiled=True)
        whole.append(lax.all_gather(tall, "fsdp", axis=1, tiled=True))
    norms = []
    for rows in (enc_norms, dec_norms):
        wide = lax.all_gather(rows.astype(BF16), "dp", axis=1, tiled=True)
        norms.append(lax.all_gather(wide, "fsdp", axis=0, tiled=True))
    return norms[0], norms[1], whole


def staged_pieces(enc_norms, dec_norms, weights):
    blocks = [w.astype(BF16).T for w in weights]
    entries = [entry_of(b.shape[0], 4 * b.shape[1]) for b in blocks]
    pieces = list(blocks)
    cores = [k for k, e in enumerate(entries) if e.by_core]
    joined = halves_to_pieces([blocks[k] for k in cores])
    start = 0
    for k in cores:
        pieces[k] = lax.slice_in_dim(joined, start, start + entries[k].part, axis=0)
        start += entries[k].part
    small = jnp.zeros((NORM_ROWS, 128), BF16)
    small = small.at[: enc_norms.shape[0], : enc_norms.shape[1]].set(enc_norms.astype(BF16))
    half = NORM_ROWS // 2
    small = small.at[half : half + dec_norms.shape[0], : dec_norms.shape[1]].set(
        dec_norms.astype(BF16)
    )
    entries = [entry_of(NORM_ROWS, 512)] + entries
    return entries, [small] + pieces


def reduce_masters(g_enc_norms, g_dec_norms, grads):
    def owner(value, rows, lanes):
        part = lax.psum_scatter(value.astype(BF16), "fsdp", scatter_dimension=lanes, tiled=True)
        return sum_at_owner(part, "dp", rows)

    return (
        owner(g_enc_norms, 1, 0),
        owner(g_dec_norms, 1, 0),
        [owner(g, 0, 1).T for g in grads],
    )


def own_block(halves, first, master):
    rows = master.shape[1] // 2
    return jnp.concatenate([h[first : first + rows] for h in halves], axis=0).T


def nn(a, b):
    return lax.dot_general(a, b, (((1,), (0,)), ((), ())), preferred_element_type=F32)


def nt(a, b):
    return lax.dot_general(a, b, (((1,), (1,)), ((), ())), preferred_element_type=F32)


def tn(a, b):
    return lax.dot_general(a, b, (((0,), (0,)), ((), ())), preferred_element_type=F32)


def unit(values):
    centred = values - jnp.mean(values, axis=-1, keepdims=True)
    scale = lax.rsqrt(jnp.mean(centred * centred, axis=-1, keepdims=True) + EPSILON)
    return centred * scale, scale


def unit_back(d_hat, hat, scale):
    along = jnp.mean(d_hat * hat, axis=-1, keepdims=True)
    return scale * (d_hat - jnp.mean(d_hat, axis=-1, keepdims=True) - hat * along)


def column_sum(values):
    return jnp.sum(values, axis=0, keepdims=True)


def gelu_pair(u):
    phi = 0.5 + 0.5 * lax.erf(u * 0.7071067811865476)
    return u * phi, phi + u * (0.3989422804014327 * jnp.exp(-0.5 * u * u))


def head_lanes(shape, head_size, h):
    return lax.broadcasted_iota(jnp.int32, shape, 1) // head_size == h


def pick(values, head_size, h):
    return jnp.where(head_lanes(values.shape, head_size, h), values, jnp.zeros_like(values))


LOG2_E = 1.4426950408889634


def attend_tile(q, k, v, bias, head_size):
    v_t = v.astype(F32).T.astype(BF16)
    mixed, totals = [], []
    for h in range(LANES // head_size):
        scores = nt(pick(k, head_size, h), q) * (head_size**-0.5 * LOG2_E) + bias
        top = jnp.max(scores, axis=0, keepdims=True)
        weight = jnp.exp2(scores - top)
        total = jnp.sum(weight, axis=0, keepdims=True)
        part = nn(v_t[h * head_size : (h + 1) * head_size], weight.astype(BF16))
        mixed.append(part * (1.0 / total))
        totals.append(top + jnp.log(total) * LOG2_E)
    return jnp.concatenate(mixed, axis=0).T, totals


def attend_tile_back(q, k, v, d_mixed, bias, totals, head_size):
    k_t = k.astype(F32).T.astype(BF16)
    d_q, d_k, d_v = [], 0.0, 0.0
    for h in range(LANES // head_size):
        scores = nt(pick(k, head_size, h), q) * (head_size**-0.5 * LOG2_E) + bias
        prob = jnp.exp2(scores - totals[h])
        d_prob = nt(pick(v, head_size, h), d_mixed)
        centre = jnp.sum(d_prob * prob, axis=0, keepdims=True)
        d_score = (prob * (d_prob - centre)).astype(BF16)
        d_v = d_v + nn(prob.astype(BF16), pick(d_mixed, head_size, h))
        d_k = d_k + nn(d_score, pick(q, head_size, h))
        d_q.append(nn(k_t[h * head_size : (h + 1) * head_size], d_score))
    d_q = jnp.concatenate(d_q, axis=0).T
    return d_q * head_size**-0.5, d_k * head_size**-0.5, d_v


def lane_tile(t):
    return pl.ds(pl.multiple_of(t * LANES, LANES), LANES)


def rows_of(i, n):
    return pl.ds(pl.multiple_of(i * n, 16), n)


def mask_bias(own, keys):
    return jnp.where(keys == own, 0.0, NEGATIVE).astype(F32)


def outer_loop(count, body):
    def step(i, carry):
        body(i)
        return carry

    lax.fori_loop(0, count, step, 0)


def weight_sum(dst, left, right, stage, sem):
    _, tile, width = stage.shape
    count = left.shape[1] // tile

    def off(t):
        slot = lax.rem(t, 2)
        rows = pl.ds(pl.multiple_of(t * tile, LANES), tile)
        return pltpu.make_async_copy(stage.at[slot], dst.at[rows, :], sem.at[slot])

    def one(t):
        @pl.when(t >= 2)
        def _():
            off(t - 2).wait()

        cols = pl.ds(pl.multiple_of(t * tile, LANES), tile)
        stage[lax.rem(t, 2)] = tn(left[:, cols], right[...]).astype(BF16)
        off(t).start()

    outer_loop(count, one)
    for t in range(max(0, count - 2), count):
        off(t).wait()


def decoder_body(
    hooks,
    head_size,
    chunk,
    table,
    marks_col,
    marks_row,
    cot,
    norms,
    w_qkv,
    w_out,
    w_up,
    w_down,
    decoded,
    d_table,
    g_norms,
    g_qkv,
    g_out,
    g_up,
    g_down,
    x,
    h_one,
    qkv,
    mixed,
    totals,
    h_two,
    act,
    slope,
    d_up,
    e_two,
    e_one,
    bias,
    d_x,
    stage,
    stage_wide,
    sem,
):
    groups, n, width = cot.shape
    real = decoded.shape[1]
    rows = groups * n
    per_group = n // chunk
    tiles = width // LANES
    per_tile = LANES // head_size
    gain = [norms[k : k + 1, :].astype(F32) for k in range(8)]
    g_norms[...] = jnp.zeros_like(g_norms)

    def start(i):
        r = rows_of(i, chunk)
        slots = lax.broadcasted_iota(jnp.int32, (chunk, table.shape[0]), 1)
        named = marks_col[r, 0:1]
        chosen = jnp.where(slots == named, 1.0, 0.0).astype(BF16)
        picked = nn(chosen, table[...])
        begin = jnp.where(named >= 0, picked, gain[6])
        x[r, :] = begin
        hat, _ = unit(begin)
        h = (hat * gain[0] + gain[1]).astype(BF16)
        h_one[r, :] = h
        qkv[r, :] = nt(h, w_qkv[...]).astype(BF16)

    outer_loop(rows // chunk, start)

    def attend(g):
        bias[...] = mask_bias(marks_row[g, 1:2, :], marks_col[rows_of(g, n), 1:2])
        r = rows_of(g, n)

        def one(t):
            q, k, v = [qkv[r, lane_tile(t + j * tiles)] for j in range(3)]
            out, logs = attend_tile(q, k, v, bias[...], head_size)
            mixed[r, lane_tile(t)] = out.astype(BF16)
            for h in range(per_tile):
                totals[g * tiles + t, h : h + 1, :] = logs[h]

        outer_loop(tiles, one)

    outer_loop(groups, attend)

    def middle(i):
        g, j = i // per_group, lax.rem(i, per_group)
        r = rows_of(i, chunk)
        one = x[r, :] + nt(mixed[r, :], w_out[...])
        hat_two, scale_two = unit(one)
        h = (hat_two * gain[2] + gain[3]).astype(BF16)
        h_two[r, :] = h
        step = 512
        for t in range(w_up.shape[0] // step):
            u = nt(h, w_up[t * step : (t + 1) * step, :])
            a, s = gelu_pair(u)
            act[r, t * step : (t + 1) * step] = a.astype(BF16)
            slope[:, t * step : (t + 1) * step] = s.astype(BF16)
        two = one + nt(act[r, :], w_down[...])
        hat, scale = unit(two)
        result = hat * gain[4] + gain[5]
        for b in range(groups):
            for c in range(per_group):
                lo = c * chunk
                hi = min(lo + chunk, real)

                @pl.when(i == b * per_group + c)
                def _(b=b, lo=lo, hi=hi):
                    decoded[b, lo:hi, :] = result[: hi - lo]

        cr = rows_of(j, chunk)
        d = cot[g, cr, :]
        g_norms[4:5, :] += column_sum(d * hat)
        g_norms[5:6, :] += column_sum(d)
        d_two = unit_back(d * gain[4], hat, scale)
        e = d_two.astype(BF16)
        e_two[r, :] = e
        for t in range(w_up.shape[0] // step):
            cols = slice(t * step, (t + 1) * step)
            d_act = nn(e, w_down[:, cols])
            d_up[r, cols] = (d_act * slope[:, cols].astype(F32)).astype(BF16)
        d_h = nn(d_up[r, :], w_up[...])
        g_norms[2:3, :] += column_sum(d_h * hat_two)
        g_norms[3:4, :] += column_sum(d_h)
        d_one = d_two + unit_back(d_h * gain[2], hat_two, scale_two)
        d_x[g, cr, :] = d_one
        e_one[r, :] = d_one.astype(BF16)

    outer_loop(rows // chunk, middle)

    weight_sum(g_down, e_two, act, stage_wide, sem)
    hooks.summed(0)
    weight_sum(g_up, d_up, h_two, stage, sem)
    hooks.summed(1)
    weight_sum(g_out, e_one, mixed, stage, sem)
    hooks.summed(2)

    def mix_back(i):
        r = rows_of(i, chunk)
        mixed[r, :] = nn(e_one[r, :], w_out[...]).astype(BF16)

    outer_loop(rows // chunk, mix_back)
    d_qkv = act

    for g in range(groups):
        bias[...] = mask_bias(marks_row[g, 1:2, :], marks_col[rows_of(g, n), 1:2])
        r = rows_of(g, n)

        def one(t, g=g, r=r):
            q, k, v = [qkv[r, lane_tile(t + j * tiles)] for j in range(3)]
            logs = [totals[g * tiles + t, h : h + 1, :] for h in range(per_tile)]
            found = attend_tile_back(q, k, v, mixed[r, lane_tile(t)], bias[...], logs, head_size)
            for j in range(3):
                d_qkv[r, lane_tile(t + j * tiles)] = found[j].astype(BF16)

        for half in range(2):
            some(half * tiles // 2, (half + 1) * tiles // 2, one)
            hooks.pause(2 * g + half)

    def finish(i):
        g, j = i // per_group, lax.rem(i, per_group)
        r, cr = rows_of(i, chunk), rows_of(j, chunk)
        d_h = nn(d_qkv[r, : 3 * width], w_qkv[...])
        hat, scale = unit(x[r, :])
        g_norms[0:1, :] += column_sum(d_h * hat)
        g_norms[1:2, :] += column_sum(d_h)
        d_start = d_x[g, cr, :] + unit_back(d_h * gain[0], hat, scale)
        seen = marks_col[r, 0:1] >= 0
        g_norms[6:7, :] += column_sum(jnp.where(seen, 0.0, d_start))
        e_two[r, :] = jnp.where(seen, d_start, 0.0).astype(BF16)

    outer_loop(rows // chunk, finish)

    slots, slot_rows, _ = d_table.shape

    def back(s):
        line = lax.broadcasted_iota(jnp.int32, (slot_rows, n), 0) + s * slot_rows
        total = 0.0
        for g in range(groups):
            chosen = jnp.where(line == marks_row[g, 0:1, :], 1.0, 0.0).astype(BF16)
            total = total + nn(chosen, e_two[g * n : (g + 1) * n, :])
        d_table[s] = total.astype(BF16)

    hooks.slots(back, slots)
    weight_sum(g_qkv, d_qkv.at[:, : 3 * width], h_one, stage, sem)
    hooks.end()


def some(lo, hi, body):
    def step(i, carry):
        body(i)
        return carry

    lax.fori_loop(lo, hi, step, 0)


class NoHooks:
    def summed(self, k):
        pass

    def pause(self, k):
        pass

    def slots(self, body, count):
        outer_loop(count, body)

    def end(self):
        pass


class MiddleHooks:
    def __init__(self, reducer, d_table, returned, swap_send, swap_recv, swap_local):
        self.reducer = reducer
        self.d_table, self.returned = d_table, returned
        self.swap = (swap_send, swap_recv, swap_local)

    def summed(self, k):
        if k == 1:
            self.reducer.step(0)
        self.reducer.begin(k)

    def pause(self, k):
        for i in range(3):
            self.reducer.step(i)

    def slots(self, body, count):
        z, x, y, c = place()
        d, f = z * 2 + x, y * 2 + c
        send_sem, recv_sem, local_sem = self.swap
        for s in range(count):
            some(s, s + 1, body)

            @pl.when(s != d)
            def _(s=s):
                send_slot(self.d_table, self.returned, s, d, send_sem, recv_sem, f).start()

            @pl.when(s == d)
            def _(s=s):
                pltpu.make_async_copy(
                    self.d_table.at[s], self.returned.at[s], local_sem.at[0]
                ).start()

    def end(self):
        z, x, y, c = place()
        for i in range(3):
            self.reducer.finish(i)
        finish_swap(self.d_table, self.returned, z * 2 + x, *self.swap, y * 2 + c)
        self.reducer.drain()


def decoder_kernel(head_size, chunk, *refs):
    decoder_body(NoHooks(), head_size, chunk, *refs)


def middle_kernel(entries, head_size, chunk, *refs):
    ins, refs = refs[:9], refs[9:]
    decoded, returned, g_norms, *refs = refs
    grads, refs = refs[:4], refs[4:]
    outs, refs = refs[:3], refs[3:]
    scratch, refs = refs[:16], refs[16:]
    d_table, *refs = refs
    bufs, refs = refs[:21], refs[21:]
    send_sem, recv_sem, local_sem, swap_send, swap_recv, swap_local = refs
    z, x, y, c = place()
    meet(z, x, y, c)
    by_entry = [grads[3], grads[2], grads[1]]
    reducer = Reducer(
        [
            reduce_stages(e, i, by_entry[i], outs[i], bufs[7 * i : 7 * i + 7], (send_sem, recv_sem), local_sem)
            for i, e in enumerate(entries)
        ]
    )
    hooks = MiddleHooks(reducer, d_table, returned, swap_send, swap_recv, swap_local)
    decoder_body(hooks, head_size, chunk, *ins, decoded, d_table, g_norms, *grads, *scratch)


def decoder(staged, table, index, segment, cotangent, norms, weights, heads):
    groups, real, width = cotangent.shape
    n = -(-real // 32) * 32
    chunk = n // 2
    rows = groups * n
    head_size = width // heads
    pad = n - real
    marks = jnp.stack([index, segment], axis=1)
    marks = jnp.pad(marks, ((0, 0), (0, 0), (0, pad)), constant_values=-1)
    cot = jnp.pad(cotangent, ((0, 0), (0, pad), (0, 0)))
    tiles = width // LANES
    ff = weights[2].shape[0]
    vm = pl.BlockSpec(memory_space=pltpu.VMEM)
    hbm = pl.BlockSpec(memory_space=pl.ANY)
    scratch = [
        pltpu.VMEM((rows, width), F32),
        pltpu.VMEM((rows, width), BF16),
        pltpu.VMEM((rows, 3 * width), BF16),
        pltpu.VMEM((rows, width), BF16),
        pltpu.VMEM((groups * tiles, LANES // head_size, n), F32),
        pltpu.VMEM((rows, width), BF16),
        pltpu.VMEM((rows, ff), BF16),
        pltpu.VMEM((chunk, ff), BF16),
        pltpu.VMEM((rows, ff), BF16),
        pltpu.VMEM((rows, width), BF16),
        pltpu.VMEM((rows, width), BF16),
        pltpu.VMEM((n, n), F32),
        pltpu.VMEM(cot.shape, F32),
        pltpu.VMEM((2, 256, width), BF16),
        pltpu.VMEM((2, LANES, ff), BF16),
        pltpu.SemaphoreType.DMA((2,)),
    ]
    args = (
        table,
        marks.transpose(0, 2, 1).reshape(rows, 2),
        marks,
        cot,
        norms,
        *weights,
    )
    slots = (8, table.shape[0] // 8, width)
    shapes = [
        jax.ShapeDtypeStruct(cotangent.shape, F32),
        jax.ShapeDtypeStruct(slots, BF16),
        jax.ShapeDtypeStruct((8, width), F32),
    ] + [jax.ShapeDtypeStruct(w.shape, BF16) for w in weights]
    if not staged:
        return pl.pallas_call(
            functools.partial(decoder_kernel, head_size, chunk),
            out_shape=shapes,
            in_specs=[vm] * 9,
            out_specs=[vm] * 3 + [hbm] * 4,
            scratch_shapes=scratch,
            compiler_params=pltpu.CompilerParams(vmem_limit_bytes=60 << 20),
            name="decoder",
        )(*args)
    entries = [entry_of(w.shape[0] // 8, w.shape[1]) for w in (weights[3], weights[2], weights[1])]
    sem = pltpu.SemaphoreType.DMA
    return pl.pallas_call(
        functools.partial(middle_kernel, entries, head_size, chunk),
        out_shape=shapes + [jax.ShapeDtypeStruct((e.part, e.q), F32) for e in entries],
        in_specs=[vm] * 9,
        out_specs=[vm, hbm, vm] + [hbm] * 4 + [vm] * 3,
        scratch_shapes=scratch
        + [pltpu.VMEM(slots, BF16)]
        + [pltpu.VMEM(shape, BF16) for e in entries for shape in reduce_buffers(e)]
        + [sem((3, 9)), sem((3, 9)), sem((3,)), sem((8,)), sem((8,)), sem((1,))],
        compiler_params=pltpu.CompilerParams(
            collective_id=1, has_side_effects=True, vmem_limit_bytes=62 << 20
        ),
        name="middle",
    )(*args)


def encoder_kernel(
    head_size,
    groups,
    chunk,
    patches,
    key_col,
    own_row,
    norms,
    shift,
    w_qkv,
    w_out,
    w_up,
    w_down,
    w_embed,
    embedded,
    qkv,
    totals,
    mixed,
    x_one,
    act,
    slope,
    sent,
):
    rows, width = patches.shape
    n = rows // groups
    tiles = width // LANES
    per_tile = LANES // head_size
    gain = [norms[k : k + 1, :].astype(F32) for k in range(4)]
    add = shift[7:8, :].astype(F32)

    def start(i):
        r = rows_of(i, chunk)
        hat, _ = unit(patches[r, :].astype(F32))
        qkv[r, :] = nt((hat * gain[0] + gain[1]).astype(BF16), w_qkv[...]).astype(BF16)

    outer_loop(rows // chunk, start)

    def attend(g):
        r = rows_of(g, n)
        bias = mask_bias(own_row[g], key_col[r, :])
        for t in range(tiles):
            q, k, v = [qkv[r, (t + j * tiles) * LANES : (t + j * tiles + 1) * LANES] for j in range(3)]
            out, logs = attend_tile(q, k, v, bias, head_size)
            mixed[r, t * LANES : (t + 1) * LANES] = out.astype(BF16)
            for h in range(per_tile):
                totals[g, t * per_tile + h : t * per_tile + h + 1, :] = logs[h]

    outer_loop(groups, attend)

    def middle(i):
        r = rows_of(i, chunk)
        one = patches[r, :].astype(F32) + nt(mixed[r, :], w_out[...])
        x_one[r, :] = one
        hat, _ = unit(one)
        h = (hat * gain[2] + gain[3]).astype(BF16)
        step = 512
        for t in range(w_up.shape[0] // step):
            u = nt(h, w_up[t * step : (t + 1) * step, :])
            a, s = gelu_pair(u)
            act[r, t * step : (t + 1) * step] = a.astype(BF16)
            slope[r, t * step : (t + 1) * step] = s.astype(BF16)
        two = (one + nt(act[r, :], w_down[...])).astype(BF16)
        sent[r, :] = two
        embedded[r, :] = (nt(two, w_embed[...]) + add).astype(BF16)

    outer_loop(rows // chunk, middle)


def encoder_back_kernel(
    head_size,
    groups,
    chunk,
    patches,
    key_col,
    own_row,
    norms,
    w_qkv,
    w_out,
    w_up,
    w_down,
    w_embed,
    d_table,
    qkv,
    totals,
    mixed,
    x_one,
    act,
    slope,
    sent,
    d_patches,
    g_norms,
    g_shift,
    g_qkv,
    g_out,
    g_up,
    g_down,
    g_embed,
    e_two,
    e_one,
    stage,
    stage_wide,
    sem,
):
    rows, width = patches.shape
    n = rows // groups
    tiles = width // LANES
    per_tile = LANES // head_size
    gain = [norms[k : k + 1, :].astype(F32) for k in range(4)]
    g_norms[...] = jnp.zeros_like(g_norms)
    g_shift[...] = jnp.zeros_like(g_shift)
    step = 512
    weight_sum(g_embed, d_table, sent, stage, sem)
    h_two = sent

    def middle(i):
        r = rows_of(i, chunk)
        d_emb = d_table[r, :]
        g_shift[0:1, :] += column_sum(d_emb.astype(F32))
        e = nn(d_emb, w_embed[...]).astype(BF16)
        e_two[r, :] = e
        for t in range(w_up.shape[0] // step):
            cols = slice(t * step, (t + 1) * step)
            d_act = nn(e, w_down[:, cols])
            slope[r, cols] = (d_act * slope[r, cols].astype(F32)).astype(BF16)
        d_h = nn(slope[r, :], w_up[...])
        hat, scale = unit(x_one[r, :])
        h_two[r, :] = (hat * gain[2] + gain[3]).astype(BF16)
        g_norms[2:3, :] += column_sum(d_h * hat)
        g_norms[3:4, :] += column_sum(d_h)
        d_one = e.astype(F32) + unit_back(d_h * gain[2], hat, scale)
        d_patches[r, :] = d_one
        e_one[r, :] = d_one.astype(BF16)

    outer_loop(rows // chunk, middle)
    weight_sum(g_down, e_two, act, stage_wide, sem)
    weight_sum(g_up, slope, h_two, stage, sem)
    weight_sum(g_out, e_one, mixed, stage, sem)

    def mix_back(i):
        r = rows_of(i, chunk)
        mixed[r, :] = nn(e_one[r, :], w_out[...]).astype(BF16)

    outer_loop(rows // chunk, mix_back)

    def attend_back(g):
        r = rows_of(g, n)
        bias = mask_bias(own_row[g], key_col[r, :])
        for t in range(tiles):
            cols = [slice((t + j * tiles) * LANES, (t + j * tiles + 1) * LANES) for j in range(3)]
            q, k, v = [qkv[r, col] for col in cols]
            logs = [totals[g, t * per_tile + h : t * per_tile + h + 1, :] for h in range(per_tile)]
            found = attend_tile_back(q, k, v, mixed[r, cols[0]], bias, logs, head_size)
            for j in range(3):
                act[r, cols[j]] = found[j].astype(BF16)

    outer_loop(groups, attend_back)
    h_one = h_two

    def finish(i):
        r = rows_of(i, chunk)
        d_h = nn(act[r, : 3 * width], w_qkv[...])
        hat, scale = unit(patches[r, :].astype(F32))
        h_one[r, :] = (hat * gain[0] + gain[1]).astype(BF16)
        g_norms[0:1, :] += column_sum(d_h * hat)
        g_norms[1:2, :] += column_sum(d_h)
        d_patches[r, :] += unit_back(d_h * gain[0], hat, scale)

    outer_loop(rows // chunk, finish)
    weight_sum(g_qkv, act.at[:, : 3 * width], h_one, stage, sem)


def slot_plan(peers, slot_rows):
    padded = -(-slot_rows // 16) * 16
    joined = max(1, 128 // padded)
    return padded, joined


def encoder_inputs(patches, counts):
    peers = counts.shape[0]
    width = patches.shape[1]
    slot_rows = patches.shape[0] // peers
    padded, joined = slot_plan(peers, slot_rows)
    rows, groups = peers * padded, peers // joined
    n = rows // groups
    x = jnp.pad(patches.reshape(peers, slot_rows, width), ((0, 0), (0, padded - slot_rows), (0, 0)))
    x = x.reshape(rows, width)
    row = jnp.arange(padded, dtype=jnp.int32)[None, :]
    slot = jnp.arange(peers, dtype=jnp.int32)[:, None]
    live = (row >= slot_rows - counts[:, None]) & (row < slot_rows)
    keys = jnp.where(live, slot, -1).reshape(rows, 1)
    own = jnp.broadcast_to(slot, (peers, padded)).reshape(groups, 1, n)
    return x, keys, own, padded


def encoder(patches, counts, norms, shift, weights, embed, heads):
    x, keys, own, _ = encoder_inputs(patches, counts)
    rows, width = x.shape
    groups, _, n = own.shape
    head_size = width // heads
    ff = weights[2].shape[0]
    vm = pl.BlockSpec(memory_space=pltpu.VMEM)
    shapes = [
        ((rows, weights[0].shape[0]), BF16),
        ((groups, -(-heads // 8) * 8, n), F32),
        ((rows, width), BF16),
        ((rows, width), F32),
        ((rows, ff), BF16),
        ((rows, ff), BF16),
        ((rows, width), BF16),
    ]
    shapes = [jax.ShapeDtypeStruct(s, t) for s, t in shapes]
    embedded, *stored = pl.pallas_call(
        functools.partial(encoder_kernel, head_size, groups, 2 * n),
        out_shape=[jax.ShapeDtypeStruct((rows, embed.shape[0]), BF16)] + shapes,
        in_specs=[vm] * 10,
        out_specs=[vm] * 8,
        compiler_params=pltpu.CompilerParams(vmem_limit_bytes=60 << 20),
        name="encoder",
    )(x, keys, own, norms, shift, *weights, embed)
    return embedded, (x, keys, own), stored


def encoder_back(rows_in, norms, weights, embed, d_table, stored, heads):
    x, keys, own = rows_in
    rows, width = x.shape
    groups, _, n = own.shape
    head_size = width // heads
    vm = pl.BlockSpec(memory_space=pltpu.VMEM)
    return pl.pallas_call(
        functools.partial(encoder_back_kernel, head_size, groups, 2 * n),
        out_shape=[
            jax.ShapeDtypeStruct((rows, width), F32),
            jax.ShapeDtypeStruct((8, width), F32),
            jax.ShapeDtypeStruct((8, embed.shape[0]), F32),
        ]
        + [jax.ShapeDtypeStruct(w.shape, BF16) for w in weights]
        + [jax.ShapeDtypeStruct(embed.shape, BF16)],
        in_specs=[vm] * 17,
        out_specs=[vm] * 3 + [pl.BlockSpec(memory_space=pl.ANY)] * 5,
        scratch_shapes=[pltpu.VMEM((rows, width), BF16)] * 2
        + [
            pltpu.VMEM((2, 256, width), BF16),
            pltpu.VMEM((2, LANES, weights[2].shape[0]), BF16),
            pltpu.SemaphoreType.DMA((2,)),
        ],
        compiler_params=pltpu.CompilerParams(vmem_limit_bytes=62 << 20),
        name="encoder_back",
    )(x, keys, own, norms, *weights, embed, d_table, *stored)


class Ticker:
    def __init__(self, plans, locals_):
        self.plans, self.locals_, self.moving, self.t = plans, locals_, {}, 0

    def tick(self, count=1):
        for _ in range(count):
            for stage in (3, 2, 1, 0):
                i = self.t - 2 * stage
                if 0 <= i < len(self.plans):
                    self.advance(i, stage)
            self.t += 1

    def advance(self, i, stage):
        if stage > 0:
            for copy in self.moving[i, stage - 1]:
                copy.wait_recv()
            if stage == 1:
                self.locals_[i].wait()
        self.moving[i, stage] = self.plans[i][stage]()
        for copy in self.moving[i, stage]:
            copy.start()

    def arrived(self, i):
        for copy in self.moving[i, 3]:
            copy.wait_recv()

    def drain(self):
        for copies in self.moving.values():
            for copy in copies:
                copy.wait_send()


def flat(ref):
    value = ref[...]
    return value.reshape(-1, value.shape[-1])


def spread_norms(tiles, start, count, part, out):
    width = 8 * part
    lane = lax.broadcasted_iota(jnp.int32, (LANES, width), 1)
    line = lax.broadcasted_iota(jnp.int32, (LANES, width), 0)
    for f in range(4):
        total = 0.0
        for d in range(8):
            put = jnp.where((lane == line + d * part) & (line < part), 1.0, 0.0).astype(BF16)
            rows = tiles[d // 2, d % 2, start : start + 16, f * LANES : (f + 1) * LANES]
            total = total + nn(rows, put)
        out[f * count : (f + 1) * count, :] = total[:count]


def front_kernel(entries, head_size, groups, chunk, sizes, *refs):
    n_in = len(entries)
    pieces, refs = refs[:n_in], refs[n_in:]
    patches, key_col, own_row, *refs = refs
    whole, refs = refs[:n_in], refs[n_in:]
    norms_e, norms_d, table, totals, *refs = refs
    kept_out, refs = refs[:6], refs[6:]
    kept, refs = refs[:6], refs[6:]
    qkv, mixed, x_one, act, slope, sent = kept
    loaded, refs = refs[:6], refs[6:]
    tiles_v, w_qkv, w_out, w_up, w_embed, w_down = loaded
    embedded, send_sem, recv_sem, local_sem, load_sem, keep_sem, swap_send, swap_recv, swap_local = refs
    rows, width = patches.shape
    n = rows // groups
    tiles = width // LANES
    per_tile = LANES // head_size
    z, x, y, c = place()
    d = z * 2 + x

    plans, locals_ = [], []
    for i, e in enumerate(entries):
        local, stages = gather_stages(e, i, pieces[i], whole[i], (send_sem, recv_sem), local_sem)
        plans.append(stages)
        locals_.append(local())
    for copy in locals_:
        copy.start()
    meet(z, x, y, c)
    ticker = Ticker(plans, locals_)

    def load(i):
        ticker.arrived(i)
        copy = pltpu.make_async_copy(whole[i], loaded[i], load_sem.at[i])
        copy.start()
        return copy

    keeping = []

    def keep(k):
        copy = pltpu.make_async_copy(kept[k], kept_out[k], keep_sem.at[k])
        copy.start()
        keeping.append(copy)

    ticker.tick(8)
    copies = [load(0), load(1)]
    for copy in copies:
        copy.wait()
    spread_norms(tiles_v, 0, sizes[0], sizes[1], norms_e)
    spread_norms(tiles_v, NORM_ROWS // 2, sizes[2], sizes[3], norms_d)
    gain = [norms_e[k : k + 1, :] for k in range(4)]
    add = norms_d[7:8, :]

    def start(i):
        r = rows_of(i, chunk)
        hat, _ = unit(patches[r, :].astype(F32))
        qkv[r, :] = nt((hat * gain[0] + gain[1]).astype(BF16), flat(w_qkv)).astype(BF16)

    some(0, 2, start)
    ticker.tick()
    some(2, 4, start)
    keep(0)

    def attend(g):
        r = rows_of(g, n)
        bias = mask_bias(own_row[g], key_col[r, :])
        for t in range(tiles):
            q, k, v = [qkv[r, (t + j * tiles) * LANES : (t + j * tiles + 1) * LANES] for j in range(3)]
            out, logs = attend_tile(q, k, v, bias, head_size)
            mixed[r, t * LANES : (t + 1) * LANES] = out.astype(BF16)
            for h in range(per_tile):
                totals[g, t * per_tile + h : t * per_tile + h + 1, :] = logs[h]

    some(0, groups, attend)
    keep(1)
    ticker.tick()
    copies = [load(2), load(3)]
    ticker.tick()
    for copy in copies:
        copy.wait()
    step = w_up.shape[-2] * (2 if len(w_up.shape) == 5 else 1)

    def lift(i):
        r = rows_of(i, chunk)
        one = patches[r, :].astype(F32) + nt(mixed[r, :], flat(w_out))
        x_one[r, :] = one
        hat, _ = unit(one)
        h = (hat * gain[2] + gain[3]).astype(BF16)
        for t in range(8):
            u = nt(h, w_up[t // 2, t % 2].reshape(step, width))
            a, s = gelu_pair(u)
            act[r, t * step : (t + 1) * step] = a.astype(BF16)
            slope[r, t * step : (t + 1) * step] = s.astype(BF16)

    some(0, 4, lift)
    copies = [load(4)]
    ticker.tick()
    copies.append(load(5))
    for k in (2, 3, 4):
        keep(k)
    for copy in copies:
        copy.wait()
    per_chunk = chunk // embedded.shape[1]
    for i in range(4):

        def lower(i):
            r = rows_of(i, chunk)
            two = (x_one[r, :] + nt(act[r, :], flat(w_down))).astype(BF16)
            sent[r, :] = two
            out = (nt(two, flat(w_embed)) + add).astype(BF16)
            for k in range(per_chunk):
                embedded[i * per_chunk + k] = out[k * embedded.shape[1] : (k + 1) * embedded.shape[1]]

        some(i, i + 1, lower)
        for k in range(per_chunk):
            s = i * per_chunk + k

            @pl.when(s != d)
            def _(s=s):
                send_slot(embedded, table, s, d, swap_send, swap_recv, y * 2 + c).start()

            @pl.when(s == d)
            def _(s=s):
                pltpu.make_async_copy(embedded.at[s], table.at[s], swap_local.at[0]).start()

        if i == 1:
            ticker.tick()
    keep(5)
    while ticker.t < n_in + 6:
        ticker.tick()
    for i in range(6, n_in):
        ticker.arrived(i)
    finish_swap(embedded, table, d, swap_send, swap_recv, swap_local, y * 2 + c)
    ticker.drain()
    for copy in keeping:
        copy.wait()


def send_slot(src, dst, s, d, sends, recvs, f):
    return pltpu.make_async_remote_copy(
        src_ref=src.at[s],
        dst_ref=dst.at[d],
        send_sem=sends.at[s],
        recv_sem=recvs.at[d],
        device_id=(s, f),
        device_id_type=MESH,
    )


def finish_swap(src, dst, d, sends, recvs, local, f):
    for s in range(8):

        @pl.when(s != d)
        def _(s=s):
            came = pltpu.make_async_remote_copy(
                src_ref=src.at[s],
                dst_ref=dst.at[s],
                send_sem=sends.at[s],
                recv_sem=recvs.at[s],
                device_id=(s, f),
                device_id_type=MESH,
            )
            came.wait_send()
            came.wait_recv()

    pltpu.make_async_copy(src.at[d], dst.at[d], local.at[0]).wait()


def front(entries, pieces, patches, counts, sizes, heads):
    peers = 8
    width = patches.shape[1]
    x, keys, own, padded = encoder_inputs(patches, counts)
    rows = x.shape[0]
    groups, _, n = own.shape
    head_size = width // heads
    by = {k: e for k, e in enumerate(entries)}
    wide, ff = 3 * width, 8 * entries[3].rows
    embed = 8 * entries[4].rows
    kept = [
        ((rows, wide), BF16),
        ((rows, width), BF16),
        ((rows, width), F32),
        ((rows, ff), BF16),
        ((rows, ff), BF16),
        ((rows, width), BF16),
    ]
    vm, hbm = pl.BlockSpec(memory_space=pltpu.VMEM), pl.BlockSpec(memory_space=pl.ANY)
    n_in = len(entries)
    sem = pltpu.SemaphoreType.DMA
    found = pl.pallas_call(
        functools.partial(front_kernel, entries, head_size, groups, rows // 4, sizes),
        out_shape=[jax.ShapeDtypeStruct(e.whole, BF16) for e in entries]
        + [
            jax.ShapeDtypeStruct((4 * sizes[0], 8 * sizes[1]), F32),
            jax.ShapeDtypeStruct((4 * sizes[2], 8 * sizes[3]), F32),
            jax.ShapeDtypeStruct((peers, padded, embed), BF16),
            jax.ShapeDtypeStruct((groups, -(-heads // 8) * 8, n), F32),
        ]
        + [jax.ShapeDtypeStruct(s, t) for s, t in kept],
        in_specs=[hbm] * n_in + [vm] * 3,
        out_specs=[hbm] * n_in + [vm, vm, hbm, vm] + [hbm] * 6,
        scratch_shapes=[pltpu.VMEM(s, t) for s, t in kept]
        + [pltpu.VMEM(by[k].whole, BF16) for k in range(6)]
        + [
            pltpu.VMEM((peers, padded, embed), BF16),
            sem((n_in, 10)),
            sem((n_in, 10)),
            sem((n_in,)),
            sem((6,)),
            sem((6,)),
            sem((8,)),
            sem((8,)),
            sem((1,)),
        ],
        compiler_params=pltpu.CompilerParams(
            collective_id=0, has_side_effects=True, vmem_limit_bytes=60 << 20
        ),
        name="front",
    )(*pieces, x, keys, own)
    whole, (norms_e, norms_d, table, totals) = found[:n_in], found[n_in : n_in + 4]
    qkv, mixed, x_one, act, slope, sent = found[n_in + 4 :]
    return whole, norms_e, norms_d, table, (x, keys, own), [qkv, totals, mixed, x_one, act, slope, sent]


class Reducer:
    def __init__(self, plans):
        self.plans, self.stage, self.moving, self.waits = plans, {}, [], {}

    def start(self, i, copies, waits):
        for copy in copies:
            copy.start()
        self.waits[i] = waits
        self.moving += waits

    def begin(self, i):
        local, stages = self.plans[i]
        copies, self.local_waits = local()
        for copy in copies:
            copy.start()
        self.waits[i, 0] = self.local_waits
        self.start(i, *stages[0][0]())
        self.stage[i] = 0

    def step(self, i):
        k = self.stage[i]
        if k == 4:
            return
        _, stages = self.plans[i]
        for copy in self.waits[i]:
            copy.wait_recv()
        if k == 0:
            for copy in self.waits[i, 0]:
                copy.wait()
        stages[k][1]()
        if k < 3:
            self.start(i, *stages[k + 1][0]())
        self.stage[i] = k + 1

    def finish(self, i):
        while self.stage[i] < 4:
            self.step(i)

    def drain(self):
        for copy in self.moving:
            copy.wait_send()


def meet(z, x, y, c):
    d = z * 2 + x
    barrier = pltpu.get_barrier_semaphore()
    peers = [(lax.rem(d + k, 8), y * 2 + c) for k in range(1, 8)]
    peers += [at(z, x, 1 - y, c), at(z, x, y, 1 - c)]
    for peer in peers:
        pl.semaphore_signal(barrier, inc=1, device_id=peer, device_id_type=MESH)
    pl.semaphore_wait(barrier, len(peers))


def gather_norms(g, start, count, part, tiles):
    width = 8 * part
    lane = lax.broadcasted_iota(jnp.int32, (width, LANES), 1)
    line = lax.broadcasted_iota(jnp.int32, (width, LANES), 0)
    rows = g.astype(BF16)
    for d in range(8):
        put = jnp.where((line == lane + d * part) & (lane < part), 1.0, 0.0).astype(BF16)
        cut = nn(rows, put).astype(BF16)
        for f in range(4):
            tiles[d // 2, d % 2, start : start + count, f * LANES : (f + 1) * LANES] = cut[
                f * count : (f + 1) * count
            ]


def rear_kernel(parts, places, n_out, head_size, groups, chunk, sizes, *refs):
    patches, key_col, own_row, norms, g_dec, g_dec_qkv, *refs = refs
    weights, refs = refs[:5], refs[5:]
    d_table, *refs = refs
    stored, refs = refs[:7], refs[7:]
    d_patches, *refs = refs
    g_embed, g_down, g_up, g_out, g_qkv, *refs = refs
    outs, refs = refs[:n_out], refs[n_out:]
    up_v, down_v, embed_v, act, slope, mixed, sent, e_two, e_one, d_emb, totals, small, *refs = refs
    stage, stage_wide, sem, g_norms, g_shift, *refs = refs
    bufs, refs = refs[: 7 * len(parts)], refs[7 * len(parts) :]
    send_sem, recv_sem, local_sem, load_sem = refs
    w_qkv, w_out, w_up, w_down, w_embed = weights
    s_qkv, s_totals, s_mixed, s_one, s_act, s_slope, s_sent = stored
    rows, width = patches.shape
    n = rows // groups
    tiles = width // LANES
    per_tile = LANES // head_size
    wide = 3 * width
    z, x, y, c = place()
    loads = {}

    def load(k, src, dst):
        loads[k] = pltpu.make_async_copy(src, dst, load_sem.at[k])
        loads[k].start()

    load(0, w_embed, embed_v)
    load(1, d_table, d_emb)
    load(2, s_act, act)
    load(3, s_sent, sent)
    load(4, w_down, down_v)
    load(5, s_slope, slope)
    load(6, w_up, up_v)
    load(7, s_one, d_patches)
    load(8, s_mixed, mixed)
    load(9, s_totals, totals)
    small[...] = jnp.zeros_like(small)
    g_norms[...] = jnp.zeros_like(g_norms)
    g_shift[...] = jnp.zeros_like(g_shift)
    meet(z, x, y, c)
    sources = {"dq": g_dec_qkv, "do": g_down, "em": g_embed, "up": g_up, "ou": g_out, "qk": g_qkv, "sm": small}
    plans = {}
    for i, (name, e, row) in enumerate(parts):
        out, first = outs[places[name[:2]][0]], places[name[:2]][1]
        plans[name] = reduce_stages(
            e, i, sources[name[:2]], out, bufs[7 * i : 7 * i + 7], (send_sem, recv_sem), local_sem, row, first
        )
    reducer = Reducer(plans)
    gain = [norms[k : k + 1, :] for k in range(4)]
    h_two, h_one = sent, e_two
    step = 512

    def enter():
        loads[0].wait()
        loads[1].wait()
        some(0, rows // chunk, enter_rows)
        loads[2].wait()

    def enter_rows(i):
        r = rows_of(i, chunk)
        g_shift[0:1, :] += column_sum(d_emb[r, :].astype(F32))
        e_two[r, :] = nn(d_emb[r, :], embed_v[...]).astype(BF16)

    def sum_down():
        weight_sum(g_down, e_two, act, stage_wide, sem)

    def sum_embed():
        loads[3].wait()
        weight_sum(g_embed, d_emb, sent, stage, sem)
        for k in range(4, 8):
            loads[k].wait()

    def middle_rows(i):
        r = rows_of(i, chunk)
        e = e_two[r, :]
        for t in range(slope.shape[1] // step):
            cols = slice(t * step, (t + 1) * step)
            d_act = nn(e, down_v[:, cols])
            slope[r, cols] = (d_act * slope[r, cols].astype(F32)).astype(BF16)
        d_h = nn(slope[r, :], up_v[...])
        hat, scale = unit(d_patches[r, :])
        h_two[r, :] = (hat * gain[2] + gain[3]).astype(BF16)
        g_norms[2:3, :] += column_sum(d_h * hat)
        g_norms[3:4, :] += column_sum(d_h)
        d_one = e.astype(F32) + unit_back(d_h * gain[2], hat, scale)
        d_patches[r, :] = d_one
        e_one[r, :] = d_one.astype(BF16)

    def middle(i):
        some(i, i + 1, middle_rows)

    def sum_up():
        load(10, w_qkv, up_v.at[:wide, :])
        load(11, w_out, up_v.at[wide:, :])
        weight_sum(g_up, slope, h_two, stage, sem)
        load(12, s_qkv, slope.at[:, :wide])

    def sum_out():
        loads[8].wait()
        loads[9].wait()
        weight_sum(g_out, e_one, mixed, stage, sem)

    def mix_rows(i):
        r = rows_of(i, chunk)
        mixed[r, :] = nn(e_one[r, :], up_v[wide:, :]).astype(BF16)
        hat, _ = unit(patches[r, :].astype(F32))
        h_one[r, :] = (hat * gain[0] + gain[1]).astype(BF16)

    def mix():
        loads[11].wait()
        some(0, rows // chunk, mix_rows)
        loads[12].wait()

    def attend_back(g):
        r = rows_of(g, n)
        bias = mask_bias(own_row[g], key_col[r, :])
        for t in range(tiles):
            cols = [slice((t + j * tiles) * LANES, (t + j * tiles + 1) * LANES) for j in range(3)]
            q, k, v = [slope[r, col] for col in cols]
            logs = [totals[g, t * per_tile + h : t * per_tile + h + 1, :] for h in range(per_tile)]
            found = attend_tile_back(q, k, v, mixed[r, cols[0]], bias, logs, head_size)
            for j in range(3):
                act[r, cols[j]] = found[j].astype(BF16)

    def attend(i):
        some(i * groups // 4, (i + 1) * groups // 4, attend_back)

    def sum_qkv():
        weight_sum(g_qkv, act.at[:, :wide], h_one, stage, sem)
        loads[10].wait()

    def finish_rows(i):
        r = rows_of(i, chunk)
        d_h = nn(act[r, :wide], up_v[:wide, :])
        hat, scale = unit(patches[r, :].astype(F32))
        g_norms[0:1, :] += column_sum(d_h * hat)
        g_norms[1:2, :] += column_sum(d_h)
        d_patches[r, :] += unit_back(d_h * gain[0], hat, scale)

    def finish(i):
        some(i, i + 1, finish_rows)

    def norms_of_all():
        gather_norms(g_norms[0:4, :], 0, sizes[0], sizes[1], small)

    def norms_of_decoder():
        line = lax.broadcasted_iota(jnp.int32, g_dec.shape, 0)
        joined = jnp.where(line == 7, g_shift[0:1, :], g_dec[...])
        gather_norms(joined, NORM_ROWS // 2, sizes[2], sizes[3], small)

    blocks = {
        "enter": enter,
        "down": sum_down,
        "embed": sum_embed,
        "up": sum_up,
        "out": sum_out,
        "mix": mix,
        "qkv": sum_qkv,
        "norms": norms_of_all,
        "dnorms": norms_of_decoder,
    }
    for i in range(4):
        blocks["mid" + str(i)] = functools.partial(middle, i)
        blocks["att" + str(i)] = functools.partial(attend, i)
        blocks["fin" + str(i)] = functools.partial(finish, i)
    for name, actions in REAR_PLAN:
        if name:
            blocks[name]()
        for action in actions:
            if action[0] == "+":
                reducer.begin(action[1:])
            else:
                reducer.step(action)
    for name, _, _ in parts:
        reducer.finish(name)
    reducer.drain()


REAR_SPLIT = {"qk": 3}
REAR_PLAN = (
    ("", ("+dq",)),
    ("enter", ()),
    ("down", ("+do", "dq")),
    ("dnorms", ()),
    ("embed", ("+em",)),
    ("mid0", ()),
    ("mid1", ("dq", "em", "do")),
    ("mid2", ()),
    ("mid3", ("dq",)),
    ("up", ("+up", "em", "dq")),
    ("out", ("+ou",)),
    ("mix", ()),
    ("att0", ("ou", "do", "up", "em")),
    ("att1", ()),
    ("att2", ("em", "ou")),
    ("att3", ("do",)),
    ("qkv", ("+qk0", "+qk1", "+qk2", "up")),
    ("fin0", ()),
    ("fin1", ("ou",)),
    ("fin2", ("qk0",)),
    ("fin3", ("qk1", "qk2")),
    ("norms", ("+sm", "up", "do", "sm", "qk0", "sm", "qk1", "qk0", "qk2", "sm", "qk1", "qk2", "ou", "up")),
)


def rear(rows_in, norms, g_dec, g_dec_qkv, weights, embed, d_table, stored, sizes):
    x, keys, own = rows_in
    rows, width = x.shape
    groups, _, n = own.shape
    head_size = width // HEADS_E
    ff = weights[2].shape[0]
    first = (8 * g_dec_qkv.shape[2], g_dec_qkv.shape[3])
    names = ("dq", "do", "em", "up", "ou", "qk", "sm")
    shapes = [first, weights[3].shape, embed.shape, weights[2].shape, weights[1].shape, weights[0].shape]
    entries = [entry_of(s[0] // 8, s[1]) for s in shapes] + [entry_of(NORM_ROWS, 512)]
    places, sums, high = {}, [], 0
    for name, e in zip(names, entries):
        if e.by_core:
            places[name] = (0, high)
            high += e.part
    sums.append((high, entries[5].q))
    for name, e in zip(names, entries):
        if not e.by_core:
            places[name] = (len(sums), 0)
            sums.append((e.part, e.q))
    parts = []
    for name, e in zip(names, entries):
        count = REAR_SPLIT.get(name, 1)
        for k in range(count):
            cut = dataclasses.replace(e, share=count)
            parts.append((name + (str(k) if count > 1 else ""), cut, k * cut.part))
    vm, hbm = pl.BlockSpec(memory_space=pltpu.VMEM), pl.BlockSpec(memory_space=pl.ANY)
    sem = pltpu.SemaphoreType.DMA
    n_in = len(parts)
    totals = stored[1]
    found = pl.pallas_call(
        functools.partial(rear_kernel, parts, places, len(sums), head_size, groups, rows // 4, sizes),
        out_shape=[jax.ShapeDtypeStruct((rows, width), F32)]
        + [jax.ShapeDtypeStruct(s, BF16) for s in (shapes[2], shapes[1], *shapes[3:])]
        + [jax.ShapeDtypeStruct(s, F32) for s in sums],
        in_specs=[vm] * 5 + [hbm] * 14,
        out_specs=[vm] + [hbm] * 5 + [vm] * len(sums),
        scratch_shapes=[
            pltpu.VMEM(weights[2].shape, BF16),
            pltpu.VMEM(weights[3].shape, BF16),
            pltpu.VMEM(embed.shape, BF16),
            pltpu.VMEM((rows, ff), BF16),
            pltpu.VMEM((rows, ff), BF16),
            pltpu.VMEM((rows, width), BF16),
            pltpu.VMEM((rows, width), BF16),
            pltpu.VMEM((rows, width), BF16),
            pltpu.VMEM((rows, width), BF16),
            pltpu.VMEM(d_table.shape, BF16),
            pltpu.VMEM(totals.shape, F32),
            pltpu.VMEM(entries[-1].whole, BF16),
            pltpu.VMEM((2, 256, width), BF16),
            pltpu.VMEM((2, LANES, ff), BF16),
            sem((2,)),
            pltpu.VMEM((8, width), F32),
            pltpu.VMEM((8, embed.shape[0]), F32),
        ]
        + [pltpu.VMEM(shape, BF16) for _, e, _ in parts for shape in reduce_buffers(e)]
        + [sem((n_in, 9)), sem((n_in, 9)), sem((n_in,)), sem((13,))],
        compiler_params=pltpu.CompilerParams(
            collective_id=2, has_side_effects=True, vmem_limit_bytes=63 << 20
        ),
        name="rear",
    )(x, keys, own, norms, g_dec, g_dec_qkv, *weights, embed, d_table, *stored)
    return found[0], found[6:], places


def per_device(
    staged,
    patches,
    send_counts,
    dec_segment,
    source_index,
    cotangent,
    enc_norms,
    enc_qkv,
    enc_out,
    enc_up,
    enc_down,
    dec_norms,
    dec_embed,
    dec_qkv,
    dec_out,
    dec_up,
    dec_down,
):
    peers = lax.axis_size("dp")
    width = patches.shape[1]
    slot_rows = patches.shape[0] // peers
    counts = send_counts.reshape(peers)
    masters = (enc_qkv, enc_out, enc_up, dec_embed, enc_down, dec_qkv, dec_out, dec_up, dec_down)
    padded = slot_plan(peers, slot_rows)[0]

    def swap(table):
        slots = table.reshape(peers, padded, table.shape[1])
        return lax.all_to_all(slots, "dp", split_axis=0, concat_axis=0, tiled=True).reshape(table.shape)

    if staged:
        entries, pieces = staged_pieces(enc_norms, dec_norms, masters)
        sizes = (*enc_norms.shape, *dec_norms.shape)
        whole, norms_e, norms_d, table, enc_inputs, stored = front(
            entries, pieces, patches, counts, sizes, HEADS_E
        )
        whole = [w.reshape(-1, w.shape[-1]) for w in whole[1:]]
        table = table.reshape(-1, table.shape[-1])
    else:
        norms_e, norms_d, whole = gather_masters(enc_norms, dec_norms, masters)
    enc_weights, embed, dec_weights = [*whole[:3], whole[4]], whole[3], whole[5:]
    if not staged:
        embedded, enc_inputs, stored = encoder(
            patches, counts, norms_e, norms_d, enc_weights, embed, HEADS_E
        )
        table = swap(embedded)
    place_of = source_index // slot_rows * padded + source_index % slot_rows
    index = jnp.where(source_index >= 0, place_of, -1)
    if staged:
        decoded, d_table, g_dec_norms, g_qkv, _, _, _, s_down, s_up, s_out = decoder(
            True, table, index, dec_segment, cotangent, norms_d, dec_weights, HEADS_D
        )
        e = entry_of(g_qkv.shape[0] // 8, g_qkv.shape[1])
        d_patches, sums, places = rear(
            enc_inputs,
            norms_e,
            g_dec_norms,
            g_qkv.reshape(e.whole),
            enc_weights,
            embed,
            d_table.reshape(table.shape),
            stored,
            sizes,
        )
        small = sums[places["sm"][0]]
        half = NORM_ROWS // 2
        s_enc_norms = small[: sizes[0], : sizes[1]]
        s_dec_norms = small[half : half + sizes[2], : sizes[3]]
        halves = pieces_to_halves(sums[0])
        e_qkv, e_out, e_up, s_embed = [
            own_block(halves, places[name][1], master)
            for name, master in (("qk", enc_qkv), ("ou", enc_out), ("up", enc_up), ("em", dec_embed))
        ]
        e_down, s_qkv = sums[places["do"][0]].T, sums[places["dq"][0]].T
        sums = [e_qkv, e_out, e_up, e_down, s_embed, s_qkv, s_out.T, s_up.T, s_down.T]
    else:
        decoded, d_table, g_dec_norms, *dec_grads = decoder(
            False, table, index, dec_segment, cotangent, norms_d, dec_weights, HEADS_D
        )
        d_patches, g_enc_norms, g_shift, *enc_grads = encoder_back(
            enc_inputs,
            norms_e,
            enc_weights,
            embed,
            swap(d_table.reshape(table.shape)),
            stored,
            HEADS_E,
        )
        g_dec_norms = jnp.concatenate([g_dec_norms[:7], g_shift[:1]], axis=0)
        s_enc_norms, s_dec_norms, sums = reduce_masters(
            g_enc_norms[:4], g_dec_norms, [*enc_grads, *dec_grads]
        )
    d_patches = d_patches.reshape(peers, padded, width)[:, :slot_rows]
    return (
        decoded,
        d_patches.reshape(-1, width),
        s_enc_norms,
        *sums[:4],
        s_dec_norms,
        *sums[4:],
    )


def solution(mesh):
    placed = (
        P(("dp", "fsdp"), None),
        P(("dp", "fsdp"), None),
        P(("dp", "fsdp"), None),
        P(("dp", "fsdp"), None),
        P(("dp", "fsdp"), None, None),
        P("fsdp", "dp"),
        P("fsdp", "dp"),
        P("fsdp", "dp"),
        P("fsdp", "dp"),
        P("fsdp", "dp"),
        P("fsdp", "dp"),
        P("fsdp", "dp"),
        P("fsdp", "dp"),
        P("fsdp", "dp"),
        P("fsdp", "dp"),
        P("fsdp", "dp"),
    )
    staged = (mesh.shape["dp"], mesh.shape["fsdp"]) == (8, 4)
    return jax.shard_map(
        functools.partial(per_device, staged),
        mesh=mesh,
        in_specs=placed,
        out_specs=(
            P(("dp", "fsdp"), None, None),
            P(("dp", "fsdp"), None),
            P("fsdp", "dp"),
            P("fsdp", "dp"),
            P("fsdp", "dp"),
            P("fsdp", "dp"),
            P("fsdp", "dp"),
            P("fsdp", "dp"),
            P("fsdp", "dp"),
            P("fsdp", "dp"),
            P("fsdp", "dp"),
            P("fsdp", "dp"),
            P("fsdp", "dp"),
        ),
        check_vma=False,
    )
```

```python
import dataclasses
import functools

import jax
import jax.numpy as jnp
from jax import lax
from jax.experimental import pallas as pl
from jax.experimental.pallas import tpu as pltpu
from jax.sharding import PartitionSpec as P

HEADS_E = 12
HEADS_D = 16


EPSILON = 1e-06
NEGATIVE = -1000000000.0
LANES = 128
MESH = pl.DeviceIdType.MESH
BF16 = jnp.bfloat16
F32 = jnp.float32


def in_blocks(value, dim, length):
    dims = value.shape
    pieces = value.reshape(*dims[:dim], length, dims[dim] // length, *dims[dim + 1 :])
    return jnp.moveaxis(pieces, dim, 0)


def sum_at_owner(value, axis, dim):
    length = lax.axis_size(axis)
    pieces = lax.all_to_all(in_blocks(value, dim, length), axis, 0, 0, tiled=True)
    return jnp.sum(pieces.astype(jnp.float32), axis=0)


@dataclasses.dataclass(frozen=True)
class Entry:
    rows: int
    width: int
    by_core: bool
    share: int = 1

    @property
    def q(self):
        return self.width // 2 if self.by_core else self.width // 4

    @property
    def block(self):
        return self.rows // 2 if self.by_core else self.rows

    @property
    def part(self):
        return self.block // self.share

    @property
    def whole(self):
        if self.by_core:
            return (4, 2, 2, self.part, self.width)
        return (4, 2, self.part, self.width)

    @property
    def cut(self):
        return -(-self.part // 32) * 16


def entry_of(rows, width):
    return Entry(rows, width, (width // 4) % 128 != 0)


def region(e, ref, zs, xs, rows, y, c):
    if e.by_core:
        return ref.at[zs, xs, c, rows, pl.ds(pl.multiple_of(y * e.q, 128), e.q)]
    return ref.at[zs, xs, rows, pl.ds(pl.multiple_of((2 * y + c) * e.q, 128), e.q)]


def region_pair(e, ref, zs, xs, rows, c):
    if e.by_core:
        return [ref.at[zs, xs, c, rows, :]]
    return [region(e, ref, zs, xs, rows, y, c) for y in range(2)]


def place():
    d, s = lax.axis_index("dp"), lax.axis_index("fsdp")
    return d // 2, lax.rem(d, 2), s // 2, lax.rem(s, 2)


def at(z, x, y, c):
    return (z * 2 + x, y * 2 + c)


def send(src, dst, sems, i, k, peer):
    return pltpu.make_async_remote_copy(
        src_ref=src,
        dst_ref=dst,
        send_sem=sems[0].at[i, k],
        recv_sem=sems[1].at[i, k],
        device_id=peer,
        device_id_type=MESH,
    )


ALL = slice(None)


def gather_stages(e, i, piece, out, sems, local_sem, z_second):
    z, x, y, c = place()
    top, bottom = slice(0, e.cut), slice(e.cut, e.part)

    def first():
        here = region(e, out, z, x, ALL, y, c)
        return [
            send(piece, here, sems, i, k - 1, at(lax.rem(z + k, 4), x, y, c)) for k in (1, 2, 3)
        ]

    def local():
        return pltpu.make_async_copy(piece, region(e, out, z, x, ALL, y, c), local_sem.at[i])

    def second():
        a = region(e, out, ALL, x, top, y, c)
        b = region(e, out, ALL, x, bottom, y, c)
        return [
            send(a, a, sems, i, 3, at(z, 1 - x, y, c)),
            send(b, b, sems, i, 4, at(z, x, 1 - y, c)),
        ]

    def first_xy():
        a, b = piece.at[top], piece.at[bottom]
        return [
            send(a, region(e, out, z, x, top, y, c), sems, i, 0, at(z, 1 - x, y, c)),
            send(b, region(e, out, z, x, bottom, y, c), sems, i, 1, at(z, x, 1 - y, c)),
        ]

    def second_z():
        blocks = [region(e, out, z, ALL, top, y, c)] + region_pair(e, out, z, x, bottom, c)
        found = []
        for k in (1, 2, 3):
            for j, b in enumerate(blocks):
                found.append(send(b, b, sems, i, 4 + 3 * k + j, at(lax.rem(z + k, 4), x, y, c)))
        return found

    def third():
        a = region(e, out, ALL, ALL, top, y, c)
        found = [send(a, a, sems, i, 4 if z_second else 5, at(z, x, 1 - y, c))]
        for k, b in enumerate(region_pair(e, out, ALL, x, bottom, c)):
            found.append(send(b, b, sems, i, (2 if z_second else 6) + k, at(z, 1 - x, y, c)))
        return found

    def fourth():
        return [
            send(b, b, sems, i, (5 if z_second else 8) + k, at(z, x, y, 1 - c))
            for k, b in enumerate(region_pair(e, out, ALL, ALL, ALL, c))
        ]

    if z_second:
        return local, [first_xy, second_z, third, fourth]
    return local, [first, second, third, fourth]


def reduce_stages(e, i, grad, out, buf, sems, local_sem, row=0, place_row=0):
    z, x, y, c = place()
    acc, r4, r3a, r3b, r2a, r2b, r1 = buf
    q, cut, part = e.q, e.cut, e.part
    top, bottom = slice(0, cut), slice(cut, part)

    def lanes(y):
        return pl.ds(pl.multiple_of(y * q, 128), q)

    def share(core, ref):
        if len(grad.shape) > 2:
            into = [ref] if e.by_core else [ref.at[:, :, :, pl.ds(k * q, q)] for k in range(2)]
            return list(zip(region_pair(e, grad, ALL, ALL, slice(row, row + part), core), into))
        found = []
        for b in range(8):
            to = ref.at[b // 2, b % 2]
            if e.by_core:
                first = pl.multiple_of((2 * b + core) * e.block + row, 16)
                found.append((grad.at[pl.ds(first, part), :], to))
                continue
            for k in range(2):
                cols = pl.ds(pl.multiple_of((2 * k + core) * q, 128), q)
                found.append((grad.at[pl.ds(b * e.block + row, part), cols], to.at[:, pl.ds(k * q, q)]))
        return found

    def local():
        copies = [pltpu.make_async_copy(src, dst, local_sem.at[i]) for src, dst in share(c, acc)]
        return copies, [pltpu.make_async_copy(acc, acc, local_sem.at[i])]

    def first():
        peer = at(z, x, y, 1 - c)
        copies = [send(src, dst, sems, i, 0, peer) for src, dst in share(1 - c, r4)]
        return copies, [send(r4, r4, sems, i, 0, peer)]

    def add_first():
        def step(k, carry):
            a, b = k // 2, lax.rem(k, 2)
            acc[a, b] = (acc[a, b].astype(F32) + r4[a, b].astype(F32)).astype(BF16)
            return carry

        lax.fori_loop(0, 8, step, 0)

    def second():
        found = [
            send(acc.at[:, :, top, lanes(1 - y)], r3a, sems, i, 2, at(z, x, 1 - y, c)),
            send(acc.at[:, 1 - x, bottom, :], r3b, sems, i, 3, at(z, 1 - x, y, c)),
        ]
        return found, found

    def add_second():
        def step(k, carry):
            for b in range(2):
                acc[k, b, top, lanes(y)] = (
                    acc[k, b, top, lanes(y)].astype(F32) + r3a[k, b].astype(F32)
                ).astype(BF16)
            acc[k, x, bottom, :] = (
                acc[k, x, bottom, :].astype(F32) + r3b[k].astype(F32)
            ).astype(BF16)
            return carry

        lax.fori_loop(0, 4, step, 0)

    def third():
        found = [
            send(acc.at[:, 1 - x, top, lanes(y)], r2a, sems, i, 4, at(z, 1 - x, y, c)),
            send(acc.at[:, x, bottom, lanes(1 - y)], r2b, sems, i, 5, at(z, x, 1 - y, c)),
        ]
        return found, found

    def add_third():
        def step(k, carry):
            acc[k, x, top, lanes(y)] = (
                acc[k, x, top, lanes(y)].astype(F32) + r2a[k].astype(F32)
            ).astype(BF16)
            acc[k, x, bottom, lanes(y)] = (
                acc[k, x, bottom, lanes(y)].astype(F32) + r2b[k].astype(F32)
            ).astype(BF16)
            return carry

        lax.fori_loop(0, 4, step, 0)

    def fourth():
        found = []
        for k in (1, 2, 3):
            there = lax.rem(z + k, 4)
            found.append(
                send(acc.at[there, x, :, lanes(y)], r1.at[k - 1], sems, i, 5 + k, at(there, x, y, c))
            )
        return found, found

    def add_fourth():
        total = acc[z, x, :, lanes(y)].astype(F32)
        for k in range(3):
            total = total + r1[k].astype(F32)
        out[place_row + row : place_row + row + part, :] = total

    return local, [(first, add_first), (second, add_second), (third, add_third), (fourth, add_fourth)]


def reduce_buffers(e):
    return [
        (4, 2, e.part, 2 * e.q),
        (4, 2, e.part, 2 * e.q),
        (4, 2, e.cut, e.q),
        (4, e.part - e.cut, 2 * e.q),
        (4, e.cut, e.q),
        (4, e.part - e.cut, e.q),
        (3, e.part, e.q),
    ]


CORE_SWAP = [(0, 1), (1, 0), (2, 3), (3, 2)]
NORM_ROWS = 32


def halves_to_pieces(blocks):
    c = lax.rem(lax.axis_index("fsdp"), 2)
    both = jnp.concatenate([b.reshape(2, b.shape[0] // 2, b.shape[1]) for b in blocks], axis=1)
    mine = lax.dynamic_index_in_dim(both, c, 0, keepdims=False)
    other = lax.dynamic_index_in_dim(both, 1 - c, 0, keepdims=False)
    came = lax.ppermute(other, "fsdp", CORE_SWAP)
    left, right = jnp.where(c == 0, mine, came), jnp.where(c == 0, came, mine)
    return jnp.concatenate([left, right], axis=1)


def pieces_to_halves(whole):
    c = lax.rem(lax.axis_index("fsdp"), 2)
    q = whole.shape[1] // 2
    left, right = whole[:, :q], whole[:, q:]
    mine, other = jnp.where(c == 0, left, right), jnp.where(c == 0, right, left)
    came = lax.ppermute(other, "fsdp", CORE_SWAP)
    return jnp.where(c == 0, mine, came), jnp.where(c == 0, came, mine)


def gather_masters(enc_norms, dec_norms, weights):
    whole = []
    for w in weights:
        tall = lax.all_gather(w.astype(BF16).T, "dp", axis=0, tiled=True)
        whole.append(lax.all_gather(tall, "fsdp", axis=1, tiled=True))
    norms = []
    for rows in (enc_norms, dec_norms):
        wide = lax.all_gather(rows.astype(BF16), "dp", axis=1, tiled=True)
        norms.append(lax.all_gather(wide, "fsdp", axis=0, tiled=True))
    return norms[0], norms[1], whole


def staged_pieces(enc_norms, dec_norms, weights):
    blocks = [w.astype(BF16).T for w in weights]
    entries = [entry_of(b.shape[0], 4 * b.shape[1]) for b in blocks]
    pieces = list(blocks)
    cores = [k for k, e in enumerate(entries) if e.by_core]
    joined = halves_to_pieces([blocks[k] for k in cores])
    start = 0
    for k in cores:
        pieces[k] = lax.slice_in_dim(joined, start, start + entries[k].part, axis=0)
        start += entries[k].part
    small = jnp.zeros((NORM_ROWS, 128), BF16)
    small = small.at[: enc_norms.shape[0], : enc_norms.shape[1]].set(enc_norms.astype(BF16))
    half = NORM_ROWS // 2
    small = small.at[half : half + dec_norms.shape[0], : dec_norms.shape[1]].set(
        dec_norms.astype(BF16)
    )
    entries = [entry_of(NORM_ROWS, 512)] + entries
    return entries, [small] + pieces


def reduce_masters(g_enc_norms, g_dec_norms, grads):
    def owner(value, rows, lanes):
        part = lax.psum_scatter(value.astype(BF16), "fsdp", scatter_dimension=lanes, tiled=True)
        return sum_at_owner(part, "dp", rows)

    return (
        owner(g_enc_norms, 1, 0),
        owner(g_dec_norms, 1, 0),
        [owner(g, 0, 1).T for g in grads],
    )


def own_block(halves, first, master):
    rows = master.shape[1] // 2
    return jnp.concatenate([h[first : first + rows] for h in halves], axis=0).T


def nn(a, b):
    return lax.dot_general(a, b, (((1,), (0,)), ((), ())), preferred_element_type=F32)


def nt(a, b):
    return lax.dot_general(a, b, (((1,), (1,)), ((), ())), preferred_element_type=F32)


def tn(a, b):
    return lax.dot_general(a, b, (((0,), (0,)), ((), ())), preferred_element_type=F32)


def unit(values):
    centred = values - jnp.mean(values, axis=-1, keepdims=True)
    scale = lax.rsqrt(jnp.mean(centred * centred, axis=-1, keepdims=True) + EPSILON)
    return centred * scale, scale


def unit_back(d_hat, hat, scale):
    along = jnp.mean(d_hat * hat, axis=-1, keepdims=True)
    return scale * (d_hat - jnp.mean(d_hat, axis=-1, keepdims=True) - hat * along)


def column_sum(values):
    return jnp.sum(values, axis=0, keepdims=True)


def gelu_pair(u):
    phi = 0.5 + 0.5 * lax.erf(u * 0.7071067811865476)
    return u * phi, phi + u * (0.3989422804014327 * jnp.exp(-0.5 * u * u))


def head_lanes(shape, head_size, h):
    return lax.broadcasted_iota(jnp.int32, shape, 1) // head_size == h


def pick(values, head_size, h):
    return jnp.where(head_lanes(values.shape, head_size, h), values, jnp.zeros_like(values))


LOG2_E = 1.4426950408889634


def attend_tile(q, k, v, bias, head_size):
    v_t = v.astype(F32).T.astype(BF16)
    mixed, totals = [], []
    for h in range(LANES // head_size):
        scores = nt(pick(k, head_size, h), q) * (head_size**-0.5 * LOG2_E) + bias
        top = jnp.max(scores, axis=0, keepdims=True)
        weight = jnp.exp2(scores - top)
        total = jnp.sum(weight, axis=0, keepdims=True)
        part = nn(v_t[h * head_size : (h + 1) * head_size], weight.astype(BF16))
        mixed.append(part * (1.0 / total))
        totals.append(top + jnp.log(total) * LOG2_E)
    return jnp.concatenate(mixed, axis=0).T, totals


def attend_tile_back(q, k, v, d_mixed, bias, totals, head_size):
    k_t = k.astype(F32).T.astype(BF16)
    d_q, d_k, d_v = [], 0.0, 0.0
    for h in range(LANES // head_size):
        scores = nt(pick(k, head_size, h), q) * (head_size**-0.5 * LOG2_E) + bias
        prob = jnp.exp2(scores - totals[h])
        d_prob = nt(pick(v, head_size, h), d_mixed)
        centre = jnp.sum(d_prob * prob, axis=0, keepdims=True)
        d_score = (prob * (d_prob - centre)).astype(BF16)
        d_v = d_v + nn(prob.astype(BF16), pick(d_mixed, head_size, h))
        d_k = d_k + nn(d_score, pick(q, head_size, h))
        d_q.append(nn(k_t[h * head_size : (h + 1) * head_size], d_score))
    d_q = jnp.concatenate(d_q, axis=0).T
    return d_q * head_size**-0.5, d_k * head_size**-0.5, d_v


def lane_tile(t):
    return pl.ds(pl.multiple_of(t * LANES, LANES), LANES)


def rows_of(i, n):
    return pl.ds(pl.multiple_of(i * n, 16), n)


def mask_bias(own, keys):
    return jnp.where(keys == own, 0.0, NEGATIVE).astype(F32)


def outer_loop(count, body):
    def step(i, carry):
        body(i)
        return carry

    lax.fori_loop(0, count, step, 0)


def weight_sum(dst, left, right, stage, sem):
    _, tile, width = stage.shape
    count = left.shape[1] // tile

    def off(t):
        slot = lax.rem(t, 2)
        rows = pl.ds(pl.multiple_of(t * tile, LANES), tile)
        return pltpu.make_async_copy(stage.at[slot], dst.at[rows, :], sem.at[slot])

    def one(t):
        @pl.when(t >= 2)
        def _():
            off(t - 2).wait()

        cols = pl.ds(pl.multiple_of(t * tile, LANES), tile)
        stage[lax.rem(t, 2)] = tn(left[:, cols], right[...]).astype(BF16)
        off(t).start()

    outer_loop(count, one)
    for t in range(max(0, count - 2), count):
        off(t).wait()


def decoder_body(
    hooks,
    head_size,
    chunk,
    table,
    marks_col,
    marks_row,
    cot,
    norms,
    w_qkv,
    w_out,
    w_up,
    w_down,
    decoded,
    d_table,
    g_norms,
    g_qkv,
    g_out,
    g_up,
    g_down,
    x,
    h_one,
    qkv,
    mixed,
    totals,
    h_two,
    act,
    slope,
    d_up,
    e_two,
    e_one,
    bias,
    d_x,
    stage,
    stage_wide,
    sem,
):
    groups, real, width = cot.shape
    n = d_x.shape[1]
    rows = groups * n
    per_group = n // chunk
    tiles = width // LANES
    per_tile = LANES // head_size
    gain = [norms[k : k + 1, :].astype(F32) for k in range(8)]
    g_norms[...] = jnp.zeros_like(g_norms)

    def start(i):
        r = rows_of(i, chunk)
        slots = lax.broadcasted_iota(jnp.int32, (chunk, table.shape[0]), 1)
        named = marks_col[r, 0:1]
        chosen = jnp.where(slots == named, 1.0, 0.0).astype(BF16)
        picked = nn(chosen, table[...])
        begin = jnp.where(named >= 0, picked, gain[6])
        x[r, :] = begin
        hat, _ = unit(begin)
        h = (hat * gain[0] + gain[1]).astype(BF16)
        h_one[r, :] = h
        qkv[r, :] = nt(h, w_qkv[...]).astype(BF16)

    outer_loop(rows // chunk, start)

    def attend(g):
        bias[...] = mask_bias(marks_row[g, 1:2, :], marks_col[rows_of(g, n), 1:2])
        r = rows_of(g, n)

        def one(t):
            q, k, v = [qkv[r, lane_tile(t + j * tiles)] for j in range(3)]
            out, logs = attend_tile(q, k, v, bias[...], head_size)
            mixed[r, lane_tile(t)] = out.astype(BF16)
            for h in range(per_tile):
                totals[g * tiles + t, h : h + 1, :] = logs[h]

        outer_loop(tiles, one)

    outer_loop(groups, attend)

    hooks.ready()

    def middle(i):
        g, j = i // per_group, lax.rem(i, per_group)
        r = rows_of(i, chunk)
        one = x[r, :] + nt(mixed[r, :], w_out[...])
        hat_two, scale_two = unit(one)
        h = (hat_two * gain[2] + gain[3]).astype(BF16)
        h_two[r, :] = h
        step = 512
        for t in range(w_up.shape[0] // step):
            u = nt(h, w_up[t * step : (t + 1) * step, :])
            a, s = gelu_pair(u)
            act[r, t * step : (t + 1) * step] = a.astype(BF16)
            slope[:, t * step : (t + 1) * step] = s.astype(BF16)
        two = one + nt(act[r, :], w_down[...])
        hat, scale = unit(two)
        result = hat * gain[4] + gain[5]
        for b in range(groups):
            for c in range(per_group):
                lo = c * chunk
                hi = min(lo + chunk, real)

                @pl.when(i == b * per_group + c)
                def _(b=b, lo=lo, hi=hi):
                    decoded[b, lo:hi, :] = result[: hi - lo]
                    d_x[b, lo:hi, :] = cot[b, lo:hi, :]
                    if hi < lo + chunk:
                        d_x[b, hi : lo + chunk, :] = jnp.zeros((lo + chunk - hi, width), F32)

        cr = rows_of(j, chunk)
        d = d_x[g, cr, :]
        g_norms[4:5, :] += column_sum(d * hat)
        g_norms[5:6, :] += column_sum(d)
        d_two = unit_back(d * gain[4], hat, scale)
        e = d_two.astype(BF16)
        e_two[r, :] = e
        for t in range(w_up.shape[0] // step):
            cols = slice(t * step, (t + 1) * step)
            d_act = nn(e, w_down[:, cols])
            d_up[r, cols] = (d_act * slope[:, cols].astype(F32)).astype(BF16)
        d_h = nn(d_up[r, :], w_up[...])
        g_norms[2:3, :] += column_sum(d_h * hat_two)
        g_norms[3:4, :] += column_sum(d_h)
        d_one = d_two + unit_back(d_h * gain[2], hat_two, scale_two)
        d_x[g, cr, :] = d_one
        e_one[r, :] = d_one.astype(BF16)

    outer_loop(rows // chunk, middle)

    weight_sum(g_down, e_two, act, stage_wide, sem)
    hooks.summed(0)
    weight_sum(g_up, d_up, h_two, stage, sem)
    hooks.summed(1)
    weight_sum(g_out, e_one, mixed, stage, sem)
    hooks.summed(2)

    def mix_back(i):
        r = rows_of(i, chunk)
        mixed[r, :] = nn(e_one[r, :], w_out[...]).astype(BF16)

    outer_loop(rows // chunk, mix_back)
    d_qkv = act

    for g in range(groups):
        bias[...] = mask_bias(marks_row[g, 1:2, :], marks_col[rows_of(g, n), 1:2])
        r = rows_of(g, n)

        def one(t, g=g, r=r):
            q, k, v = [qkv[r, lane_tile(t + j * tiles)] for j in range(3)]
            logs = [totals[g * tiles + t, h : h + 1, :] for h in range(per_tile)]
            found = attend_tile_back(q, k, v, mixed[r, lane_tile(t)], bias[...], logs, head_size)
            for j in range(3):
                d_qkv[r, lane_tile(t + j * tiles)] = found[j].astype(BF16)

        for half in range(2):
            some(half * tiles // 2, (half + 1) * tiles // 2, one)
            hooks.pause(2 * g + half)

    def finish(i):
        g, j = i // per_group, lax.rem(i, per_group)
        r, cr = rows_of(i, chunk), rows_of(j, chunk)
        d_h = nn(d_qkv[r, : 3 * width], w_qkv[...])
        hat, scale = unit(x[r, :])
        g_norms[0:1, :] += column_sum(d_h * hat)
        g_norms[1:2, :] += column_sum(d_h)
        d_start = d_x[g, cr, :] + unit_back(d_h * gain[0], hat, scale)
        seen = marks_col[r, 0:1] >= 0
        g_norms[6:7, :] += column_sum(jnp.where(seen, 0.0, d_start))
        e_two[r, :] = jnp.where(seen, d_start, 0.0).astype(BF16)

    outer_loop(rows // chunk, finish)

    slots, slot_rows, _ = d_table.shape

    def back(s):
        line = lax.broadcasted_iota(jnp.int32, (slot_rows, n), 0) + s * slot_rows
        total = 0.0
        for g in range(groups):
            chosen = jnp.where(line == marks_row[g, 0:1, :], 1.0, 0.0).astype(BF16)
            total = total + nn(chosen, e_two[g * n : (g + 1) * n, :])
        d_table[s] = total.astype(BF16)

    hooks.slots(back, slots)
    weight_sum(g_qkv, d_qkv.at[:, : 3 * width], h_one, stage, sem)
    hooks.end()


def some(lo, hi, body):
    def step(i, carry):
        body(i)
        return carry

    lax.fori_loop(lo, hi, step, 0)


class NoHooks:
    def ready(self):
        pass

    def summed(self, k):
        pass

    def pause(self, k):
        pass

    def slots(self, body, count):
        outer_loop(count, body)

    def end(self):
        pass


class MiddleHooks:
    def __init__(self, loads, reducer, d_table, returned, swap_send, swap_recv, swap_local):
        self.loads, self.reducer = loads, reducer
        self.d_table, self.returned = d_table, returned
        self.swap = (swap_send, swap_recv, swap_local)

    def ready(self):
        for copy in self.loads:
            copy.wait()

    def summed(self, k):
        if k == 1:
            self.reducer.step(0)
        self.reducer.begin(k)

    def pause(self, k):
        for i in range(3):
            self.reducer.step(i)

    def slots(self, body, count):
        z, x, y, c = place()
        d, f = z * 2 + x, y * 2 + c
        send_sem, recv_sem, local_sem = self.swap
        for s in range(count):
            some(s, s + 1, body)

            @pl.when(s != d)
            def _(s=s):
                send_slot(self.d_table, self.returned, s, d, send_sem, recv_sem, f).start()

            @pl.when(s == d)
            def _(s=s):
                pltpu.make_async_copy(
                    self.d_table.at[s], self.returned.at[s], local_sem.at[0]
                ).start()

    def end(self):
        z, x, y, c = place()
        for i in range(3):
            self.reducer.finish(i)
        finish_swap(self.d_table, self.returned, z * 2 + x, *self.swap, y * 2 + c)
        self.reducer.drain()


def decoder_kernel(head_size, chunk, *refs):
    decoder_body(NoHooks(), head_size, chunk, *refs)


def middle_kernel(entries, head_size, chunk, *refs):
    ins, late, refs = refs[:6], refs[6:9], refs[9:]
    decoded, returned, g_norms, *refs = refs
    grads, refs = refs[:4], refs[4:]
    outs, refs = refs[:3], refs[3:]
    scratch, refs = refs[:16], refs[16:]
    loaded, refs = refs[:3], refs[3:]
    d_table, *refs = refs
    bufs, refs = refs[:21], refs[21:]
    send_sem, recv_sem, local_sem, swap_send, swap_recv, swap_local, load_sem = refs
    loads = [pltpu.make_async_copy(late[k], loaded[k], load_sem.at[k]) for k in range(3)]
    for copy in loads:
        copy.start()
    z, x, y, c = place()
    meet(z, x, y, c)
    by_entry = [grads[3], grads[2], grads[1]]
    reducer = Reducer(
        [
            reduce_stages(e, i, by_entry[i], outs[i], bufs[7 * i : 7 * i + 7], (send_sem, recv_sem), local_sem)
            for i, e in enumerate(entries)
        ]
    )
    hooks = MiddleHooks(loads, reducer, d_table, returned, swap_send, swap_recv, swap_local)
    decoder_body(hooks, head_size, chunk, *ins, *loaded, decoded, d_table, g_norms, *grads, *scratch)


def decoder(staged, table, index, segment, cotangent, norms, weights, heads):
    groups, real, width = cotangent.shape
    n = -(-real // 32) * 32
    chunk = n // 2
    rows = groups * n
    head_size = width // heads
    pad = n - real
    marks = jnp.stack([index, segment], axis=1)
    marks = jnp.pad(marks, ((0, 0), (0, 0), (0, pad)), constant_values=-1)
    tiles = width // LANES
    ff = weights[2].shape[0]
    vm = pl.BlockSpec(memory_space=pltpu.VMEM)
    hbm = pl.BlockSpec(memory_space=pl.ANY)
    scratch = [
        pltpu.VMEM((rows, width), F32),
        pltpu.VMEM((rows, width), BF16),
        pltpu.VMEM((rows, 3 * width), BF16),
        pltpu.VMEM((rows, width), BF16),
        pltpu.VMEM((groups * tiles, LANES // head_size, n), F32),
        pltpu.VMEM((rows, width), BF16),
        pltpu.VMEM((rows, ff), BF16),
        pltpu.VMEM((chunk, ff), BF16),
        pltpu.VMEM((rows, ff), BF16),
        pltpu.VMEM((rows, width), BF16),
        pltpu.VMEM((rows, width), BF16),
        pltpu.VMEM((n, n), F32),
        pltpu.VMEM((groups, n, width), F32),
        pltpu.VMEM((2, 256, width), BF16),
        pltpu.VMEM((2, LANES, ff), BF16),
        pltpu.SemaphoreType.DMA((2,)),
    ]
    args = (
        table,
        marks.transpose(0, 2, 1).reshape(rows, 2),
        marks,
        cotangent,
        norms,
        *weights,
    )
    slots = (8, table.shape[0] // 8, width)
    shapes = [
        jax.ShapeDtypeStruct(cotangent.shape, F32),
        jax.ShapeDtypeStruct(slots, BF16),
        jax.ShapeDtypeStruct((8, width), F32),
    ] + [jax.ShapeDtypeStruct(w.shape, BF16) for w in weights]
    if not staged:
        return pl.pallas_call(
            functools.partial(decoder_kernel, head_size, chunk),
            out_shape=shapes,
            in_specs=[vm] * 9,
            out_specs=[vm] * 3 + [hbm] * 4,
            scratch_shapes=scratch,
            compiler_params=pltpu.CompilerParams(vmem_limit_bytes=60 << 20),
            name="decoder",
        )(*args)
    entries = [entry_of(w.shape[0] // 8, w.shape[1]) for w in (weights[3], weights[2], weights[1])]
    sem = pltpu.SemaphoreType.DMA
    return pl.pallas_call(
        functools.partial(middle_kernel, entries, head_size, chunk),
        out_shape=shapes + [jax.ShapeDtypeStruct((e.part, e.q), F32) for e in entries],
        in_specs=[vm] * 6 + [hbm] * 3,
        out_specs=[vm, hbm, vm] + [hbm] * 4 + [vm] * 3,
        scratch_shapes=scratch
        + [pltpu.VMEM(w.shape, BF16) for w in weights[1:]]
        + [pltpu.VMEM(slots, BF16)]
        + [pltpu.VMEM(shape, BF16) for e in entries for shape in reduce_buffers(e)]
        + [sem((3, 9)), sem((3, 9)), sem((3,)), sem((8,)), sem((8,)), sem((1,)), sem((3,))],
        compiler_params=pltpu.CompilerParams(
            collective_id=1, has_side_effects=True, vmem_limit_bytes=62 << 20
        ),
        name="middle",
    )(*args)


def encoder_kernel(
    head_size,
    groups,
    chunk,
    patches,
    key_col,
    own_row,
    norms,
    shift,
    w_qkv,
    w_out,
    w_up,
    w_down,
    w_embed,
    embedded,
    qkv,
    totals,
    mixed,
    x_one,
    act,
    slope,
    sent,
):
    rows, width = patches.shape
    n = rows // groups
    tiles = width // LANES
    per_tile = LANES // head_size
    gain = [norms[k : k + 1, :].astype(F32) for k in range(4)]
    add = shift[7:8, :].astype(F32)

    def start(i):
        r = rows_of(i, chunk)
        hat, _ = unit(patches[r, :].astype(F32))
        qkv[r, :] = nt((hat * gain[0] + gain[1]).astype(BF16), w_qkv[...]).astype(BF16)

    outer_loop(rows // chunk, start)

    def attend(g):
        r = rows_of(g, n)
        bias = mask_bias(own_row[g], key_col[r, :])
        for t in range(tiles):
            q, k, v = [qkv[r, (t + j * tiles) * LANES : (t + j * tiles + 1) * LANES] for j in range(3)]
            out, logs = attend_tile(q, k, v, bias, head_size)
            mixed[r, t * LANES : (t + 1) * LANES] = out.astype(BF16)
            for h in range(per_tile):
                totals[g, t * per_tile + h : t * per_tile + h + 1, :] = logs[h]

    outer_loop(groups, attend)

    def middle(i):
        r = rows_of(i, chunk)
        one = patches[r, :].astype(F32) + nt(mixed[r, :], w_out[...])
        x_one[r, :] = one
        hat, _ = unit(one)
        h = (hat * gain[2] + gain[3]).astype(BF16)
        step = 512
        for t in range(w_up.shape[0] // step):
            u = nt(h, w_up[t * step : (t + 1) * step, :])
            a, s = gelu_pair(u)
            act[r, t * step : (t + 1) * step] = a.astype(BF16)
            slope[r, t * step : (t + 1) * step] = s.astype(BF16)
        two = (one + nt(act[r, :], w_down[...])).astype(BF16)
        sent[r, :] = two
        embedded[r, :] = (nt(two, w_embed[...]) + add).astype(BF16)

    outer_loop(rows // chunk, middle)


def encoder_back_kernel(
    head_size,
    groups,
    chunk,
    patches,
    key_col,
    own_row,
    norms,
    w_qkv,
    w_out,
    w_up,
    w_down,
    w_embed,
    d_table,
    qkv,
    totals,
    mixed,
    x_one,
    act,
    slope,
    sent,
    d_patches,
    g_norms,
    g_shift,
    g_qkv,
    g_out,
    g_up,
    g_down,
    g_embed,
    e_two,
    e_one,
    stage,
    stage_wide,
    sem,
):
    rows, width = patches.shape
    n = rows // groups
    tiles = width // LANES
    per_tile = LANES // head_size
    gain = [norms[k : k + 1, :].astype(F32) for k in range(4)]
    g_norms[...] = jnp.zeros_like(g_norms)
    g_shift[...] = jnp.zeros_like(g_shift)
    step = 512
    weight_sum(g_embed, d_table, sent, stage, sem)
    h_two = sent

    def middle(i):
        r = rows_of(i, chunk)
        d_emb = d_table[r, :]
        g_shift[0:1, :] += column_sum(d_emb.astype(F32))
        e = nn(d_emb, w_embed[...]).astype(BF16)
        e_two[r, :] = e
        for t in range(w_up.shape[0] // step):
            cols = slice(t * step, (t + 1) * step)
            d_act = nn(e, w_down[:, cols])
            slope[r, cols] = (d_act * slope[r, cols].astype(F32)).astype(BF16)
        d_h = nn(slope[r, :], w_up[...])
        hat, scale = unit(x_one[r, :])
        h_two[r, :] = (hat * gain[2] + gain[3]).astype(BF16)
        g_norms[2:3, :] += column_sum(d_h * hat)
        g_norms[3:4, :] += column_sum(d_h)
        d_one = e.astype(F32) + unit_back(d_h * gain[2], hat, scale)
        d_patches[r, :] = d_one
        e_one[r, :] = d_one.astype(BF16)

    outer_loop(rows // chunk, middle)
    weight_sum(g_down, e_two, act, stage_wide, sem)
    weight_sum(g_up, slope, h_two, stage, sem)
    weight_sum(g_out, e_one, mixed, stage, sem)

    def mix_back(i):
        r = rows_of(i, chunk)
        mixed[r, :] = nn(e_one[r, :], w_out[...]).astype(BF16)

    outer_loop(rows // chunk, mix_back)

    def attend_back(g):
        r = rows_of(g, n)
        bias = mask_bias(own_row[g], key_col[r, :])
        for t in range(tiles):
            cols = [slice((t + j * tiles) * LANES, (t + j * tiles + 1) * LANES) for j in range(3)]
            q, k, v = [qkv[r, col] for col in cols]
            logs = [totals[g, t * per_tile + h : t * per_tile + h + 1, :] for h in range(per_tile)]
            found = attend_tile_back(q, k, v, mixed[r, cols[0]], bias, logs, head_size)
            for j in range(3):
                act[r, cols[j]] = found[j].astype(BF16)

    outer_loop(groups, attend_back)
    h_one = h_two

    def finish(i):
        r = rows_of(i, chunk)
        d_h = nn(act[r, : 3 * width], w_qkv[...])
        hat, scale = unit(patches[r, :].astype(F32))
        h_one[r, :] = (hat * gain[0] + gain[1]).astype(BF16)
        g_norms[0:1, :] += column_sum(d_h * hat)
        g_norms[1:2, :] += column_sum(d_h)
        d_patches[r, :] += unit_back(d_h * gain[0], hat, scale)

    outer_loop(rows // chunk, finish)
    weight_sum(g_qkv, act.at[:, : 3 * width], h_one, stage, sem)


def slot_plan(peers, slot_rows):
    padded = -(-slot_rows // 16) * 16
    joined = max(1, 128 // padded)
    return padded, joined


def encoder_inputs(patches, counts):
    peers = counts.shape[0]
    width = patches.shape[1]
    slot_rows = patches.shape[0] // peers
    padded, joined = slot_plan(peers, slot_rows)
    rows, groups = peers * padded, peers // joined
    n = rows // groups
    x = jnp.pad(patches.reshape(peers, slot_rows, width), ((0, 0), (0, padded - slot_rows), (0, 0)))
    x = x.reshape(rows, width)
    row = jnp.arange(padded, dtype=jnp.int32)[None, :]
    slot = jnp.arange(peers, dtype=jnp.int32)[:, None]
    live = (row >= slot_rows - counts[:, None]) & (row < slot_rows)
    keys = jnp.where(live, slot, -1).reshape(rows, 1)
    own = jnp.broadcast_to(slot, (peers, padded)).reshape(groups, 1, n)
    return x, keys, own, padded


def encoder(patches, counts, norms, shift, weights, embed, heads):
    x, keys, own, _ = encoder_inputs(patches, counts)
    rows, width = x.shape
    groups, _, n = own.shape
    head_size = width // heads
    ff = weights[2].shape[0]
    vm = pl.BlockSpec(memory_space=pltpu.VMEM)
    shapes = [
        ((rows, weights[0].shape[0]), BF16),
        ((groups, -(-heads // 8) * 8, n), F32),
        ((rows, width), BF16),
        ((rows, width), F32),
        ((rows, ff), BF16),
        ((rows, ff), BF16),
        ((rows, width), BF16),
    ]
    shapes = [jax.ShapeDtypeStruct(s, t) for s, t in shapes]
    embedded, *stored = pl.pallas_call(
        functools.partial(encoder_kernel, head_size, groups, 2 * n),
        out_shape=[jax.ShapeDtypeStruct((rows, embed.shape[0]), BF16)] + shapes,
        in_specs=[vm] * 10,
        out_specs=[vm] * 8,
        compiler_params=pltpu.CompilerParams(vmem_limit_bytes=60 << 20),
        name="encoder",
    )(x, keys, own, norms, shift, *weights, embed)
    return embedded, (x, keys, own), stored


def encoder_back(rows_in, norms, weights, embed, d_table, stored, heads):
    x, keys, own = rows_in
    rows, width = x.shape
    groups, _, n = own.shape
    head_size = width // heads
    vm = pl.BlockSpec(memory_space=pltpu.VMEM)
    return pl.pallas_call(
        functools.partial(encoder_back_kernel, head_size, groups, 2 * n),
        out_shape=[
            jax.ShapeDtypeStruct((rows, width), F32),
            jax.ShapeDtypeStruct((8, width), F32),
            jax.ShapeDtypeStruct((8, embed.shape[0]), F32),
        ]
        + [jax.ShapeDtypeStruct(w.shape, BF16) for w in weights]
        + [jax.ShapeDtypeStruct(embed.shape, BF16)],
        in_specs=[vm] * 17,
        out_specs=[vm] * 3 + [pl.BlockSpec(memory_space=pl.ANY)] * 5,
        scratch_shapes=[pltpu.VMEM((rows, width), BF16)] * 2
        + [
            pltpu.VMEM((2, 256, width), BF16),
            pltpu.VMEM((2, LANES, weights[2].shape[0]), BF16),
            pltpu.SemaphoreType.DMA((2,)),
        ],
        compiler_params=pltpu.CompilerParams(vmem_limit_bytes=62 << 20),
        name="encoder_back",
    )(x, keys, own, norms, *weights, embed, d_table, *stored)


class Ticker:
    def __init__(self, plans, locals_):
        self.plans, self.locals_, self.moving, self.t = plans, locals_, {}, 0

    def tick(self, count=1):
        for _ in range(count):
            self.part((3, 2, 1, 0))
            self.t += 1

    def part(self, stages):
        for stage in stages:
            i = self.t - 2 * stage
            if 0 <= i < len(self.plans):
                self.advance(i, stage)

    def rest(self):
        self.part((2, 1, 0))
        self.t += 1

    def advance(self, i, stage):
        if stage > 0:
            for copy in self.moving[i, stage - 1]:
                copy.wait_recv()
            if stage == 1:
                self.locals_[i].wait()
        self.moving[i, stage] = self.plans[i][stage]()
        for copy in self.moving[i, stage]:
            copy.start()

    def arrived(self, i):
        for copy in self.moving[i, 3]:
            copy.wait_recv()

    def drain(self):
        for copies in self.moving.values():
            for copy in copies:
                copy.wait_send()


def flat(ref):
    value = ref[...]
    return value.reshape(-1, value.shape[-1])


def spread_norms(tiles, start, count, part, out):
    width = 8 * part
    lane = lax.broadcasted_iota(jnp.int32, (LANES, width), 1)
    line = lax.broadcasted_iota(jnp.int32, (LANES, width), 0)
    for f in range(4):
        total = 0.0
        for d in range(8):
            put = jnp.where((lane == line + d * part) & (line < part), 1.0, 0.0).astype(BF16)
            rows = tiles[d // 2, d % 2, start : start + 16, f * LANES : (f + 1) * LANES]
            total = total + nn(rows, put)
        out[f * count : (f + 1) * count, :] = total[:count]


def front_kernel(entries, head_size, groups, chunk, sizes, *refs):
    n_in = len(entries)
    pieces, refs = refs[:n_in], refs[n_in:]
    patches, key_col, own_row, *refs = refs
    whole, refs = refs[:n_in], refs[n_in:]
    norms_e, norms_d, table, totals, *refs = refs
    kept_out, refs = refs[:6], refs[6:]
    kept, refs = refs[:6], refs[6:]
    qkv, mixed, x_one, act, slope, sent = kept
    loaded, refs = refs[:6], refs[6:]
    tiles_v, w_qkv, w_out, w_up, w_embed, w_down = loaded
    embedded, send_sem, recv_sem, local_sem, load_sem, keep_sem, swap_send, swap_recv, swap_local = refs
    rows, width = patches.shape
    n = rows // groups
    tiles = width // LANES
    per_tile = LANES // head_size
    z, x, y, c = place()
    d = z * 2 + x

    plans, locals_ = [], []
    for i, e in enumerate(entries):
        local, stages = gather_stages(
            e, i, pieces[i], whole[i], (send_sem, recv_sem), local_sem, i >= 6
        )
        plans.append(stages)
        locals_.append(local())
    for copy in locals_:
        copy.start()
    meet(z, x, y, c)
    ticker = Ticker(plans, locals_)

    def load(i):
        ticker.arrived(i)
        copy = pltpu.make_async_copy(whole[i], loaded[i], load_sem.at[i])
        copy.start()
        return copy

    keeping = []

    def keep(k):
        copy = pltpu.make_async_copy(kept[k], kept_out[k], keep_sem.at[k])
        copy.start()
        keeping.append(copy)

    ticker.tick(7)
    ticker.part((3,))
    copies = [load(0), load(1)]
    for copy in copies:
        copy.wait()
    spread_norms(tiles_v, 0, sizes[0], sizes[1], norms_e)
    spread_norms(tiles_v, NORM_ROWS // 2, sizes[2], sizes[3], norms_d)
    gain = [norms_e[k : k + 1, :] for k in range(4)]
    add = norms_d[7:8, :]

    def start(i):
        r = rows_of(i, chunk)
        hat, _ = unit(patches[r, :].astype(F32))
        qkv[r, :] = nt((hat * gain[0] + gain[1]).astype(BF16), flat(w_qkv)).astype(BF16)

    some(0, 2, start)
    ticker.rest()
    some(2, 4, start)
    ticker.tick()
    keep(0)

    def attend(g):
        r = rows_of(g, n)
        bias = mask_bias(own_row[g], key_col[r, :])
        for t in range(tiles):
            q, k, v = [qkv[r, (t + j * tiles) * LANES : (t + j * tiles + 1) * LANES] for j in range(3)]
            out, logs = attend_tile(q, k, v, bias, head_size)
            mixed[r, t * LANES : (t + 1) * LANES] = out.astype(BF16)
            for h in range(per_tile):
                totals[g, t * per_tile + h : t * per_tile + h + 1, :] = logs[h]

    some(0, 3 * groups // 4, attend)
    ticker.tick()
    some(3 * groups // 4, groups, attend)
    keep(1)
    copies = [load(2), load(3)]
    ticker.tick()
    for copy in copies:
        copy.wait()
    step = w_up.shape[-2] * (2 if len(w_up.shape) == 5 else 1)

    def lift(i):
        r = rows_of(i, chunk)
        one = patches[r, :].astype(F32) + nt(mixed[r, :], flat(w_out))
        x_one[r, :] = one
        hat, _ = unit(one)
        h = (hat * gain[2] + gain[3]).astype(BF16)
        for t in range(8):
            u = nt(h, w_up[t // 2, t % 2].reshape(step, width))
            a, s = gelu_pair(u)
            act[r, t * step : (t + 1) * step] = a.astype(BF16)
            slope[r, t * step : (t + 1) * step] = s.astype(BF16)

    some(0, 3, lift)
    ticker.tick()
    some(3, 4, lift)
    copies = [load(4), load(5)]
    for k in (2, 3, 4):
        keep(k)
    for copy in copies:
        copy.wait()
    per_chunk = chunk // embedded.shape[1]
    for i in range(4):

        def lower(i):
            r = rows_of(i, chunk)
            two = (x_one[r, :] + nt(act[r, :], flat(w_down))).astype(BF16)
            sent[r, :] = two
            out = (nt(two, flat(w_embed)) + add).astype(BF16)
            for k in range(per_chunk):
                embedded[i * per_chunk + k] = out[k * embedded.shape[1] : (k + 1) * embedded.shape[1]]

        some(i, i + 1, lower)
        for k in range(per_chunk):
            s = i * per_chunk + k

            @pl.when(s != d)
            def _(s=s):
                send_slot(embedded, table, s, d, swap_send, swap_recv, y * 2 + c).start()

            @pl.when(s == d)
            def _(s=s):
                pltpu.make_async_copy(embedded.at[s], table.at[s], swap_local.at[0]).start()

        if i == 1:
            ticker.tick()
    keep(5)
    while ticker.t < n_in + 6:
        ticker.tick()
    for i in range(6, n_in):
        ticker.arrived(i)
    finish_swap(embedded, table, d, swap_send, swap_recv, swap_local, y * 2 + c)
    ticker.drain()
    for copy in keeping:
        copy.wait()


def send_slot(src, dst, s, d, sends, recvs, f):
    return pltpu.make_async_remote_copy(
        src_ref=src.at[s],
        dst_ref=dst.at[d],
        send_sem=sends.at[s],
        recv_sem=recvs.at[d],
        device_id=(s, f),
        device_id_type=MESH,
    )


def finish_swap(src, dst, d, sends, recvs, local, f):
    for s in range(8):

        @pl.when(s != d)
        def _(s=s):
            came = pltpu.make_async_remote_copy(
                src_ref=src.at[s],
                dst_ref=dst.at[s],
                send_sem=sends.at[s],
                recv_sem=recvs.at[s],
                device_id=(s, f),
                device_id_type=MESH,
            )
            came.wait_send()
            came.wait_recv()

    pltpu.make_async_copy(src.at[d], dst.at[d], local.at[0]).wait()


def front(entries, pieces, patches, counts, sizes, heads):
    peers = 8
    width = patches.shape[1]
    x, keys, own, padded = encoder_inputs(patches, counts)
    rows = x.shape[0]
    groups, _, n = own.shape
    head_size = width // heads
    by = {k: e for k, e in enumerate(entries)}
    wide, ff = 3 * width, 8 * entries[3].rows
    embed = 8 * entries[4].rows
    kept = [
        ((rows, wide), BF16),
        ((rows, width), BF16),
        ((rows, width), F32),
        ((rows, ff), BF16),
        ((rows, ff), BF16),
        ((rows, width), BF16),
    ]
    vm, hbm = pl.BlockSpec(memory_space=pltpu.VMEM), pl.BlockSpec(memory_space=pl.ANY)
    n_in = len(entries)
    sem = pltpu.SemaphoreType.DMA
    found = pl.pallas_call(
        functools.partial(front_kernel, entries, head_size, groups, rows // 4, sizes),
        out_shape=[jax.ShapeDtypeStruct(e.whole, BF16) for e in entries]
        + [
            jax.ShapeDtypeStruct((4 * sizes[0], 8 * sizes[1]), F32),
            jax.ShapeDtypeStruct((4 * sizes[2], 8 * sizes[3]), F32),
            jax.ShapeDtypeStruct((peers, padded, embed), BF16),
            jax.ShapeDtypeStruct((groups, -(-heads // 8) * 8, n), F32),
        ]
        + [jax.ShapeDtypeStruct(s, t) for s, t in kept],
        in_specs=[hbm] * n_in + [vm] * 3,
        out_specs=[hbm] * n_in + [vm, vm, hbm, vm] + [hbm] * 6,
        scratch_shapes=[pltpu.VMEM(s, t) for s, t in kept]
        + [pltpu.VMEM(by[k].whole, BF16) for k in range(6)]
        + [
            pltpu.VMEM((peers, padded, embed), BF16),
            sem((n_in, 16)),
            sem((n_in, 16)),
            sem((n_in,)),
            sem((6,)),
            sem((6,)),
            sem((8,)),
            sem((8,)),
            sem((1,)),
        ],
        compiler_params=pltpu.CompilerParams(
            collective_id=0, has_side_effects=True, vmem_limit_bytes=60 << 20
        ),
        name="front",
    )(*pieces, x, keys, own)
    whole, (norms_e, norms_d, table, totals) = found[:n_in], found[n_in : n_in + 4]
    qkv, mixed, x_one, act, slope, sent = found[n_in + 4 :]
    return whole, norms_e, norms_d, table, (x, keys, own), [qkv, totals, mixed, x_one, act, slope, sent]


class Reducer:
    def __init__(self, plans):
        self.plans, self.stage, self.moving, self.waits = plans, {}, [], {}

    def start(self, i, copies, waits):
        for copy in copies:
            copy.start()
        self.waits[i] = waits
        self.moving += waits

    def begin(self, i):
        local, stages = self.plans[i]
        copies, self.local_waits = local()
        for copy in copies:
            copy.start()
        self.waits[i, 0] = self.local_waits
        self.start(i, *stages[0][0]())
        self.stage[i] = 0

    def step(self, i):
        k = self.stage[i]
        if k == 4:
            return
        _, stages = self.plans[i]
        for copy in self.waits[i]:
            copy.wait_recv()
        if k == 0:
            for copy in self.waits[i, 0]:
                copy.wait()
        stages[k][1]()
        if k < 3:
            self.start(i, *stages[k + 1][0]())
        self.stage[i] = k + 1

    def finish(self, i):
        while self.stage[i] < 4:
            self.step(i)

    def drain(self):
        for copy in self.moving:
            copy.wait_send()


def meet(z, x, y, c):
    d = z * 2 + x
    barrier = pltpu.get_barrier_semaphore()
    peers = [(lax.rem(d + k, 8), y * 2 + c) for k in range(1, 8)]
    peers += [at(z, x, 1 - y, c), at(z, x, y, 1 - c)]
    for peer in peers:
        pl.semaphore_signal(barrier, inc=1, device_id=peer, device_id_type=MESH)
    pl.semaphore_wait(barrier, len(peers))


def gather_norms(g, start, count, part, tiles):
    width = 8 * part
    lane = lax.broadcasted_iota(jnp.int32, (width, LANES), 1)
    line = lax.broadcasted_iota(jnp.int32, (width, LANES), 0)
    rows = g.astype(BF16)
    for d in range(8):
        put = jnp.where((line == lane + d * part) & (lane < part), 1.0, 0.0).astype(BF16)
        cut = nn(rows, put).astype(BF16)
        for f in range(4):
            tiles[d // 2, d % 2, start : start + count, f * LANES : (f + 1) * LANES] = cut[
                f * count : (f + 1) * count
            ]


def rear_kernel(parts, places, n_out, head_size, groups, chunk, sizes, *refs):
    patches, key_col, own_row, norms, g_dec, g_dec_qkv, *refs = refs
    weights, refs = refs[:5], refs[5:]
    d_table, *refs = refs
    stored, refs = refs[:7], refs[7:]
    d_patches, *refs = refs
    g_embed, g_down, g_up, g_out, g_qkv, *refs = refs
    outs, refs = refs[:n_out], refs[n_out:]
    up_v, down_v, embed_v, act, slope, mixed, sent, e_two, e_one, d_emb, totals, small, *refs = refs
    stage, stage_wide, sem, g_norms, g_shift, *refs = refs
    bufs, refs = refs[: 7 * len(parts)], refs[7 * len(parts) :]
    send_sem, recv_sem, local_sem, load_sem = refs
    w_qkv, w_out, w_up, w_down, w_embed = weights
    s_qkv, s_totals, s_mixed, s_one, s_act, s_slope, s_sent = stored
    rows, width = patches.shape
    n = rows // groups
    tiles = width // LANES
    per_tile = LANES // head_size
    wide = 3 * width
    z, x, y, c = place()
    loads = {}

    def load(k, src, dst):
        loads[k] = pltpu.make_async_copy(src, dst, load_sem.at[k])
        loads[k].start()

    load(0, w_embed, embed_v)
    load(1, d_table, d_emb)
    load(2, s_act, act)
    load(3, s_sent, sent)
    load(4, w_down, down_v)
    load(5, s_slope, slope)
    load(6, w_up, up_v)
    load(7, s_one, d_patches)
    load(8, s_mixed, mixed)
    load(9, s_totals, totals)
    small[...] = jnp.zeros_like(small)
    g_norms[...] = jnp.zeros_like(g_norms)
    g_shift[...] = jnp.zeros_like(g_shift)
    meet(z, x, y, c)
    sources = {"dq": g_dec_qkv, "do": g_down, "em": g_embed, "up": g_up, "ou": g_out, "qk": g_qkv, "sm": small}
    plans = {}
    for i, (name, e, row) in enumerate(parts):
        out, first = outs[places[name[:2]][0]], places[name[:2]][1]
        plans[name] = reduce_stages(
            e, i, sources[name[:2]], out, bufs[7 * i : 7 * i + 7], (send_sem, recv_sem), local_sem, row, first
        )
    reducer = Reducer(plans)
    gain = [norms[k : k + 1, :] for k in range(4)]
    h_two, h_one = sent, e_two
    step = 512

    def enter():
        loads[0].wait()
        loads[1].wait()
        some(0, rows // chunk, enter_rows)
        loads[2].wait()

    def enter_rows(i):
        r = rows_of(i, chunk)
        g_shift[0:1, :] += column_sum(d_emb[r, :].astype(F32))
        e_two[r, :] = nn(d_emb[r, :], embed_v[...]).astype(BF16)

    def sum_down():
        weight_sum(g_down, e_two, act, stage_wide, sem)

    def sum_embed():
        loads[3].wait()
        weight_sum(g_embed, d_emb, sent, stage, sem)
        for k in range(4, 8):
            loads[k].wait()

    def middle_rows(i):
        r = rows_of(i, chunk)
        e = e_two[r, :]
        for t in range(slope.shape[1] // step):
            cols = slice(t * step, (t + 1) * step)
            d_act = nn(e, down_v[:, cols])
            slope[r, cols] = (d_act * slope[r, cols].astype(F32)).astype(BF16)
        d_h = nn(slope[r, :], up_v[...])
        hat, scale = unit(d_patches[r, :])
        h_two[r, :] = (hat * gain[2] + gain[3]).astype(BF16)
        g_norms[2:3, :] += column_sum(d_h * hat)
        g_norms[3:4, :] += column_sum(d_h)
        d_one = e.astype(F32) + unit_back(d_h * gain[2], hat, scale)
        d_patches[r, :] = d_one
        e_one[r, :] = d_one.astype(BF16)

    def middle(i):
        some(i, i + 1, middle_rows)

    def sum_up():
        load(10, w_qkv, up_v.at[:wide, :])
        load(11, w_out, up_v.at[wide:, :])
        weight_sum(g_up, slope, h_two, stage, sem)
        load(12, s_qkv, slope.at[:, :wide])

    def sum_out():
        loads[8].wait()
        loads[9].wait()
        weight_sum(g_out, e_one, mixed, stage, sem)

    def mix_rows(i):
        r = rows_of(i, chunk)
        mixed[r, :] = nn(e_one[r, :], up_v[wide:, :]).astype(BF16)
        hat, _ = unit(patches[r, :].astype(F32))
        h_one[r, :] = (hat * gain[0] + gain[1]).astype(BF16)

    def mix():
        loads[11].wait()
        some(0, rows // chunk, mix_rows)
        loads[12].wait()

    def attend_back(g):
        r = rows_of(g, n)
        bias = mask_bias(own_row[g], key_col[r, :])
        for t in range(tiles):
            cols = [slice((t + j * tiles) * LANES, (t + j * tiles + 1) * LANES) for j in range(3)]
            q, k, v = [slope[r, col] for col in cols]
            logs = [totals[g, t * per_tile + h : t * per_tile + h + 1, :] for h in range(per_tile)]
            found = attend_tile_back(q, k, v, mixed[r, cols[0]], bias, logs, head_size)
            for j in range(3):
                act[r, cols[j]] = found[j].astype(BF16)

    def attend(i):
        some(i * groups // 4, (i + 1) * groups // 4, attend_back)

    def sum_qkv():
        weight_sum(g_qkv, act.at[:, :wide], h_one, stage, sem)
        loads[10].wait()

    def finish_rows(i):
        r = rows_of(i, chunk)
        d_h = nn(act[r, :wide], up_v[:wide, :])
        hat, scale = unit(patches[r, :].astype(F32))
        g_norms[0:1, :] += column_sum(d_h * hat)
        g_norms[1:2, :] += column_sum(d_h)
        d_patches[r, :] += unit_back(d_h * gain[0], hat, scale)

    def finish(i):
        some(i, i + 1, finish_rows)

    def norms_of_all():
        gather_norms(g_norms[0:4, :], 0, sizes[0], sizes[1], small)

    def norms_of_decoder():
        line = lax.broadcasted_iota(jnp.int32, g_dec.shape, 0)
        joined = jnp.where(line == 7, g_shift[0:1, :], g_dec[...])
        gather_norms(joined, NORM_ROWS // 2, sizes[2], sizes[3], small)

    blocks = {
        "enter": enter,
        "down": sum_down,
        "embed": sum_embed,
        "up": sum_up,
        "out": sum_out,
        "mix": mix,
        "qkv": sum_qkv,
        "norms": norms_of_all,
        "dnorms": norms_of_decoder,
    }
    for i in range(4):
        blocks["mid" + str(i)] = functools.partial(middle, i)
        blocks["att" + str(i)] = functools.partial(attend, i)
        blocks["fin" + str(i)] = functools.partial(finish, i)
    for name, actions in REAR_PLAN:
        if name:
            blocks[name]()
        for action in actions:
            if action[0] == "+":
                reducer.begin(action[1:])
            else:
                reducer.step(action)
    for name, _, _ in parts:
        reducer.finish(name)
    reducer.drain()


REAR_SPLIT = {"qk": 3}
REAR_PLAN = (
    ("", ("+dq",)),
    ("enter", ()),
    ("down", ("+do", "dq")),
    ("dnorms", ()),
    ("embed", ("+em",)),
    ("mid0", ()),
    ("mid1", ("dq", "em", "do")),
    ("mid2", ()),
    ("mid3", ("dq",)),
    ("up", ("+up", "em", "dq")),
    ("out", ("+ou",)),
    ("mix", ()),
    ("att0", ("ou", "do", "up", "em")),
    ("att1", ()),
    ("att2", ("em", "ou")),
    ("att3", ("do",)),
    ("qkv", ("+qk0", "+qk1", "+qk2", "up")),
    ("fin0", ()),
    ("fin1", ("ou",)),
    ("fin2", ("qk0",)),
    ("fin3", ("qk1", "qk2")),
    ("norms", ("+sm", "up", "do", "sm", "qk0", "sm", "qk1", "qk0", "qk2", "sm", "qk1", "qk2", "ou", "up")),
)


def rear(rows_in, norms, g_dec, g_dec_qkv, weights, embed, d_table, stored, sizes):
    x, keys, own = rows_in
    rows, width = x.shape
    groups, _, n = own.shape
    head_size = width // HEADS_E
    ff = weights[2].shape[0]
    first = (8 * g_dec_qkv.shape[2], g_dec_qkv.shape[3])
    names = ("dq", "do", "em", "up", "ou", "qk", "sm")
    shapes = [first, weights[3].shape, embed.shape, weights[2].shape, weights[1].shape, weights[0].shape]
    entries = [entry_of(s[0] // 8, s[1]) for s in shapes] + [entry_of(NORM_ROWS, 512)]
    places, sums, high = {}, [], 0
    for name, e in zip(names, entries):
        if e.by_core:
            places[name] = (0, high)
            high += e.part
    sums.append((high, entries[5].q))
    for name, e in zip(names, entries):
        if not e.by_core:
            places[name] = (len(sums), 0)
            sums.append((e.part, e.q))
    parts = []
    for name, e in zip(names, entries):
        count = REAR_SPLIT.get(name, 1)
        for k in range(count):
            cut = dataclasses.replace(e, share=count)
            parts.append((name + (str(k) if count > 1 else ""), cut, k * cut.part))
    vm, hbm = pl.BlockSpec(memory_space=pltpu.VMEM), pl.BlockSpec(memory_space=pl.ANY)
    sem = pltpu.SemaphoreType.DMA
    n_in = len(parts)
    totals = stored[1]
    found = pl.pallas_call(
        functools.partial(rear_kernel, parts, places, len(sums), head_size, groups, rows // 4, sizes),
        out_shape=[jax.ShapeDtypeStruct((rows, width), F32)]
        + [jax.ShapeDtypeStruct(s, BF16) for s in (shapes[2], shapes[1], *shapes[3:])]
        + [jax.ShapeDtypeStruct(s, F32) for s in sums],
        in_specs=[vm] * 5 + [hbm] * 14,
        out_specs=[vm] + [hbm] * 5 + [vm] * len(sums),
        scratch_shapes=[
            pltpu.VMEM(weights[2].shape, BF16),
            pltpu.VMEM(weights[3].shape, BF16),
            pltpu.VMEM(embed.shape, BF16),
            pltpu.VMEM((rows, ff), BF16),
            pltpu.VMEM((rows, ff), BF16),
            pltpu.VMEM((rows, width), BF16),
            pltpu.VMEM((rows, width), BF16),
            pltpu.VMEM((rows, width), BF16),
            pltpu.VMEM((rows, width), BF16),
            pltpu.VMEM(d_table.shape, BF16),
            pltpu.VMEM(totals.shape, F32),
            pltpu.VMEM(entries[-1].whole, BF16),
            pltpu.VMEM((2, 256, width), BF16),
            pltpu.VMEM((2, LANES, ff), BF16),
            sem((2,)),
            pltpu.VMEM((8, width), F32),
            pltpu.VMEM((8, embed.shape[0]), F32),
        ]
        + [pltpu.VMEM(shape, BF16) for _, e, _ in parts for shape in reduce_buffers(e)]
        + [sem((n_in, 9)), sem((n_in, 9)), sem((n_in,)), sem((13,))],
        compiler_params=pltpu.CompilerParams(
            collective_id=2, has_side_effects=True, vmem_limit_bytes=63 << 20
        ),
        name="rear",
    )(x, keys, own, norms, g_dec, g_dec_qkv, *weights, embed, d_table, *stored)
    return found[0], found[6:], places


def per_device(
    staged,
    patches,
    send_counts,
    dec_segment,
    source_index,
    cotangent,
    enc_norms,
    enc_qkv,
    enc_out,
    enc_up,
    enc_down,
    dec_norms,
    dec_embed,
    dec_qkv,
    dec_out,
    dec_up,
    dec_down,
):
    peers = lax.axis_size("dp")
    width = patches.shape[1]
    slot_rows = patches.shape[0] // peers
    counts = send_counts.reshape(peers)
    masters = (enc_qkv, enc_out, enc_up, dec_embed, enc_down, dec_qkv, dec_out, dec_up, dec_down)
    padded = slot_plan(peers, slot_rows)[0]

    def swap(table):
        slots = table.reshape(peers, padded, table.shape[1])
        return lax.all_to_all(slots, "dp", split_axis=0, concat_axis=0, tiled=True).reshape(table.shape)

    if staged:
        entries, pieces = staged_pieces(enc_norms, dec_norms, masters)
        sizes = (*enc_norms.shape, *dec_norms.shape)
        whole, norms_e, norms_d, table, enc_inputs, stored = front(
            entries, pieces, patches, counts, sizes, HEADS_E
        )
        whole = [w.reshape(-1, w.shape[-1]) for w in whole[1:]]
        table = table.reshape(-1, table.shape[-1])
    else:
        norms_e, norms_d, whole = gather_masters(enc_norms, dec_norms, masters)
    enc_weights, embed, dec_weights = [*whole[:3], whole[4]], whole[3], whole[5:]
    if not staged:
        embedded, enc_inputs, stored = encoder(
            patches, counts, norms_e, norms_d, enc_weights, embed, HEADS_E
        )
        table = swap(embedded)
    place_of = source_index // slot_rows * padded + source_index % slot_rows
    index = jnp.where(source_index >= 0, place_of, -1)
    if staged:
        decoded, d_table, g_dec_norms, g_qkv, _, _, _, s_down, s_up, s_out = decoder(
            True, table, index, dec_segment, cotangent, norms_d, dec_weights, HEADS_D
        )
        e = entry_of(g_qkv.shape[0] // 8, g_qkv.shape[1])
        d_patches, sums, places = rear(
            enc_inputs,
            norms_e,
            g_dec_norms,
            g_qkv.reshape(e.whole),
            enc_weights,
            embed,
            d_table.reshape(table.shape),
            stored,
            sizes,
        )
        small = sums[places["sm"][0]]
        half = NORM_ROWS // 2
        s_enc_norms = small[: sizes[0], : sizes[1]]
        s_dec_norms = small[half : half + sizes[2], : sizes[3]]
        halves = pieces_to_halves(sums[0])
        e_qkv, e_out, e_up, s_embed = [
            own_block(halves, places[name][1], master)
            for name, master in (("qk", enc_qkv), ("ou", enc_out), ("up", enc_up), ("em", dec_embed))
        ]
        e_down, s_qkv = sums[places["do"][0]].T, sums[places["dq"][0]].T
        sums = [e_qkv, e_out, e_up, e_down, s_embed, s_qkv, s_out.T, s_up.T, s_down.T]
    else:
        decoded, d_table, g_dec_norms, *dec_grads = decoder(
            False, table, index, dec_segment, cotangent, norms_d, dec_weights, HEADS_D
        )
        d_patches, g_enc_norms, g_shift, *enc_grads = encoder_back(
            enc_inputs,
            norms_e,
            enc_weights,
            embed,
            swap(d_table.reshape(table.shape)),
            stored,
            HEADS_E,
        )
        g_dec_norms = jnp.concatenate([g_dec_norms[:7], g_shift[:1]], axis=0)
        s_enc_norms, s_dec_norms, sums = reduce_masters(
            g_enc_norms[:4], g_dec_norms, [*enc_grads, *dec_grads]
        )
    d_patches = d_patches.reshape(peers, padded, width)[:, :slot_rows]
    return (
        decoded,
        d_patches.reshape(-1, width),
        s_enc_norms,
        *sums[:4],
        s_dec_norms,
        *sums[4:],
    )


def solution(mesh):
    placed = (
        P(("dp", "fsdp"), None),
        P(("dp", "fsdp"), None),
        P(("dp", "fsdp"), None),
        P(("dp", "fsdp"), None),
        P(("dp", "fsdp"), None, None),
        P("fsdp", "dp"),
        P("fsdp", "dp"),
        P("fsdp", "dp"),
        P("fsdp", "dp"),
        P("fsdp", "dp"),
        P("fsdp", "dp"),
        P("fsdp", "dp"),
        P("fsdp", "dp"),
        P("fsdp", "dp"),
        P("fsdp", "dp"),
        P("fsdp", "dp"),
    )
    staged = (mesh.shape["dp"], mesh.shape["fsdp"]) == (8, 4)
    return jax.shard_map(
        functools.partial(per_device, staged),
        mesh=mesh,
        in_specs=placed,
        out_specs=(
            P(("dp", "fsdp"), None, None),
            P(("dp", "fsdp"), None),
            P("fsdp", "dp"),
            P("fsdp", "dp"),
            P("fsdp", "dp"),
            P("fsdp", "dp"),
            P("fsdp", "dp"),
            P("fsdp", "dp"),
            P("fsdp", "dp"),
            P("fsdp", "dp"),
            P("fsdp", "dp"),
            P("fsdp", "dp"),
            P("fsdp", "dp"),
        ),
        check_vma=False,
    )
```
